32 devices in a mesh: dp: 8 (over z, y), seq: 4 (over x, core).
Axes of the slice: x: 2, y: 2, z: 4, core: 2. Of those that a mesh axis runs over, the one named last changes fastest.
Arguments:
- tokens: bfloat16 [8, 4096, 768], P('dp', 'seq'), may hold values from -6 to 6
- time_steps: int32 [8, 2], P('dp'), may hold values from 0 to 999
- data_group: int32 [8], P('dp'), may hold values from 0 to 1, as said below
- cotangent: bfloat16 [8, 4096, 768], P('dp', 'seq'), may hold values from -6 to 6
- attn_norm_gain: bfloat16 [768], replicated, may hold values from 0.25 to 1.75
- attn_norm_bias: bfloat16 [768], replicated, may hold values from -1.75 to 1.75
- qkv_weight: bfloat16 [768, 2304], replicated, may hold values from -0.21875 to 0.21875
- query_bias: bfloat16 [768], replicated, may hold values from -3 to 3
- value_bias: bfloat16 [768], replicated, may hold values from -3 to 3
- out_weight: bfloat16 [768, 768], replicated, may hold values from -0.625 to 0.625
- out_bias: bfloat16 [768], replicated, may hold values from -1.75 to 1.75
- mlp_norm_gain: bfloat16 [768], replicated, may hold values from 0.25 to 1.75
- mlp_norm_bias: bfloat16 [768], replicated, may hold values from -1.75 to 1.75
- up_weight: bfloat16 [768, 3072], replicated, may hold values from -0.21875 to 0.21875
- up_bias: bfloat16 [3072], replicated, may hold values from -3 to 3
- down_weight: bfloat16 [3072, 768], replicated, may hold values from -0.15625 to 0.15625
- down_bias: bfloat16 [768], replicated, may hold values from -1.75 to 1.75
- time_table: bfloat16 [1000, 768], replicated, may hold values from -3 to 3
Outputs:
- output: bfloat16 [8, 4096, 768], P('dp', 'seq')
- grad_tokens: bfloat16 [8, 4096, 768], P('dp', 'seq')
- grad_attn_norm_gain: float32 [768], replicated
- grad_attn_norm_bias: float32 [768], replicated
- grad_qkv_weight: float32 [768, 2304], P(None, 'dp')
- grad_query_bias: float32 [768], replicated
- grad_value_bias: float32 [768], replicated
- grad_out_weight: float32 [768, 768], P(None, 'dp')
- grad_out_bias: float32 [768], replicated
- grad_mlp_norm_gain: float32 [768], replicated
- grad_mlp_norm_bias: float32 [768], replicated
- grad_up_weight: float32 [768, 3072], P(None, 'dp')
- grad_up_bias: float32 [3072], replicated
- grad_down_weight: float32 [3072, 768], P(None, 'dp')
- grad_down_bias: float32 [768], replicated
- grad_time_table: float32 [1000, 768], P(None, 'dp')
The draws below stay inside these ranges and needn't reach their ends.
Inputs may be any that keep to these rules, and one draw needn't show every extreme that they name: `data_group`: exactly half of the 8 blocks have the value 1.
All inputs are finite; a program needn't handle non-finite values.
Results may differ from the reference program's by a relative error of at most 0.012.
Values may be sent and summed in bfloat16 or wider, within the bound.
No kernel may reach another device: no remote copies, remote signals or barrier semaphores. Data moves between devices by JAX's collectives and lax.ppermute only.
A program may use at most 256 MiB of HBM per device.

```python
import math
import jax
import jax.numpy as jnp
from jax import lax

D = 768
HEADS = 12
HEAD_DIM = 64
FF = 3072
TSTEPS = 1000
LEN_LONG = 4096
LEN_SHORT = 2048
DATA_BLOCKS = 8
TOK_BLOCK = 4096
ROWS_MAX = 2
N_SEQ = 4


def draw_data_group(key, part):
    order = jax.random.permutation(key, DATA_BLOCKS)
    return (order % 2).astype(jnp.int32)


def plant(array, own_key, smallest, top_value):
    shape = array.shape
    spot = [jax.random.randint(jax.random.fold_in(own_key, axis), (), 0, shape[axis]) for axis in range(len(shape))]
    array = array.at[tuple(spot)].set(smallest)
    longest = shape.index(max(shape))
    spot[longest] = (spot[longest] + 1) % shape[longest]
    return array.at[tuple(spot)].set(top_value)


def strengthened(drawn, key, source, target, shards_of, factor):
    owner, partner = [(jnp.arange(drawn.shape[position]) // (drawn.shape[position] // shards_of)).reshape([-1 if axis == position else 1 for axis in range(drawn.ndim)]) for position in (source, target)]
    chosen = jax.random.permutation(key, shards_of)[partner]
    strong = (owner == chosen) | (owner == (partner + shards_of // 2) % shards_of)
    return jnp.where(strong, factor * drawn, drawn)


def level_of(stream_key, dims, cuts, smallest, top_value):
    factor_of, own = 1.0, jax.random.fold_in(stream_key, 6)
    for axis_at, blocks in cuts:
        steps = jnp.exp(jax.random.uniform(jax.random.fold_in(own, axis_at), (blocks,), jnp.float32, smallest / len(cuts), top_value / len(cuts)))
        factor_of = factor_of * jnp.repeat(steps, dims[axis_at] // blocks).reshape([-1 if axis == axis_at else 1 for axis in range(len(dims))])
    return factor_of


def scatter_about(key, shape, scale, reach, cuts=(), kind=jnp.bfloat16):
    entries = scale * jax.random.normal(key, shape, jnp.float32)
    if cuts:
        entries = entries * level_of(key, shape, cuts, -0.22, 0.18)
    return jnp.clip(entries, -reach, reach).astype(kind)


def gaussian_with(own_key, extent, deviation, reach, pieces, heavy, held_as=jnp.bfloat16):
    drawn = deviation * jax.random.normal(own_key, extent, jnp.float32)
    if pieces:
        drawn = drawn * level_of(own_key, extent, pieces, -0.22, 0.18)
    return jnp.clip(strengthened(drawn, jax.random.fold_in(own_key, 3), *heavy), -reach, reach).astype(held_as)


def setup_inputs(seed: int = 0) -> dict:
    keys = jax.random.split(jax.random.key(seed), 19)
    tokens = scatter_about(keys[0], (DATA_BLOCKS, TOK_BLOCK, D), 1.0, 6.0, ((0, 8), (1, 4)))
    time_steps = plant(jax.random.randint(keys[1], (DATA_BLOCKS, ROWS_MAX), 0, TSTEPS), jax.random.fold_in(keys[1], 1), 0, TSTEPS - 1).astype(jnp.int32)
    data_group = draw_data_group(jax.random.fold_in(keys[18], 71), 0)
    cotangent = gaussian_with(keys[3], (DATA_BLOCKS, TOK_BLOCK, D), 1.0, 6.0, ((0, 8), (1, 4)), (0, 2, 8, 2.0))
    attn_norm_gain = jnp.clip(1.0 + 0.15 * jax.random.normal(keys[4], (D,), jnp.float32), 0.25, 1.75).astype(jnp.bfloat16)
    attn_norm_bias = scatter_about(keys[5], (D,), 0.3, 1.75)
    qkv_weight = scatter_about(keys[6], (D, 3 * D), D ** -0.5, 0.21875)
    query_bias = scatter_about(keys[7], (D,), 0.5, 3.0)
    value_bias = scatter_about(keys[8], (D,), 0.5, 3.0)
    out_weight = scatter_about(keys[9], (D, D), (D // 8) ** -0.5, 0.625)
    out_bias = scatter_about(keys[10], (D,), 0.3, 1.75)
    mlp_norm_gain = jnp.clip(1.0 + 0.15 * jax.random.normal(keys[11], (D,), jnp.float32), 0.25, 1.75).astype(jnp.bfloat16)
    mlp_norm_bias = scatter_about(keys[12], (D,), 0.3, 1.75)
    up_weight = scatter_about(keys[13], (D, FF), D ** -0.5, 0.21875)
    up_bias = scatter_about(keys[14], (FF,), 0.5, 3.0)
    down_weight = scatter_about(keys[15], (FF, D), (FF // 2) ** -0.5, 0.15625)
    down_bias = scatter_about(keys[16], (D,), 0.3, 1.75)
    time_table = scatter_about(keys[17], (TSTEPS, D), 0.5, 3.0)
    return {"tokens": tokens, "time_steps": time_steps, "data_group": data_group, "cotangent": cotangent, "attn_norm_gain": attn_norm_gain, "attn_norm_bias": attn_norm_bias, "qkv_weight": qkv_weight, "query_bias": query_bias, "value_bias": value_bias, "out_weight": out_weight, "out_bias": out_bias, "mlp_norm_gain": mlp_norm_gain, "mlp_norm_bias": mlp_norm_bias, "up_weight": up_weight, "up_bias": up_bias, "down_weight": down_weight, "down_bias": down_bias, "time_table": time_table}


@jax.custom_vjp
def low(v):
    return lax.optimization_barrier(v.astype(jnp.bfloat16)).astype(jnp.float32)

@jax.custom_vjp
def low_back(v):
    return v

def low_keep(v):
    return (low(v), None)

def low_pass(kept, grad):
    return (grad,)

def back_keep(v):
    return (v, None)

def back_low(kept, grad):
    return (low(grad),)
low.defvjp(low_keep, low_pass)
low_back.defvjp(back_keep, back_low)
EPSILON = 1e-05
HIGHEST = lax.Precision.HIGHEST

def layer_norm(hidden, gain, shift):
    center = hidden - lax.optimization_barrier(jnp.mean(hidden, -1, keepdims=True))
    spread = lax.optimization_barrier(jnp.mean(center * center, -1, keepdims=True))
    return center * lax.rsqrt(spread + EPSILON) * gain + shift

def to_rows(values, part_count, segment):
    per_part = values.shape[0] // part_count
    row_count = per_part // segment
    shaped = values.reshape((part_count, row_count, segment) + values.shape[1:])
    return jnp.swapaxes(shaped, 0, 1).reshape((row_count, part_count * segment) + values.shape[1:])

def from_rows(values, part_count):
    row_count = values.shape[0]
    segment = values.shape[1] // part_count
    shaped = values.reshape((row_count, part_count, segment) + values.shape[2:])
    return jnp.swapaxes(shaped, 0, 1).reshape((part_count * row_count * segment,) + values.shape[2:])

def attend(queries, keys_all, values, segment):
    scale = 1.0 / math.sqrt(HEAD_DIM)
    query_rows = to_rows(queries, N_SEQ, segment)
    key_rows = to_rows(keys_all, N_SEQ, segment)
    value_rows = to_rows(values, N_SEQ, segment)
    row_count, length = (query_rows.shape[0], query_rows.shape[1])
    block = min(512, length)
    count = length // block
    query_blocks = jnp.swapaxes(query_rows.reshape((row_count, count, block) + query_rows.shape[2:]), 0, 1)

    def one_block(query_block):
        scores = jnp.einsum('rqhe,rkhe->rhqk', query_block, key_rows, precision=HIGHEST) * scale
        scores = low_back(scores)
        weights = low(jax.nn.softmax(scores, axis=-1))
        return jnp.einsum('rhqk,rkhe->rqhe', weights, value_rows, precision=HIGHEST)
    mixed = lax.map(jax.checkpoint(one_block), query_blocks)
    mixed_rows = jnp.swapaxes(mixed, 0, 1).reshape(query_rows.shape)
    return from_rows(mixed_rows, N_SEQ)

def layer_block(tokens_blk, steps_blk, group_blk, params):
    gain_one, shift_one, w_qkv, bias_query, bias_value, w_out, bias_out, gain_two, shift_two, w_up, bias_up, w_down, bias_down, table = params
    total = tokens_blk.shape[0]
    width = tokens_blk.shape[1]
    per_dev = total // N_SEQ
    offset = jnp.arange(total, dtype=jnp.int32) % per_dev
    segment = jnp.where(group_blk == 0, LEN_SHORT // N_SEQ, LEN_LONG // N_SEQ).astype(jnp.int32)
    row_index = offset // segment
    hidden = tokens_blk + table[steps_blk[row_index]]
    normed = low(layer_norm(hidden, gain_one, shift_one))
    bias_all = jnp.concatenate([bias_query, jnp.zeros_like(bias_query), bias_value])
    projected = low(low_back(jnp.dot(normed, w_qkv, precision=HIGHEST) + bias_all))
    split = projected.reshape(total, 3, HEADS, HEAD_DIM)
    attended = lax.cond(group_blk == 0, lambda: attend(split[:, 0], split[:, 1], split[:, 2], LEN_SHORT // N_SEQ), lambda: attend(split[:, 0], split[:, 1], split[:, 2], LEN_LONG // N_SEQ))
    attended = low(low_back(attended.reshape(total, width)))
    branch = low_back(jnp.dot(attended, w_out, precision=HIGHEST) + bias_out)
    resid = hidden + branch
    normed_two = low(layer_norm(resid, gain_two, shift_two))
    up_act = low_back(jnp.dot(normed_two, w_up, precision=HIGHEST) + bias_up)
    gelu_act = low(jax.nn.gelu(up_act, approximate=False))
    down_out = low_back(jnp.dot(gelu_act, w_down, precision=HIGHEST) + bias_down)
    return resid + down_out

def forward(tokens_all, params, time_steps, data_group):

    def step_fn(carry, inputs):
        tokens_blk, steps_blk, group_blk = inputs
        return (carry, jax.checkpoint(layer_block)(tokens_blk, steps_blk, group_blk, params))
    start = jnp.zeros((), jnp.float32)
    finish, outputs = lax.scan(step_fn, start, (tokens_all, time_steps, data_group))
    return outputs

def reference(tokens, time_steps, data_group, cotangent, attn_norm_gain, attn_norm_bias, qkv_weight, query_bias, value_bias, out_weight, out_bias, mlp_norm_gain, mlp_norm_bias, up_weight, up_bias, down_weight, down_bias, time_table):
    params = tuple((item.astype(jnp.float32) for item in (attn_norm_gain, attn_norm_bias, qkv_weight, query_bias, value_bias, out_weight, out_bias, mlp_norm_gain, mlp_norm_bias, up_weight, up_bias, down_weight, down_bias, time_table)))
    primal = tokens.astype(jnp.float32)
    result, pullback = jax.vjp(lambda tok_all, weights: forward(tok_all, weights, time_steps, data_group), primal, params)
    grad_in, grads = pullback(cotangent.astype(jnp.float32))
    g_gain_one, g_shift_one, g_qkv, g_query, g_value, g_out, g_out_bias, g_gain_two, g_shift_two, g_up, g_up_bias, g_down, g_down_bias, g_table = grads
    return (result.astype(jnp.bfloat16), grad_in.astype(jnp.bfloat16), g_gain_one, g_shift_one, g_qkv, g_query, g_value, g_out, g_out_bias, g_gain_two, g_shift_two, g_up, g_up_bias, g_down, g_down_bias, g_table)
```

```python
from functools import partial

import jax
import jax.numpy as jnp
from jax import lax
from jax.experimental import pallas as pl
from jax.experimental.pallas import tpu as pltpu
from jax.sharding import PartitionSpec as P

HEADS = 12
HEAD_DIM = 64
EPSILON = 1e-05
LOG2E = 1.4426950408889634
SCALE = HEAD_DIM**-0.5
BF16 = jnp.bfloat16
F32 = jnp.float32
NN = (((1,), (0,)), ((), ()))
NT = (((1,), (1,)), ((), ()))
TN = (((0,), (0,)), ((), ()))


def dot(left, right, dims=NN):
    return lax.dot_general(left, right, dims, preferred_element_type=F32)


def split_low(values, count):
    parts = []
    for _ in range(count):
        term = values.astype(BF16)
        parts.append(term)
        values = values - term.astype(F32)
    return parts


def attend_kernel(short_ref, heads_ref, sent_ref, mixed_ref, log_ref, keys, values, *, segment):
    step = pl.program_id(1)
    chunks = keys.shape[0]

    @pl.when(step == 0)
    def _():
        for chunk in range(chunks):
            source, part = divmod(chunk, 2)
            cols = slice(part * segment, (part + 1) * segment)
            key = heads_ref[source, 1, 0, :, cols]
            keys[chunk, 0:64, :] = key
            keys[chunk, 64:128, :] = key
            values[chunk, 0:64, :] = heads_ref[source, 2, 0, :, cols]
            values[chunk, 64:80, :] = jnp.ones((16, segment), BF16)

    source, part = step // 2, step % 2
    cols = pl.ds(pl.multiple_of(part * segment, segment), segment)
    scaled = heads_ref[source, 0, 0, :, cols].astype(F32) * (SCALE * LOG2E)
    queries = jnp.concatenate(split_low(scaled, 2), 0)

    def run(order):
        peak = total = None
        after = dot(keys[order[0]], queries, TN)
        for index, chunk in enumerate(order):
            scores = after
            if index + 1 < len(order):
                after = dot(keys[order[index + 1]], queries, TN)
            here = jnp.max(scores, 0, keepdims=True)
            top = here if peak is None else jnp.maximum(peak, here)
            weights = jnp.exp2(scores - top).astype(BF16)
            mixed = dot(values[chunk], weights)
            total = mixed if peak is None else total * jnp.exp2(peak - top) + mixed
            peak = top
        norm = total[64:65, :]
        mixed = total[:64] / norm
        mixed_ref[0, 0] = mixed
        sent_ref[0, 0] = mixed.astype(BF16)
        log_ref[0, 0] = peak + jnp.log2(norm)

    is_short = short_ref[0] != 0

    @pl.when(is_short)
    def _():
        run([2 * index + part for index in range(chunks // 2)])

    @pl.when(jnp.logical_not(is_short))
    def _():
        run(list(range(chunks)))


def attend(is_short, heads):
    sources, _, count, depth, tokens = heads.shape
    segment = tokens // 2
    work = count * (sources * tokens) ** 2
    return pl.pallas_call(
        partial(attend_kernel, segment=segment),
        grid_spec=pltpu.PrefetchScalarGridSpec(
            num_scalar_prefetch=1,
            grid=(count, 2 * sources),
            in_specs=[pl.BlockSpec((sources, 3, 1, depth, tokens), lambda h, i, s: (0, 0, h, 0, 0))],
            out_specs=[
                pl.BlockSpec((1, 1, depth, segment), lambda h, i, s: (h, i // 2, 0, i % 2)),
                pl.BlockSpec((1, 1, depth, segment), lambda h, i, s: (h, i // 2, 0, i % 2)),
                pl.BlockSpec((1, 1, 1, segment), lambda h, i, s: (h, i, 0, 0)),
            ],
            scratch_shapes=[
                pltpu.VMEM((2 * sources, 128, segment), BF16),
                pltpu.VMEM((2 * sources, 80, segment), BF16),
            ],
        ),
        out_shape=[
            jax.ShapeDtypeStruct((count, sources, depth, tokens), BF16),
            jax.ShapeDtypeStruct((count, sources, depth, tokens), F32),
            jax.ShapeDtypeStruct((count, 2 * sources, 1, segment), F32),
        ],
        compiler_params=pltpu.CompilerParams(vmem_limit_bytes=40 << 20),
        cost_estimate=pl.CostEstimate(
            flops=16 * work * depth, transcendentals=work, bytes_accessed=8 * heads.size // 3
        ),
        name="attend",
    )(is_short, heads)


def attend_back_kernel(
    short_ref, heads_ref, mixed_ref, grad_ref, log_ref, out_ref, q_aug, g_aug, k_aug, v_aug, grad_q, *, segment
):
    step = pl.program_id(1)
    chunks = q_aug.shape[0]

    @pl.when(step == 0)
    def _():
        minus = jnp.full((16, segment), -1.0, BF16)
        zeros = jnp.zeros((13, segment), BF16)
        for chunk in range(chunks):
            source, part = divmod(chunk, 2)
            cols = slice(part * segment, (part + 1) * segment)
            scaled = heads_ref[source, 0, 0, :, cols].astype(F32) * (SCALE * LOG2E)
            high, low = split_low(scaled, 2)
            q_aug[chunk, 0:64, :] = high
            q_aug[chunk, 64:128, :] = low
            q_aug[chunk, 128:144, :] = jnp.concatenate(split_low(log_ref[0, chunk], 3) + [zeros], 0)
            grad = grad_ref[0, source, :, cols]
            inner = jnp.sum(
                grad.astype(F32) * mixed_ref[0, source, :, cols], 0, keepdims=True
            )
            g_aug[chunk, 0:64, :] = grad
            g_aug[chunk, 64:80, :] = jnp.concatenate(split_low(inner, 3) + [zeros], 0)
            key = heads_ref[source, 1, 0, :, cols]
            k_aug[chunk, 0:64, :] = key
            k_aug[chunk, 64:128, :] = key
            k_aug[chunk, 128:144, :] = minus
            v_aug[chunk, 0:64, :] = heads_ref[source, 2, 0, :, cols]
            v_aug[chunk, 64:80, :] = minus
        grad_q[...] = jnp.zeros_like(grad_q)

    source, part = step // 2, step % 2
    cols = pl.ds(pl.multiple_of(part * segment, segment), segment)

    def run(order):
        key, value = k_aug[step], v_aug[step]
        turned = key[0:64].T

        def products(chunk):
            return dot(q_aug[chunk], key, TN), dot(g_aug[chunk], value, TN)

        key_total = value_total = None
        after = products(order[0])
        for index, chunk in enumerate(order):
            scores, grads = after
            if index + 1 < len(order):
                after = products(order[index + 1])
            weights = jnp.exp2(scores)
            g_scores = (weights * grads).astype(BF16)
            value_part = dot(g_aug[chunk, 0:64, :], weights.astype(BF16))
            key_part = dot(q_aug[chunk, 0:128, :], g_scores)
            value_total = value_part if value_total is None else value_total + value_part
            key_total = key_part if key_total is None else key_total + key_part
            grad_q[chunk] += dot(g_scores, turned)
        out_ref[source, 1, 0, :, cols] = (
            (key_total[0:64] + key_total[64:128]) * (1.0 / LOG2E)
        ).astype(BF16)
        out_ref[source, 2, 0, :, cols] = value_total.astype(BF16)

    is_short = short_ref[0] != 0

    @pl.when(is_short)
    def _():
        run([2 * index + part for index in range(chunks // 2)])

    @pl.when(jnp.logical_not(is_short))
    def _():
        run(list(range(chunks)))

    @pl.when(step == chunks - 1)
    def _():
        for chunk in range(chunks):
            source, part = divmod(chunk, 2)
            cols = slice(part * segment, (part + 1) * segment)
            out_ref[source, 0, 0, :, cols] = (grad_q[chunk] * SCALE).T.astype(BF16)


def attend_back(is_short, heads, mixed, grad, log_sums):
    sources, _, count, depth, tokens = heads.shape
    segment = tokens // 2
    work = count * (sources * tokens) ** 2
    return pl.pallas_call(
        partial(attend_back_kernel, segment=segment),
        grid_spec=pltpu.PrefetchScalarGridSpec(
            num_scalar_prefetch=1,
            grid=(count, 2 * sources),
            in_specs=[
                pl.BlockSpec((sources, 3, 1, depth, tokens), lambda h, i, s: (0, 0, h, 0, 0)),
                pl.BlockSpec((1, sources, depth, tokens), lambda h, i, s: (h, 0, 0, 0)),
                pl.BlockSpec((1, sources, depth, tokens), lambda h, i, s: (h, 0, 0, 0)),
                pl.BlockSpec((1, 2 * sources, 1, segment), lambda h, i, s: (h, 0, 0, 0)),
            ],
            out_specs=pl.BlockSpec((sources, 3, 1, depth, tokens), lambda h, i, s: (0, 0, h, 0, 0)),
            scratch_shapes=[
                pltpu.VMEM((2 * sources, 144, segment), BF16),
                pltpu.VMEM((2 * sources, 80, segment), BF16),
                pltpu.VMEM((2 * sources, 144, segment), BF16),
                pltpu.VMEM((2 * sources, 80, segment), BF16),
                pltpu.VMEM((2 * sources, segment, depth), F32),
            ],
        ),
        out_shape=jax.ShapeDtypeStruct(heads.shape, BF16),
        compiler_params=pltpu.CompilerParams(vmem_limit_bytes=40 << 20),
        cost_estimate=pl.CostEstimate(
            flops=40 * work * depth, transcendentals=work, bytes_accessed=6 * heads.size
        ),
        name="attend_back",
    )(is_short, heads, mixed, grad, log_sums)


def swap(values, axis, bit):
    size = lax.axis_size(axis)
    return lax.ppermute(values, axis, [(j, j ^ bit) for j in range(size)])


def sum_all(values):
    for axis in ("seq", "dp"):
        bit = 1
        while bit < lax.axis_size(axis):
            values = values + swap(values, axis, bit)
            bit *= 2
    return values


def halve(parts, axis, flag, bit):
    kept = lax.dynamic_index_in_dim(parts, flag, axis, keepdims=False)
    sent = lax.dynamic_index_in_dim(parts, 1 - flag, axis, keepdims=False)
    got = swap(sent, "seq", bit)
    return (kept.astype(F32) + got.astype(F32)).astype(BF16)


def reduce_columns(grad):
    dp = lax.axis_size("dp")
    place = lax.axis_index("seq")
    columns, rows = grad.shape
    parts = grad.reshape(dp, 2, 2, columns // dp // 4, rows)
    parts = halve(parts, 2, place % 2, 1)
    parts = halve(parts, 1, place // 2, 2)
    parts = lax.all_to_all(parts, "dp", split_axis=0, concat_axis=0, tiled=True)
    share = jnp.sum(parts.astype(F32), 0).astype(BF16)
    return lax.all_gather(share, "seq", axis=0, tiled=True).astype(F32)


def layer_norm(hidden, gain, shift):
    center = hidden - jnp.mean(hidden, -1, keepdims=True)
    spread = jnp.mean(center * center, -1, keepdims=True)
    return center * lax.rsqrt(spread + EPSILON) * gain + shift


def on_device(
    tokens,
    time_steps,
    data_group,
    cotangent,
    attn_norm_gain,
    attn_norm_bias,
    qkv_weight,
    query_bias,
    value_bias,
    out_weight,
    out_bias,
    mlp_norm_gain,
    mlp_norm_bias,
    up_weight,
    up_bias,
    down_weight,
    down_bias,
    time_table,
):
    sources = lax.axis_size("seq")
    dp = lax.axis_size("dp")
    inputs = tokens[0].astype(F32)
    tok_here, width = inputs.shape
    rounds = HEADS // sources
    half = tok_here // 2
    is_short = data_group[0] == 0
    short_flag = is_short.astype(jnp.int32)[None]
    row_table = time_table[time_steps[0]].astype(F32)
    second = jnp.where(is_short, row_table[1], row_table[0])
    hidden = (inputs.reshape(2, half, width) + jnp.stack([row_table[0], second])[:, None, :]).reshape(
        tok_here, width
    )
    gain_one = attn_norm_gain.astype(F32)
    shift_one = attn_norm_bias.astype(F32)
    normed, norm_one_back = jax.vjp(layer_norm, hidden, gain_one, shift_one)
    normed_low = normed.astype(BF16)
    bias_all = jnp.concatenate([query_bias, jnp.zeros_like(query_bias), value_bias]).astype(F32)
    projected = (dot(qkv_weight, normed_low, (((0,), (1,)), ((), ()))) + bias_all[:, None]).astype(BF16)
    by_round = projected.reshape(3, sources, rounds, HEAD_DIM, tok_here)

    def exchange(values):
        return lax.all_to_all(values, "seq", split_axis=0, concat_axis=0, tiled=True)

    heads, mixed, logs, returned = [], [], [], []
    for r in range(rounds):
        heads.append(exchange(jnp.swapaxes(by_round[:, :, r], 0, 1))[:, :, None])
    for r in range(rounds):
        sent, whole, log = attend(short_flag, heads[r])
        mixed.append(whole)
        logs.append(log)
        returned.append(exchange(sent[0]))
    attended = jnp.stack(returned, 1).reshape(width, tok_here)
    branch = dot(attended, out_weight, TN) + out_bias.astype(F32)
    resid = hidden + branch
    gain_two = mlp_norm_gain.astype(F32)
    shift_two = mlp_norm_bias.astype(F32)
    normed_two, norm_two_back = jax.vjp(layer_norm, resid, gain_two, shift_two)
    normed_two_low = normed_two.astype(BF16)
    up_act = dot(normed_two_low, up_weight) + up_bias.astype(F32)
    gelu_act, gelu_back = jax.vjp(partial(jax.nn.gelu, approximate=False), up_act)
    gelu_low = gelu_act.astype(BF16)
    down_out = dot(gelu_low, down_weight) + down_bias.astype(F32)
    result = (resid + down_out).astype(BF16)
    grad_out = cotangent[0].astype(F32)
    grad_down_low = cotangent[0]
    grad_down_b = jnp.sum(grad_down_low, 0, dtype=F32)
    grad_gelu = dot(grad_down_low, down_weight, NT)
    (grad_up_act,) = gelu_back(grad_gelu)
    grad_up_low = grad_up_act.astype(BF16)
    grad_up_b = jnp.sum(grad_up_low, 0, dtype=F32)
    grad_normed_two = dot(grad_up_low, up_weight, NT)
    grad_resid_norm, grad_gain_two, grad_shift_two = norm_two_back(grad_normed_two)
    grad_resid = grad_out + grad_resid_norm
    grad_branch = grad_resid.astype(BF16)
    grad_out_b = jnp.sum(grad_branch, 0, dtype=F32)
    grad_attended = dot(out_weight, grad_branch, NT).astype(BF16)
    grad_by_round = grad_attended.reshape(sources, rounds, HEAD_DIM, tok_here)
    grad_heads = [exchange(grad_by_round[:, r])[None] for r in range(rounds)]

    g_down_t = dot(grad_down_low, gelu_low, TN).astype(BF16)
    g_up_t = dot(grad_up_low, normed_two_low, TN).astype(BF16)
    g_out_t = dot(grad_branch, attended, (((0,), (1,)), ((), ()))).astype(BF16)
    sum_down = reduce_columns(g_down_t)
    sum_up = reduce_columns(g_up_t)
    sum_out = reduce_columns(g_out_t)
    mine = (jnp.arange(dp) == lax.axis_index("dp"))[:, None]
    first = lax.axis_index("seq") == 0
    steps_slot = jnp.where(mine & first, time_steps.astype(F32), 0.0)
    early = sum_all(
        jnp.concatenate(
            [grad_gain_two, grad_shift_two, grad_up_b, grad_down_b, grad_out_b, steps_slot.reshape(-1)]
        )
    )

    grad_back = []
    for r in range(rounds):
        g = attend_back(short_flag, heads[r], mixed[r], grad_heads[r], logs[r])
        grad_back.append(exchange(g[:, :, 0]))
    grad_qkv = jnp.swapaxes(jnp.stack(grad_back, 2), 0, 1).reshape(3 * width, tok_here)
    g_qkv_t = dot(grad_qkv, normed_low).astype(BF16)
    sum_qkv = reduce_columns(g_qkv_t)
    grad_qkv_b = jnp.sum(grad_qkv, 1, dtype=F32)
    grad_normed = dot(grad_qkv, qkv_weight, (((0,), (1,)), ((), ())))
    grad_hidden_norm, grad_gain_one, grad_shift_one = norm_one_back(grad_normed)
    grad_hidden = grad_resid + grad_hidden_norm
    grad_input = grad_hidden.astype(BF16)
    halves = jnp.sum(grad_hidden.reshape(2, half, width), 1)
    row_sums = jnp.where(
        is_short, halves, jnp.stack([halves[0] + halves[1], jnp.zeros_like(halves[0])])
    )
    row_slot = jnp.where(mine[:, :, None], row_sums[None], 0.0)
    late = sum_all(
        jnp.concatenate(
            [
                grad_gain_one,
                grad_shift_one,
                grad_qkv_b[:width],
                grad_qkv_b[2 * width :],
                row_slot.reshape(-1),
            ]
        )
    )
    ends = [width, width, up_bias.shape[0], width, width]
    points = [sum(ends[: i + 1]) for i in range(len(ends))]
    sum_gain_two, sum_shift_two, sum_up_b, sum_down_b, sum_out_b, all_steps = jnp.split(early, points)
    sum_gain_one, sum_shift_one, sum_query, sum_value, all_rows = jnp.split(
        late, [width, 2 * width, 3 * width, 4 * width]
    )
    table_rows = time_table.shape[0]
    share = width // dp
    rows_mine = lax.dynamic_slice_in_dim(
        all_rows.reshape(-1, width), lax.axis_index("dp") * share, share, 1
    )
    hits = (
        jnp.arange(table_rows, dtype=jnp.int32)[:, None] == all_steps.astype(jnp.int32)[None, :]
    ).astype(F32)
    sum_table = jnp.dot(hits, rows_mine, precision=lax.Precision.HIGHEST)
    return (
        result[None],
        grad_input[None],
        sum_gain_one,
        sum_shift_one,
        sum_qkv.T,
        sum_query,
        sum_value,
        sum_out.T,
        sum_out_b,
        sum_gain_two,
        sum_shift_two,
        sum_up.T,
        sum_up_b,
        sum_down.T,
        sum_down_b,
        sum_table,
    )


def solution(mesh):
    placed = (P("dp", "seq", None), P("dp", None), P("dp"), P("dp", "seq", None)) + (P(),) * 14
    column = P(None, "dp")
    return jax.shard_map(
        on_device,
        mesh=mesh,
        in_specs=placed,
        out_specs=(
            P("dp", "seq", None),
            P("dp", "seq", None),
            P(),
            P(),
            column,
            P(),
            P(),
            column,
            P(),
            P(),
            P(),
            column,
            P(),
            column,
            P(),
            column,
        ),
        check_vma=False,
    )
```

```python
from functools import partial

import jax
import jax.numpy as jnp
from jax import lax
from jax.experimental import pallas as pl
from jax.experimental.pallas import tpu as pltpu
from jax.sharding import PartitionSpec as P

HEADS = 12
HEAD_DIM = 64
EPSILON = 1e-05
LOG2E = 1.4426950408889634
SCALE = HEAD_DIM**-0.5
BF16 = jnp.bfloat16
F32 = jnp.float32
NN = (((1,), (0,)), ((), ()))
NT = (((1,), (1,)), ((), ()))
TN = (((0,), (0,)), ((), ()))
VMEM = 62 << 20
SMALL_VMEM = 40 << 20


def dot(left, right, dims=NN):
    return lax.dot_general(left, right, dims, preferred_element_type=F32)


def split_low(values, count):
    parts = []
    for _ in range(count):
        term = values.astype(BF16)
        parts.append(term)
        values = values - term.astype(F32)
    return parts


def whole(*shape):
    return pl.BlockSpec(shape, lambda *_: (0,) * len(shape))


def halves(sources, segment):
    for chunk in range(2 * sources):
        source, part = divmod(chunk, 2)
        yield chunk, source, slice(part * segment, (part + 1) * segment)


def by_length(short_ref, run, chunks):
    part = pl.program_id(0) % 2
    is_short = short_ref[0] != 0

    @pl.when(is_short)
    def _():
        run([2 * index + part for index in range(chunks // 2)])

    @pl.when(jnp.logical_not(is_short))
    def _():
        run(list(range(chunks)))


def attend_kernel(short_ref, *refs, sources, segment, held):
    heads, refs = refs[:sources], refs[sources:]
    earlier, refs = refs[: sources * held], refs[sources * held :]
    sent, refs = refs[:sources], refs[sources:]
    mixed_ref, log_ref, queries, keys, values = refs
    step = pl.program_id(0)
    chunks = 2 * sources

    @pl.when(step == 0)
    def _():
        for old, new in zip(earlier, sent):
            new[0] = old[0]
        for chunk, source, cols in halves(sources, segment):
            scaled = heads[source][0, :, cols].astype(F32) * (SCALE * LOG2E)
            high, low = split_low(scaled, 2)
            queries[chunk, 0:64, :] = high
            queries[chunk, 64:128, :] = low
            key = heads[source][1, :, cols]
            keys[chunk, 0:64, :] = key
            keys[chunk, 64:128, :] = key
            values[chunk, 0:64, :] = heads[source][2, :, cols]
            values[chunk, 64:80, :] = jnp.ones((16, segment), BF16)

    def run(order):
        query = queries[step]
        peak = total = None
        later = dot(keys[order[0]], query, TN)
        for index, chunk in enumerate(order):
            scores = later
            if index + 1 < len(order):
                later = dot(keys[order[index + 1]], query, TN)
            here = jnp.max(scores, 0, keepdims=True)
            top = here if peak is None else jnp.maximum(peak, here)
            weights = jnp.exp2(scores - top).astype(BF16)
            mixed = dot(values[chunk], weights)
            total = mixed if peak is None else total * jnp.exp2(peak - top) + mixed
            peak = top
        norm = total[64:65, :]
        result = total[:64] / norm
        mixed_ref[step] = result
        log_ref[step] = peak + jnp.log2(norm)
        for chunk, source, cols in halves(sources, segment):

            @pl.when(step == chunk)
            def _():
                sent[source][held, :, cols] = result.astype(BF16)

    by_length(short_ref, run, chunks)


def attend(is_short, heads, earlier=()):
    sources = len(heads)
    _, depth, tokens = heads[0].shape
    segment, chunks = tokens // 2, 2 * sources
    work = (sources * tokens) ** 2
    held = len(earlier) // sources
    out = pl.pallas_call(
        partial(attend_kernel, sources=sources, segment=segment, held=held),
        grid_spec=pltpu.PrefetchScalarGridSpec(
            num_scalar_prefetch=1,
            grid=(chunks,),
            in_specs=[whole(3, depth, tokens)] * sources + [whole(1, depth, tokens)] * len(earlier),
            out_specs=[whole(1 + held, depth, tokens)] * sources
            + [whole(chunks, depth, segment), whole(chunks, 1, segment)],
            scratch_shapes=[
                pltpu.VMEM((chunks, 128, segment), BF16),
                pltpu.VMEM((chunks, 128, segment), BF16),
                pltpu.VMEM((chunks, 80, segment), BF16),
            ],
        ),
        out_shape=[jax.ShapeDtypeStruct((1 + held, depth, tokens), BF16)] * sources
        + [
            jax.ShapeDtypeStruct((chunks, depth, segment), F32),
            jax.ShapeDtypeStruct((chunks, 1, segment), F32),
        ],
        compiler_params=pltpu.CompilerParams(vmem_limit_bytes=SMALL_VMEM),
        cost_estimate=pl.CostEstimate(
            flops=16 * work * depth, transcendentals=work, bytes_accessed=16 * sources * tokens * depth
        ),
        name="attend",
    )(is_short, *heads, *earlier)
    return out[:sources], out[-2], out[-1]


def attend_back_kernel(short_ref, *refs, sources, segment):
    heads, grads, (mixed_ref, log_ref), refs = (
        refs[:sources],
        refs[sources : 2 * sources],
        refs[2 * sources : 2 * sources + 2],
        refs[2 * sources + 2 :],
    )
    outs, (q_aug, g_aug, k_aug, v_aug, grad_q) = refs[:sources], refs[sources:]
    step = pl.program_id(0)
    chunks = 2 * sources

    @pl.when(step == 0)
    def _():
        minus = jnp.full((16, segment), -1.0, BF16)
        zeros = jnp.zeros((13, segment), BF16)
        for chunk, source, cols in halves(sources, segment):
            scaled = heads[source][0, :, cols].astype(F32) * (SCALE * LOG2E)
            high, low = split_low(scaled, 2)
            q_aug[chunk, 0:64, :] = high
            q_aug[chunk, 64:128, :] = low
            q_aug[chunk, 128:144, :] = jnp.concatenate(split_low(log_ref[chunk], 3) + [zeros], 0)
            grad = grads[source][0, :, cols]
            inner = jnp.sum(grad.astype(F32) * mixed_ref[chunk], 0, keepdims=True)
            g_aug[chunk, 0:64, :] = grad
            g_aug[chunk, 64:80, :] = jnp.concatenate(split_low(inner, 3) + [zeros], 0)
            key = heads[source][1, :, cols]
            k_aug[chunk, 0:64, :] = key
            k_aug[chunk, 64:128, :] = key
            k_aug[chunk, 128:144, :] = minus
            v_aug[chunk, 0:64, :] = heads[source][2, :, cols]
            v_aug[chunk, 64:80, :] = minus
        grad_q[...] = jnp.zeros_like(grad_q)

    def run(order):
        key, value = k_aug[step], v_aug[step]
        turned = key[0:64].T

        def products(chunk):
            return dot(q_aug[chunk], key, TN), dot(g_aug[chunk], value, TN)

        key_total = value_total = None
        later = products(order[0])
        for index, chunk in enumerate(order):
            scores, slopes = later
            if index + 1 < len(order):
                later = products(order[index + 1])
            weights = jnp.exp2(scores)
            g_scores = (weights * slopes).astype(BF16)
            value_part = dot(g_aug[chunk, 0:64, :], weights.astype(BF16))
            key_part = dot(q_aug[chunk, 0:128, :], g_scores)
            value_total = value_part if value_total is None else value_total + value_part
            key_total = key_part if key_total is None else key_total + key_part
            grad_q[chunk] += dot(g_scores, turned)
        key_grad = ((key_total[0:64] + key_total[64:128]) * (1.0 / LOG2E)).astype(BF16)
        value_grad = value_total.astype(BF16)
        for chunk, source, cols in halves(sources, segment):

            @pl.when(step == chunk)
            def _():
                outs[source][1, :, cols] = key_grad
                outs[source][2, :, cols] = value_grad

    by_length(short_ref, run, chunks)

    @pl.when(step == chunks - 1)
    def _():
        for chunk, source, cols in halves(sources, segment):
            outs[source][0, :, cols] = (grad_q[chunk] * SCALE).T.astype(BF16)


def attend_back(is_short, heads, mixed, grads, log_sums, at):
    sources = len(heads)
    _, depth, tokens = heads[0].shape
    segment, chunks = tokens // 2, 2 * sources
    work = (sources * tokens) ** 2
    return pl.pallas_call(
        partial(attend_back_kernel, sources=sources, segment=segment),
        grid_spec=pltpu.PrefetchScalarGridSpec(
            num_scalar_prefetch=1,
            grid=(chunks,),
            in_specs=[whole(3, depth, tokens)] * sources
            + [pl.BlockSpec((1, depth, tokens), lambda i, s: (at, 0, 0))] * sources
            + [whole(chunks, depth, segment), whole(chunks, 1, segment)],
            out_specs=[whole(3, depth, tokens)] * sources,
            scratch_shapes=[
                pltpu.VMEM((chunks, 144, segment), BF16),
                pltpu.VMEM((chunks, 80, segment), BF16),
                pltpu.VMEM((chunks, 144, segment), BF16),
                pltpu.VMEM((chunks, 80, segment), BF16),
                pltpu.VMEM((chunks, segment, depth), F32),
            ],
        ),
        out_shape=[jax.ShapeDtypeStruct((3, depth, tokens), BF16)] * sources,
        compiler_params=pltpu.CompilerParams(vmem_limit_bytes=VMEM),
        cost_estimate=pl.CostEstimate(
            flops=40 * work * depth, transcendentals=work, bytes_accessed=40 * sources * tokens * depth
        ),
        name="attend_back",
    )(is_short, *heads, *grads, mixed, log_sums)


def normalize(hidden):
    center = hidden - jnp.mean(hidden, -1, keepdims=True)
    spread = jnp.mean(center * center, -1, keepdims=True)
    inverse = lax.rsqrt(spread + EPSILON)
    return center * inverse, inverse


def token_block(index, size):
    return pl.ds(pl.multiple_of(index * size, size), size)


def column_sum(values):
    return jnp.sum(values.astype(F32), 0, keepdims=True)


def project_kernel(place_ref, tokens, rows, gain, shift, weight, bias, normed, *refs, sources, rounds, block):
    outs, turned = refs[:-1], refs[-1]
    step = pl.program_id(0)
    count = tokens.shape[0] // block

    @pl.when(step == 0)
    def _():
        def body(index, _):
            here = token_block(index, block)
            row = rows[pl.ds(index // (count // 2), 1), :]
            scaled, _ = normalize(tokens[here, :].astype(F32) + row)
            low = (scaled * gain[...] + shift[...]).astype(BF16)
            normed[here, :] = low
            turned[:, here] = low.T
            return 0

        lax.fori_loop(0, count, body, 0)

    result = (dot(weight[...], turned[...], TN) + bias[...]).astype(BF16)
    pair, low_bit = step % (sources // 2), place_ref[0] % 2
    for high in range(sources // 2):
        for bit in range(2):

            @pl.when((pair == high) & (low_bit == bit))
            def _():
                for low in range(2):
                    for r in range(rounds):
                        at = (low * rounds + r) * HEAD_DIM
                        outs[r * sources + 2 * high + (low ^ bit)][0] = result[at : at + HEAD_DIM]


def project(place, tokens, rows, gain, shift, weight, bias, sources, rounds):
    tok_here, width = tokens.shape
    pair = 2 * rounds * HEAD_DIM
    pairs = sources // 2
    block_of = lambda i, p: i // pairs * pairs + (i % pairs ^ p[0] // 2)
    out = pl.pallas_call(
        partial(project_kernel, sources=sources, rounds=rounds, block=tok_here // 4),
        grid_spec=pltpu.PrefetchScalarGridSpec(
            num_scalar_prefetch=1,
            grid=(3 * pairs,),
            in_specs=[
                whole(tok_here, width),
                whole(2, width),
                whole(1, width),
                whole(1, width),
                pl.BlockSpec((width, pair), lambda i, p: (0, block_of(i, p))),
                pl.BlockSpec((pair, 1), lambda i, p: (block_of(i, p), 0)),
            ],
            out_specs=[whole(tok_here, width)]
            + [pl.BlockSpec((1, HEAD_DIM, tok_here), lambda i, p: (i // pairs, 0, 0))] * (rounds * sources),
            scratch_shapes=[pltpu.VMEM((width, tok_here), BF16)],
        ),
        out_shape=[jax.ShapeDtypeStruct((tok_here, width), BF16)]
        + [jax.ShapeDtypeStruct((3, HEAD_DIM, tok_here), BF16)] * (rounds * sources),
        compiler_params=pltpu.CompilerParams(vmem_limit_bytes=SMALL_VMEM),
        cost_estimate=pl.CostEstimate(
            flops=2 * tok_here * weight.size, transcendentals=0, bytes_accessed=4 * weight.size
        ),
        name="project",
    )(place, tokens, rows, gain, shift, weight, bias)
    return out[0], [out[1 + r * sources : 1 + (r + 1) * sources] for r in range(rounds)]


def mlp_kernel(place_ref, *refs, groups, sources, block):
    (in_groups, out_groups), rounds = groups, sum(map(len, groups[0]))
    gathered, refs = refs[: len(in_groups) * sources], refs[len(in_groups) * sources :]
    pieces = len(out_groups) * sources
    tokens, rows, cotangent, out_w, out_b, gain, shift, up_w, up_b, down_w, down_b = refs[:11]
    result, g_resid = refs[11:13]
    sent_grads = refs[13 : 13 + pieces]
    send, keep, vectors, g_up_b = refs[13 + pieces : 17 + pieces]
    attended, normed, resid, gelu_act, g_up, down_sum, g_normed, g_branch, g_attended = refs[17 + pieces :]
    step, last = pl.program_id(0), pl.num_programs(0) - 1
    tok_here, width = tokens.shape
    count = tok_here // block
    place = place_ref[0]
    low_bit = place % 2 == 0

    def head_rows(groups):
        for index in range(len(groups) * sources):
            group, j = divmod(index, sources)
            for at, r in enumerate(groups[group]):
                start = ((place ^ j) * rounds + r) * HEAD_DIM
                yield index, at, pl.ds(pl.multiple_of(start, HEAD_DIM), HEAD_DIM)

    def put(slot, grad):
        grad = grad.astype(BF16)
        middle = grad.shape[1] // 2
        left, right = grad[:, :middle], grad[:, middle:]

        @pl.when(low_bit)
        def _():
            keep[slot], send[slot] = left, right

        @pl.when(jnp.logical_not(low_bit))
        def _():
            keep[slot], send[slot] = right, left

    @pl.when(step == 0)
    def _():
        for index, at, here in head_rows(in_groups):
            attended[here, :] = gathered[index][at]

        def body(index, _):
            here = token_block(index, block)
            row = rows[pl.ds(index // (count // 2), 1), :]
            hidden = tokens[here, :].astype(F32) + row
            total = hidden + (dot(attended[:, here], out_w[...], TN) + out_b[...])
            resid[here, :] = total
            scaled, _ = normalize(total)
            normed[here, :] = (scaled * gain[...] + shift[...]).astype(BF16)
            return 0

        lax.fori_loop(0, count, body, 0)
        down_sum[...] = jnp.zeros_like(down_sum)
        g_normed[...] = jnp.zeros_like(g_normed)

    @pl.when(step < last)
    def _():
        def body(index, total):
            here = token_block(index, block)
            act = dot(normed[here, :], up_w[...]) + up_b[...]
            g_gelu = dot(cotangent[here, :], down_w[...], NT)
            below = 0.5 * (1.0 + lax.erf(act * 0.7071067811865476))
            density = 0.3989422804014327 * jnp.exp(-0.5 * act * act)
            low = (act * below).astype(BF16)
            grad = (g_gelu * (below + act * density)).astype(BF16)
            gelu_act[here, :] = low
            g_up[here, :] = grad
            down_sum[here, :] += dot(low, down_w[...])
            g_normed[here, :] += dot(grad, up_w[...], NT)
            return total + column_sum(grad)

        g_up_b[...] = lax.fori_loop(0, count, body, jnp.zeros(up_b.shape, F32))
        put(0, dot(g_up[...], normed[...], TN))
        put(1, dot(cotangent[...], gelu_act[...], TN))

    @pl.when(step == last)
    def _():
        def body(index, sums):
            here = token_block(index, block)
            total = resid[here, :]
            result[here, :] = (total + (down_sum[here, :] + down_b[...])).astype(BF16)
            scaled, inverse = normalize(total)
            grad = g_normed[here, :]
            inner = grad * gain[...]
            g_out = cotangent[here, :].astype(F32)
            g_total = g_out + inverse * (
                inner
                - jnp.mean(inner, -1, keepdims=True)
                - scaled * jnp.mean(inner * scaled, -1, keepdims=True)
            )
            g_resid[here, :] = g_total
            low = g_total.astype(BF16)
            g_branch[here, :] = low
            g_attended[:, here] = dot(out_w[...], low, NT).astype(BF16)
            parts = (grad * scaled, grad, low, g_out)
            return tuple(old + column_sum(new) for old, new in zip(sums, parts))

        empty = jnp.zeros((1, width), F32)
        sums = lax.fori_loop(0, count, body, (empty,) * 4)
        for index, at, here in head_rows(out_groups):
            sent_grads[index][at] = g_attended[here, :]
        for index, total in enumerate(sums):
            vectors[index : index + 1, :] = total
        put(0, dot(g_branch[...], attended[...], (((0,), (1,)), ((), ()))))
        put(1, jnp.zeros((width, width), F32))


def mlp(place, groups, gathered, tokens, rows, cotangent, out_w, out_b, gain, shift, up_w, up_b, down_w, down_b):
    tok_here, width = tokens.shape
    hidden_units = up_w.shape[1]
    sources = len(gathered[0])
    pieces = [part for group in gathered for part in group]
    depth = pieces[0].shape[1]
    shapes = [(len(group), depth, tok_here) for group in groups[1] for _ in range(sources)]
    steps = hidden_units // width
    slots = pl.BlockSpec((2, width, width // 2), lambda j, b: (j, 0, 0))
    at = lambda j: jnp.minimum(j, steps - 1)
    slot_shape = jax.ShapeDtypeStruct((2 * steps + 2, width, width // 2), BF16)
    out = pl.pallas_call(
        partial(mlp_kernel, groups=groups, sources=sources, block=tok_here // 2),
        grid_spec=pltpu.PrefetchScalarGridSpec(
            num_scalar_prefetch=1,
            grid=(steps + 1,),
            in_specs=[whole(*part.shape) for part in pieces]
            + [
                whole(tok_here, width),
                whole(2, width),
                whole(tok_here, width),
                whole(width, width),
                whole(1, width),
                whole(1, width),
                whole(1, width),
                pl.BlockSpec((width, width), lambda j, b: (0, at(j))),
                pl.BlockSpec((1, width), lambda j, b: (0, at(j))),
                pl.BlockSpec((width, width), lambda j, b: (at(j), 0)),
                whole(1, width),
            ],
            out_specs=[whole(tok_here, width)] * 2
            + [whole(*shape) for shape in shapes]
            + [slots, slots, whole(4, width), pl.BlockSpec((1, width), lambda j, b: (0, at(j)))],
            scratch_shapes=[
                pltpu.VMEM((width, tok_here), BF16),
                pltpu.VMEM((tok_here, width), BF16),
                pltpu.VMEM((tok_here, width), F32),
                pltpu.VMEM((tok_here, width), BF16),
                pltpu.VMEM((tok_here, width), BF16),
                pltpu.VMEM((tok_here, width), F32),
                pltpu.VMEM((tok_here, width), F32),
                pltpu.VMEM((tok_here, width), BF16),
                pltpu.VMEM((width, tok_here), BF16),
            ],
        ),
        out_shape=[
            jax.ShapeDtypeStruct((tok_here, width), BF16),
            jax.ShapeDtypeStruct((tok_here, width), F32),
        ]
        + [jax.ShapeDtypeStruct(shape, BF16) for shape in shapes]
        + [
            slot_shape,
            slot_shape,
            jax.ShapeDtypeStruct((4, width), F32),
            jax.ShapeDtypeStruct((1, hidden_units), F32),
        ],
        compiler_params=pltpu.CompilerParams(vmem_limit_bytes=VMEM),
        cost_estimate=pl.CostEstimate(
            flops=12 * tok_here * up_w.size, transcendentals=0, bytes_accessed=8 * up_w.size
        ),
        name="mlp",
    )(place, *pieces, tokens, rows, cotangent, out_w, out_b, gain, shift, up_w, up_b, down_w, down_b)
    grads = out[2 : 2 + len(shapes)]
    grads = [grads[g * sources : (g + 1) * sources] for g in range(len(groups[1]))]
    return out[0], out[1], grads, out[-4:]


def finish_kernel(place_ref, *refs, rounds, sources, block):
    pieces = rounds * sources
    back, refs = refs[:pieces], refs[pieces:]
    weight, tokens, rows, gain, g_resid, vectors, g_up_b, g_tokens, sums, g_normed, packed = refs
    step, last = pl.program_id(0), pl.num_programs(0) - 1
    pair, low_bit = step % (sources // 2), place_ref[0] % 2
    for high in range(sources // 2):

        @pl.when(pair == high)
        def _():
            for j in range(2 * high, 2 * high + 2):
                for r in range(rounds):
                    at = ((j % 2 ^ low_bit) * rounds + r) * HEAD_DIM
                    packed[pl.ds(pl.multiple_of(at, HEAD_DIM), HEAD_DIM), :] = back[r * sources + j][0]

    pairs, size = sources // 2, packed.shape[0]
    ones = jnp.ones((8, packed.shape[1]), BF16)
    bias = dot(ones, packed[...], NT)[0:1]
    for part in range(3):
        for at in range(pairs):

            @pl.when((step // pairs == part) & ((pair ^ place_ref[0] // 2) == at))
            def _():
                sums[10 + part : 11 + part, at * size : (at + 1) * size] = bias

    added = dot(packed[...], weight[...], (((0,), (1,)), ((), ())))

    @pl.when(step == 0)
    def _():
        g_normed[...] = added

    @pl.when(step > 0)
    def _():
        g_normed[...] += added

    @pl.when(step == last)
    def _():
        width = tokens.shape[1]
        count = tokens.shape[0] // block
        empty = jnp.zeros((1, width), F32)

        def half(first):
            def body(index, totals):
                here = token_block(index + first * (count // 2), block)
                scaled, inverse = normalize(tokens[here, :].astype(F32) + rows[first : first + 1, :])
                grad = g_normed[here, :]
                inner = grad * gain[...]
                g_hidden = g_resid[here, :] + inverse * (
                    inner
                    - jnp.mean(inner, -1, keepdims=True)
                    - scaled * jnp.mean(inner * scaled, -1, keepdims=True)
                )
                g_tokens[here, :] = g_hidden.astype(BF16)
                parts = (grad * scaled, grad, g_hidden)
                return tuple(old + column_sum(new) for old, new in zip(totals, parts))

            return lax.fori_loop(0, count // 2, body, (empty,) * 3)

        one, two = half(0), half(1)
        sums[0:1, :], sums[1:2, :] = one[0] + two[0], one[1] + two[1]
        sums[2:6, :] = vectors[...]
        for index in range(4):
            sums[6 + index : 7 + index, :] = g_up_b[:, index * width : (index + 1) * width]
        sums[13:14, :] = empty
        is_short = place_ref[1] != 0
        sums[14:15, :] = jnp.where(is_short, one[2], one[2] + two[2])
        sums[15:16, :] = jnp.where(is_short, two[2], 0.0)


def finish(place, back, weight, tokens, rows, gain, g_resid, vectors, g_up_b):
    tok_here, width = tokens.shape
    rounds, sources = len(back), len(back[0])
    pieces = [part for group in back for part in group]
    pair = 2 * rounds * HEAD_DIM
    pairs = sources // 2
    return pl.pallas_call(
        partial(finish_kernel, rounds=rounds, sources=sources, block=tok_here // 4),
        grid_spec=pltpu.PrefetchScalarGridSpec(
            num_scalar_prefetch=1,
            grid=(3 * pairs,),
            in_specs=[pl.BlockSpec((1, HEAD_DIM, tok_here), lambda i, p: (i // pairs, 0, 0))] * len(pieces)
            + [
                pl.BlockSpec(
                    (width, pair), lambda i, p: (0, i // pairs * pairs + (i % pairs ^ p[0] // 2))
                ),
                whole(tok_here, width),
                whole(2, width),
                whole(1, width),
                whole(tok_here, width),
                whole(*vectors.shape),
                whole(*g_up_b.shape),
            ],
            out_specs=[whole(tok_here, width), whole(16, width)],
            scratch_shapes=[pltpu.VMEM((tok_here, width), F32), pltpu.VMEM((pair, tok_here), BF16)],
        ),
        out_shape=[
            jax.ShapeDtypeStruct((tok_here, width), BF16),
            jax.ShapeDtypeStruct((16, width), F32),
        ],
        compiler_params=pltpu.CompilerParams(vmem_limit_bytes=SMALL_VMEM),
        cost_estimate=pl.CostEstimate(
            flops=2 * tok_here * weight.size, transcendentals=0, bytes_accessed=8 * weight.size
        ),
        name="finish",
    )(place, *pieces, weight, tokens, rows, gain, g_resid, vectors, g_up_b)


def qkv_grad_kernel(block_ref, *refs, rounds, sources, order):
    grads, refs = refs[: rounds * sources], refs[rounds * sources :]
    normed, (first, second, store) = refs[:sources], refs[sources:]
    size = 3 * HEAD_DIM
    for r in range(rounds):
        total = None
        for grad, part in zip(grads[r * sources : (r + 1) * sources], normed):
            here = jnp.concatenate([grad[p] for p in range(3)], 0)
            term = dot(here, part[...])
            total = term if total is None else total + term
        store[:, r * size : (r + 1) * size] = total.T.astype(BF16)
    half = len(order) // 2
    rows = first.shape[1]
    for at, index in enumerate(order):
        start = (block_ref[0] ^ index) * rows
        here = pl.ds(pl.multiple_of(start, rows), rows) if half > 1 else slice(at * rows, (at + 1) * rows)
        (second if at >= half else first)[at % half] = store[here, :]


def qkv_grad(block, grads, normed, order):
    rounds, sources = len(grads), len(normed)
    tok_here, width = normed[0].shape
    size = 3 * HEAD_DIM * rounds
    pieces = [part for group in grads for part in group]
    half = (len(order) // 2, width // len(order), size)
    return pl.pallas_call(
        partial(qkv_grad_kernel, rounds=rounds, sources=sources, order=order),
        grid_spec=pltpu.PrefetchScalarGridSpec(
            num_scalar_prefetch=1,
            grid=(1,),
            in_specs=[whole(*pieces[0].shape)] * len(pieces) + [whole(tok_here, width)] * sources,
            out_specs=[whole(*half)] * 2,
            scratch_shapes=[pltpu.VMEM((width, size), BF16)],
        ),
        out_shape=[jax.ShapeDtypeStruct(half, BF16)] * 2,
        compiler_params=pltpu.CompilerParams(vmem_limit_bytes=SMALL_VMEM),
        cost_estimate=pl.CostEstimate(
            flops=8 * tok_here * width * size, transcendentals=0, bytes_accessed=12 * tok_here * width
        ),
        name="qkv_grad",
    )(block, *pieces, *normed)


def swap(values, axis, bit):
    size = lax.axis_size(axis)
    return lax.ppermute(values, axis, [(j, j ^ bit) for j in range(size)])


def trade(parts, axis):
    return [parts[0]] + [swap(part, axis, i) for i, part in enumerate(parts) if i]


def spread(values, axis, count):
    return [values] + [swap(values, axis, i) for i in range(1, count)]


def total_of(parts):
    total = parts[0].astype(F32)
    for part in parts[1:]:
        total = total + part.astype(F32)
    return total


def after(values, *others):
    return lax.optimization_barrier((values, *others))[0]


def deal_kernel(bits_ref, *refs, steps):
    keep, got, (outgoing, staying) = refs[: steps + 2], refs[steps + 2 : 2 * steps + 4], refs[-2:]
    gate = bits_ref[0]
    for out, side in ((outgoing, 1 - gate), (staying, gate)):
        at = 0
        for left, right in zip(keep, got):
            rows = left.shape[2] // 2
            here = pl.ds(pl.multiple_of(side * rows, rows), rows)
            total = left[0, 0, here, :].astype(F32) + right[0, 0, here, :].astype(F32)
            out[0, at : at + rows, :] = total.astype(BF16)
            at += rows


def deal(gate, keep, got, dp):
    slots, width, lanes = keep.shape
    steps = slots // 2 - 1
    up_each, each = width * steps // dp, width // dp
    per_slot = width // up_each
    up = pl.BlockSpec(
        (1, 1, up_each, lanes),
        lambda i, b: (2 * (i // per_slot), i % per_slot, 0, 0),
    )
    rest = [
        pl.BlockSpec((1, 1, each, lanes), lambda i, b, slot=slot: (slot, i, 0, 0))
        for slot in [2 * k + 1 for k in range(steps)] + [2 * steps]
    ]
    views = lambda array: [array.reshape(slots, per_slot, up_each, lanes)] + [
        array.reshape(slots, dp, each, lanes)
    ] * (steps + 1)
    rows = up_each // 2 + (steps + 1) * each // 2
    shape = jax.ShapeDtypeStruct((dp, rows, lanes), BF16)
    return pl.pallas_call(
        partial(deal_kernel, steps=steps),
        grid_spec=pltpu.PrefetchScalarGridSpec(
            num_scalar_prefetch=1,
            grid=(dp,),
            in_specs=([up] + rest) * 2,
            out_specs=[pl.BlockSpec((1, rows, lanes), lambda i, b: (i, 0, 0))] * 2,
        ),
        out_shape=[shape, shape],
        cost_estimate=pl.CostEstimate(flops=keep.size, transcendentals=0, bytes_accessed=6 * keep.size),
        name="deal",
    )(gate, *views(keep), *views(got))


def undeal_kernel(place_ref, *refs, sources, steps, each):
    shares, (up, down, out, store) = refs[:sources], refs[sources:]
    lanes = store.shape[2]
    for j, share in enumerate(shares):
        store[place_ref[0] ^ j] = share[...].astype(F32)
    wide = steps * each
    for low in range(2):
        both = lambda at, size: jnp.concatenate([store[low, at : at + size], store[2 + low, at : at + size]], 0).T
        up[low * lanes : (low + 1) * lanes, :] = both(0, wide)
        for k in range(steps):
            at = (2 * k + low) * lanes
            down[at : at + lanes, :] = both(wide + k * each, each)
        out[low * lanes : (low + 1) * lanes, :] = both(2 * wide, each)


def undeal(place, shares, steps, width, dp):
    rows, lanes = shares[0].shape
    shapes = [(width, width * steps // dp), (width * steps, width // dp), (width, width // dp)]
    return pl.pallas_call(
        partial(undeal_kernel, sources=len(shares), steps=steps, each=width // dp // 2),
        grid_spec=pltpu.PrefetchScalarGridSpec(
            num_scalar_prefetch=1,
            grid=(1,),
            in_specs=[whole(rows, lanes)] * len(shares),
            out_specs=[whole(*shape) for shape in shapes],
            scratch_shapes=[pltpu.VMEM((len(shares), rows, lanes), F32)],
        ),
        out_shape=[jax.ShapeDtypeStruct(shape, F32) for shape in shapes],
        cost_estimate=pl.CostEstimate(flops=0, transcendentals=0, bytes_accessed=24 * rows * lanes),
        name="undeal",
    )(place, *shares)


def turn_kernel(*refs):
    *parts, out = refs
    half = len(parts) // 2
    at = 0
    for kept, got in zip(parts[:half], parts[half:]):
        total = (kept[0].astype(F32) + got[...].astype(F32)).T.astype(BF16)
        out[at : at + total.shape[0], :] = total
        at += total.shape[0]


def turn(kept, got):
    columns, rows = sum(part.shape[1] for part in got), got[0].shape[0]
    return pl.pallas_call(
        turn_kernel, out_shape=jax.ShapeDtypeStruct((columns, rows), BF16), name="turn"
    )(*kept, *got)


def regroup_kernel(place_ref, *refs, rounds):
    *shares, out = refs
    sources = len(shares)
    for j, share in enumerate(shares):
        for r in range(rounds):
            for p in range(3):
                at = ((p * sources + (place_ref[0] ^ j)) * rounds + r) * HEAD_DIM
                start = (r * 3 + p) * HEAD_DIM
                out[pl.ds(pl.multiple_of(at, HEAD_DIM), HEAD_DIM), :] = share[start : start + HEAD_DIM]


def regroup(place, shares, rounds):
    columns, rows = shares[0].shape
    total = columns * len(shares)
    return pl.pallas_call(
        partial(regroup_kernel, rounds=rounds),
        grid_spec=pltpu.PrefetchScalarGridSpec(
            num_scalar_prefetch=1,
            grid=(1,),
            in_specs=[whole(columns, rows)] * len(shares),
            out_specs=whole(total, rows),
        ),
        out_shape=jax.ShapeDtypeStruct((total, rows), BF16),
        name="regroup",
    )(place, *shares)


def stack_kernel(parts, out):
    rows = parts.shape[2]
    for index in range(parts.shape[0]):
        out[index * rows : (index + 1) * rows, :] = parts[index].astype(F32).T


def stack_rows(parts):
    count, columns, rows = parts.shape
    return pl.pallas_call(
        stack_kernel, out_shape=jax.ShapeDtypeStruct((rows * count, columns), F32), name="stack_rows"
    )(parts)


def exchange(values, axis):
    return lax.all_to_all(values, axis, split_axis=0, concat_axis=0, tiled=True)


def wide_sums(slots, place, dp):
    steps, width, lanes = slots.shape[0] // 2 - 1, slots.shape[1], slots.shape[2]
    pairs = slots.reshape(steps + 1, 2, width, lanes)
    up = pairs[:steps, 0].reshape(dp, 2, -1, lanes)
    down = pairs[:steps, 1].reshape(steps, dp, 2, -1, lanes)
    down = jnp.moveaxis(down, 0, 2).reshape(dp, 2, -1, lanes)
    out = pairs[steps, 0].reshape(dp, 2, -1, lanes)
    dealt = jnp.concatenate([up, down, out], 2)
    gate = place // 2
    pick = lambda index: lax.dynamic_index_in_dim(dealt, index, 1, keepdims=False)
    half_sum = total_of([pick(gate), swap(pick(1 - gate), "seq", 2)]).astype(BF16)
    share = jnp.sum(exchange(half_sum, "dp").astype(F32), 0).astype(BF16)
    shares = lax.all_gather(share, "seq", axis=0).reshape(2, 2, -1, lanes).astype(F32)
    each = width // dp // 2
    up, down, out = jnp.split(shares, [steps * each, 2 * steps * each], 2)
    turned = lambda part: jnp.transpose(part, (1, 3, 0, 2)).reshape(2 * lanes, -1)
    down = down.reshape(2, 2, steps, each, lanes)
    down = jnp.transpose(down, (2, 1, 4, 0, 3)).reshape(steps * 2 * lanes, 2 * each)
    return turned(up), down, turned(out)


def wide_columns(grads, dp, sources, rounds):
    grad = jnp.concatenate(grads, 2).reshape(-1, 3 * HEAD_DIM * rounds)
    width, columns = grad.shape
    rows = width // dp
    summed = jnp.sum(exchange(grad.reshape(dp, rows, columns), "dp").astype(F32), 0).astype(BF16)
    gathered = lax.all_gather(summed, "seq", axis=0).reshape(sources, rows, rounds, 3, HEAD_DIM)
    ordered = jnp.transpose(gathered, (1, 3, 0, 2, 4)).reshape(rows, dp, -1)
    return exchange(jnp.swapaxes(ordered, 0, 1), "dp").reshape(width, -1).astype(F32)


def on_device(
    tokens,
    time_steps,
    data_group,
    cotangent,
    attn_norm_gain,
    attn_norm_bias,
    qkv_weight,
    query_bias,
    value_bias,
    out_weight,
    out_bias,
    mlp_norm_gain,
    mlp_norm_bias,
    up_weight,
    up_bias,
    down_weight,
    down_bias,
    time_table,
):
    sources, dp = lax.axis_size("seq"), lax.axis_size("dp")
    place, block = lax.axis_index("seq"), lax.axis_index("dp")
    tokens, cotangent = tokens[0], cotangent[0]
    tok_here, width = tokens.shape
    hidden_units = up_weight.shape[1]
    rounds = HEADS // sources
    is_short = data_group[0] == 0
    short_flag = is_short.astype(jnp.int32)[None]
    rows = time_table[jnp.where(is_short, time_steps[0], time_steps[0, 0])].astype(F32)
    flat = lambda vector: vector.astype(F32)[None]
    qkv_bias = jnp.concatenate([query_bias, jnp.zeros_like(query_bias), value_bias]).astype(F32)

    place_arg = place.astype(jnp.int32)[None]
    block_arg = block.astype(jnp.int32)[None]
    few = dp <= 8

    normed, sending = project(
        place_arg,
        tokens,
        rows,
        flat(attn_norm_gain),
        flat(attn_norm_bias),
        qkv_weight,
        qkv_bias[:, None],
        sources,
        rounds,
    )
    heads, mixed, logs, sent = [trade(sending[0], "seq")], [], [], []
    returned = []
    for r in range(rounds):
        if r + 1 < rounds:
            ahead = sending[r + 1] if r < 1 else after(sending[r + 1], logs[r - 1])
            heads.append(trade(ahead, "seq"))
        out, full, log = attend(short_flag, heads[r], sent[0] if r == 1 else ())
        mixed.append(full)
        logs.append(log)
        sent.append(out)
        if r >= 1:
            returned.append(trade(out, "seq"))

    across = swap(after(normed, log), "seq", 2)
    groups = (((0, 1), (2,)), ((0,), (1, 2)))
    result, g_resid, sent_grads, (send, keep, vectors, g_up_b) = mlp(
        place_arg,
        groups,
        returned,
        tokens,
        rows,
        cotangent,
        out_weight,
        flat(out_bias),
        flat(mlp_norm_gain),
        flat(mlp_norm_bias),
        up_weight,
        flat(up_bias),
        down_weight,
        flat(down_bias),
    )
    got = swap(send, "seq", 1)
    first_grads = trade(sent_grads[0], "seq")
    if few:
        outgoing, staying = deal(place_arg // 2, keep, got, dp)
        got = swap(outgoing, "seq", 2)
        ready = outgoing
    else:
        ready = summed = total_of([keep, got]).astype(BF16)
    rest_grads = trade(sent_grads[1], "seq")
    beside = [normed, swap(normed, "seq", 1), across, swap(across, "seq", 1)]
    held = after(heads[0], ready)
    grads = [attend_back(short_flag, held, mixed[0], first_grads, logs[0], 0)]
    back = [trade(grads[0], "seq")]
    grads.append(attend_back(short_flag, heads[1], mixed[1], rest_grads, logs[1], 0))
    back.append(trade(grads[1], "seq"))
    order = (0, 4, 2, 6, 1, 5, 3, 7) if few else (0, 1)
    stay_a, away_a = qkv_grad(block_arg, grads, beside, order)
    if few:
        got_a = swap(away_a, "dp", 1)
        half_sum = total_of([staying, after(got, grads[1])]).astype(BF16)
        dealt = exchange(half_sum, "dp")
        ready = half_sum
    held = after(heads[2], stay_a, ready, *back[0])
    grads.append(attend_back(short_flag, held, mixed[2], rest_grads, logs[2], 1))
    back.append(trade(grads[2], "seq"))
    grads[2] = after(grads[2], *back[1])
    stay_b, away_b = qkv_grad(block_arg, grads[2:], beside, order)
    if few:
        parts = [stay_a, stay_b], [after(got_a, grads[2]), swap(away_b, "dp", 1)]
        for bit in (2, 4):
            kept = [total_of(pair).astype(BF16) for pair in zip(*parts)]
            size = kept[0].shape[0] // 2
            parts = [part[:size] for part in kept], [swap(part[size:], "dp", bit) for part in kept]
        summed = turn(parts[0], [part[0] for part in parts[1]])
        columns = regroup(place_arg, spread(summed, "seq", sources), rounds)

    flags = jnp.concatenate([place_arg, short_flag])
    g_tokens, small = finish(
        flags, back, qkv_weight, tokens, rows, flat(attn_norm_gain), g_resid, vectors, g_up_b
    )
    for bit in (1, 2):
        small = small + swap(small, "seq", bit)
    by_block = (jnp.arange(dp) == block)[:, None]
    row_slot = jnp.where(by_block[:, :, None], small[None, 14:], 0.0).reshape(-1, width)
    small = jnp.concatenate([small[:14], row_slot])
    steps = jnp.where(by_block, time_steps.astype(F32), 0.0)
    bit = 1
    while bit < dp:
        small = small + swap(small, "dp", bit)
        steps = steps + swap(steps, "dp", bit)
        bit *= 2
    if few:
        share = total_of([dealt[i] for i in range(dp)]).astype(BF16)
        shares = spread(share, "seq", sources)
        sum_up, sum_down, sum_out = undeal(place_arg, shares, hidden_units // width, width, dp)
        sum_qkv = stack_rows(exchange(columns.reshape(dp, 3 * width // dp, width // dp), "dp"))
    else:
        sum_up, sum_down, sum_out = wide_sums(summed, place, dp)
        sum_qkv = wide_columns(
            [jnp.stack(pair).reshape(2, width // 2, -1) for pair in ((stay_a, away_a), (stay_b, away_b))],
            dp,
            sources,
            rounds,
        )
    share_cols = width // dp
    rows_mine = lax.dynamic_slice_in_dim(small[14:], block * share_cols, share_cols, 1)
    table_rows = time_table.shape[0]
    hits = jnp.arange(table_rows, dtype=jnp.int32)[:, None] == steps.reshape(1, -1).astype(jnp.int32)
    sum_table = jnp.dot(hits.astype(F32), rows_mine, precision=lax.Precision.HIGHEST)
    return (
        result[None],
        g_tokens[None],
        small[0],
        small[1],
        sum_qkv,
        small[10],
        small[12],
        sum_out,
        small[4],
        small[2],
        small[3],
        sum_up,
        small[6:10].reshape(-1),
        sum_down,
        small[5],
        sum_table,
    )


def solution(mesh):
    placed = (P("dp", "seq", None), P("dp", None), P("dp"), P("dp", "seq", None)) + (P(),) * 14
    column = P(None, "dp")
    return jax.shard_map(
        on_device,
        mesh=mesh,
        in_specs=placed,
        out_specs=(
            P("dp", "seq", None),
            P("dp", "seq", None),
            P(),
            P(),
            column,
            P(),
            P(),
            column,
            P(),
            P(),
            P(),
            column,
            P(),
            column,
            P(),
            column,
        ),
        check_vma=False,
    )
```

```python
from functools import partial

import jax
import jax.numpy as jnp
from jax import lax
from jax.experimental import pallas as pl
from jax.experimental.pallas import tpu as pltpu
from jax.sharding import PartitionSpec as P

HEADS = 12
HEAD_DIM = 64
EPSILON = 1e-05
LOG2E = 1.4426950408889634
SCALE = HEAD_DIM**-0.5
BF16 = jnp.bfloat16
F32 = jnp.float32
NN = (((1,), (0,)), ((), ()))
NT = (((1,), (1,)), ((), ()))
TN = (((0,), (0,)), ((), ()))
VMEM = 62 << 20
SMALL_VMEM = 40 << 20


def dot(left, right, dims=NN):
    return lax.dot_general(left, right, dims, preferred_element_type=F32)


def split_low(values, count):
    parts = []
    for _ in range(count):
        term = values.astype(BF16)
        parts.append(term)
        values = values - term.astype(F32)
    return parts


def whole(*shape):
    return pl.BlockSpec(shape, lambda *_: (0,) * len(shape))


def halves(sources, segment):
    for chunk in range(2 * sources):
        source, part = divmod(chunk, 2)
        yield chunk, source, slice(part * segment, (part + 1) * segment)


def over_chunks(short_ref, chunks, body):
    is_short = short_ref[0] != 0
    part = lax.rem(pl.program_id(0), 2)

    @pl.when(is_short)
    def _():
        body([2 * k + part for k in range(chunks // 2)], True)

    @pl.when(jnp.logical_not(is_short))
    def _():
        body(list(range(chunks)), True)


def attend_kernel(short_ref, *refs, sources, segment, held):
    heads, refs = refs[:sources], refs[sources:]
    earlier, refs = refs[: sources * held], refs[sources * held :]
    sent, refs = refs[:sources], refs[sources:]
    mixed_ref, inverse_ref, weights_ref, queries, keys, values, sums, bounded = refs
    step = pl.program_id(0)
    chunks = 2 * sources
    depth = HEAD_DIM

    @pl.when(step == 0)
    def _():
        for old, new in zip(earlier, sent):
            new[0] = old[0]
        longest = [jnp.zeros((1, segment), F32)] * 2
        for chunk, source, cols in halves(sources, segment):
            scaled = heads[source][0, :, cols].astype(F32) * (SCALE * LOG2E)
            high, low = split_low(scaled, 2)
            queries[chunk, 0:64, :] = high
            queries[chunk, 64:128, :] = low
            queries[chunk, 128:144, :] = jnp.zeros((16, segment), BF16)
            key = heads[source][1, :, cols]
            keys[chunk, 0:64, :] = key
            keys[chunk, 64:128, :] = key
            keys[chunk, 128:144, :] = jnp.full((16, segment), -1.0, BF16)
            values[chunk, 0:64, :] = heads[source][2, :, cols]
            values[chunk, 64:80, :] = jnp.ones((16, segment), BF16)
            sizes = [jnp.sum(x * x, 0, keepdims=True) for x in (scaled, key.astype(F32))]
            longest = [jnp.maximum(old, new) for old, new in zip(longest, sizes)]
        bound = jnp.max(longest[0]) * jnp.max(longest[1])
        bounded[0] = (bound <= 3600.0).astype(jnp.int32)

    @pl.when(bounded[0] == 0)
    def _():
        query = queries[step][0:128]
        is_short = (short_ref[0] != 0).astype(jnp.int32)

        def body(index, peak):
            chunk = jnp.where(is_short != 0, 2 * index + lax.rem(step, 2), index)
            scores = dot(keys[chunk][0:128], query, TN)
            return jnp.maximum(peak, jnp.max(scores, 0, keepdims=True))

        start = jnp.full((1, segment), -jnp.inf, F32)
        peak = lax.fori_loop(0, jnp.where(is_short != 0, chunks // 2, chunks), body, start)
        zeros = jnp.zeros((13, segment), BF16)
        queries[step, 128:144, :] = jnp.concatenate(split_low(peak, 3) + [zeros], 0)

    def body(order, first):
        query = queries[step]
        total = None
        later = dot(keys[order[0]], query, TN)
        for index, chunk in enumerate(order):
            scores = later
            if index + 1 < len(order):
                later = dot(keys[order[index + 1]], query, TN)
            weights = jnp.exp2(scores).astype(BF16)
            weights_ref[0, chunk] = weights.T
            mixed = dot(values[chunk], weights)
            total = mixed if total is None else total + mixed
        sums[...] = total if first else sums[...] + total

    over_chunks(short_ref, chunks, body)
    total = sums[...]
    inverse = 1.0 / total[depth : depth + 1, :]
    result = total[:depth] * inverse
    mixed_ref[step] = result
    inverse_ref[step] = inverse
    for chunk, source, cols in halves(sources, segment):

        @pl.when(step == chunk)
        def _():
            sent[source][held, :, cols] = result.astype(BF16)


def attend(is_short, heads, earlier=()):
    sources = len(heads)
    _, depth, tokens = heads[0].shape
    segment, chunks = tokens // 2, 2 * sources
    work = (sources * tokens) ** 2
    held = len(earlier) // sources
    out = pl.pallas_call(
        partial(attend_kernel, sources=sources, segment=segment, held=held),
        grid_spec=pltpu.PrefetchScalarGridSpec(
            num_scalar_prefetch=1,
            grid=(chunks,),
            in_specs=[whole(3, depth, tokens)] * sources + [whole(1, depth, tokens)] * len(earlier),
            out_specs=[whole(1 + held, depth, tokens)] * sources
            + [
                whole(chunks, depth, segment),
                whole(chunks, 1, segment),
                pl.BlockSpec((1, chunks, segment, segment), lambda i, s: (i, 0, 0, 0)),
            ],
            scratch_shapes=[
                pltpu.VMEM((chunks, 144, segment), BF16),
                pltpu.VMEM((chunks, 144, segment), BF16),
                pltpu.VMEM((chunks, 80, segment), BF16),
                pltpu.VMEM((80, segment), F32),
                pltpu.SMEM((1,), jnp.int32),
            ],
        ),
        out_shape=[jax.ShapeDtypeStruct((1 + held, depth, tokens), BF16)] * sources
        + [
            jax.ShapeDtypeStruct((chunks, depth, segment), F32),
            jax.ShapeDtypeStruct((chunks, 1, segment), F32),
            jax.ShapeDtypeStruct((chunks, chunks, segment, segment), BF16),
        ],
        compiler_params=pltpu.CompilerParams(vmem_limit_bytes=SMALL_VMEM),
        cost_estimate=pl.CostEstimate(
            flops=16 * work * depth, transcendentals=work, bytes_accessed=2 * work
        ),
        name="attend",
    )(is_short, *heads, *earlier)
    return out[:sources], out[-3:]


def attend_back_kernel(short_ref, *refs, sources, segment):
    heads, grads, (mixed_ref, inverse_ref, weights_ref), refs = (
        refs[:sources],
        refs[sources : 2 * sources],
        refs[2 * sources : 2 * sources + 3],
        refs[2 * sources + 3 :],
    )
    outs, (queries, g_aug, v_aug, grad_q, grad_kv) = refs[:sources], refs[sources:]
    step = pl.program_id(0)
    chunks = 2 * sources

    @pl.when(step == 0)
    def _():
        zeros = jnp.zeros((13, segment), BF16)
        for chunk, source, cols in halves(sources, segment):
            queries[chunk] = heads[source][0, :, cols]
            grad = grads[source][0, :, cols].astype(F32) * inverse_ref[chunk]
            high, low = split_low(grad, 2)
            g_aug[chunk, 0:64, :] = high
            g_aug[chunk, 64:128, :] = low
            inner = jnp.sum(grad * mixed_ref[chunk], 0, keepdims=True)
            g_aug[chunk, 128:144, :] = jnp.concatenate(split_low(inner, 3) + [zeros], 0)
        grad_q[...] = jnp.zeros_like(grad_q)

    def column(index):
        for chunk, source, cols in halves(sources, segment):

            @pl.when(step == chunk)
            def _():
                index(source, cols)

    def load(source, cols):
        value = heads[source][2, :, cols]
        v_aug[0:64, :] = value
        v_aug[64:128, :] = value
        v_aug[128:144, :] = jnp.full((16, segment), -1.0, BF16)
        v_aug[144:208, :] = heads[source][1, :, cols]

    column(load)
    value = v_aug[0:144]
    turned = v_aug[144:208].T

    def body(order, first):
        key_total = value_total = None
        later = dot(g_aug[order[0]], value, TN)
        for index, chunk in enumerate(order):
            slopes = later
            if index + 1 < len(order):
                later = dot(g_aug[order[index + 1]], value, TN)
            weights = weights_ref[chunk, 0]
            g_scores = (weights.astype(F32) * slopes).astype(BF16)
            value_part = dot(g_aug[chunk, 0:128, :], weights)
            key_part = dot(queries[chunk], g_scores)
            value_total = value_part if value_total is None else value_total + value_part
            key_total = key_part if key_total is None else key_total + key_part
            grad_q[chunk] += dot(g_scores, turned)
        both = jnp.concatenate([key_total, value_total[0:64] + value_total[64:128]], 0)
        grad_kv[...] = both if first else grad_kv[...] + both

    over_chunks(short_ref, chunks, body)

    def save(source, cols):
        outs[source][1, :, cols] = (grad_kv[0:64] * SCALE).astype(BF16)
        outs[source][2, :, cols] = grad_kv[64:128].astype(BF16)

    column(save)

    @pl.when(step == chunks - 1)
    def _():
        for chunk, source, cols in halves(sources, segment):
            outs[source][0, :, cols] = (grad_q[chunk] * SCALE).T.astype(BF16)


def attend_back(is_short, heads, saved, grads, at):
    sources = len(heads)
    _, depth, tokens = heads[0].shape
    segment, chunks = tokens // 2, 2 * sources
    work = (sources * tokens) ** 2
    return pl.pallas_call(
        partial(attend_back_kernel, sources=sources, segment=segment),
        grid_spec=pltpu.PrefetchScalarGridSpec(
            num_scalar_prefetch=1,
            grid=(chunks,),
            in_specs=[whole(3, depth, tokens)] * sources
            + [pl.BlockSpec((1, depth, tokens), lambda i, s: (at, 0, 0))] * sources
            + [
                whole(chunks, depth, segment),
                whole(chunks, 1, segment),
                pl.BlockSpec((chunks, 1, segment, segment), lambda i, s: (0, i, 0, 0)),
            ],
            out_specs=[whole(3, depth, tokens)] * sources,
            scratch_shapes=[
                pltpu.VMEM((chunks, 64, segment), BF16),
                pltpu.VMEM((chunks, 144, segment), BF16),
                pltpu.VMEM((208, segment), BF16),
                pltpu.VMEM((chunks, segment, depth), F32),
                pltpu.VMEM((2 * depth, segment), F32),
            ],
        ),
        out_shape=[jax.ShapeDtypeStruct((3, depth, tokens), BF16)] * sources,
        compiler_params=pltpu.CompilerParams(vmem_limit_bytes=VMEM),
        cost_estimate=pl.CostEstimate(
            flops=40 * work * depth, transcendentals=work, bytes_accessed=2 * work
        ),
        name="attend_back",
    )(is_short, *heads, *grads, *saved)


def normalize(hidden):
    center = hidden - jnp.mean(hidden, -1, keepdims=True)
    spread = jnp.mean(center * center, -1, keepdims=True)
    inverse = lax.rsqrt(spread + EPSILON)
    return center * inverse, inverse


def token_block(index, size):
    return pl.ds(pl.multiple_of(index * size, size), size)


def column_sum(values):
    return jnp.sum(values.astype(F32), 0, keepdims=True)


def row_of(vector):
    return vector[...].astype(F32)[None, :]


def project_kernel(
    scalars, tokens, first_rows, second_rows, gain, shift, weight, query_bias, value_bias, normed, rows, *refs,
    sources, rounds, block
):
    outs, turned, column = refs[:-2], refs[-2], refs[-1]
    step = pl.program_id(0)
    pairs = sources // 2
    count = tokens.shape[0] // block
    size = column.shape[1]

    @pl.when(step == 0)
    def _():
        for index, group in enumerate((first_rows, second_rows)):
            all_rows = group[...].astype(F32)
            chosen = lax.broadcasted_iota(jnp.int32, all_rows.shape, 0) == scalars[4 + index]
            rows[index : index + 1, :] = jnp.sum(jnp.where(chosen, all_rows, 0.0), 0, keepdims=True)
        biases = row_of(query_bias), jnp.zeros((1, pairs * size), F32), row_of(value_bias)
        for part, bias in enumerate(biases):
            for pair in range(pairs):
                here = jnp.broadcast_to(bias[:, pair * size : (pair + 1) * size], (128, size))
                column[part * pairs + pair] = here.T

        def body(index, _):
            here = token_block(index, block)
            row = rows[pl.ds(lax.div(index, count // 2), 1), :]
            scaled, _ = normalize(tokens[here, :].astype(F32) + row)
            low = (scaled * row_of(gain) + row_of(shift)).astype(BF16)
            normed[here, :] = low
            turned[:, here] = low.T
            return 0

        lax.fori_loop(0, count, body, 0)

    pair, high_bit, low_bit = lax.rem(step, pairs), lax.div(scalars[0], 2), lax.rem(scalars[0], 2)
    bias = column[step - pair + (pair ^ high_bit)][:, 0:1]
    result = (dot(weight[...], turned[...], TN) + bias).astype(BF16)
    for high in range(pairs):
        for bit in range(2):

            @pl.when((pair == high) & (low_bit == bit))
            def _():
                for low in range(2):
                    for r in range(rounds):
                        at = (low * rounds + r) * HEAD_DIM
                        outs[r * sources + 2 * high + (low ^ bit)][0] = result[at : at + HEAD_DIM]


def project(scalars, tokens, time_table, gain, shift, weight, query_bias, value_bias, sources, rounds):
    tok_here, width = tokens.shape
    pair = 2 * rounds * HEAD_DIM
    pairs = sources // 2
    group = lambda index: pl.BlockSpec((8, width), lambda i, p: (p[2 + index], 0))
    out = pl.pallas_call(
        partial(project_kernel, sources=sources, rounds=rounds, block=tok_here // 4),
        grid_spec=pltpu.PrefetchScalarGridSpec(
            num_scalar_prefetch=1,
            grid=(3 * pairs,),
            in_specs=[
                whole(tok_here, width),
                group(0),
                group(1),
                whole(width),
                whole(width),
                pl.BlockSpec((width, pair), lambda i, p: (0, pair_block(i, p, pairs))),
                whole(width),
                whole(width),
            ],
            out_specs=[whole(tok_here, width), whole(2, width)]
            + [pl.BlockSpec((1, HEAD_DIM, tok_here), lambda i, p: (lax.div(i, pairs), 0, 0))]
            * (rounds * sources),
            scratch_shapes=[
                pltpu.VMEM((width, tok_here), BF16),
                pltpu.VMEM((3 * pairs, pair, 128), F32),
            ],
        ),
        out_shape=[
            jax.ShapeDtypeStruct((tok_here, width), BF16),
            jax.ShapeDtypeStruct((2, width), F32),
        ]
        + [jax.ShapeDtypeStruct((3, HEAD_DIM, tok_here), BF16)] * (rounds * sources),
        compiler_params=pltpu.CompilerParams(vmem_limit_bytes=VMEM),
        cost_estimate=pl.CostEstimate(
            flops=2 * tok_here * weight.size, transcendentals=0, bytes_accessed=4 * weight.size
        ),
        name="project",
    )(scalars, tokens, time_table, time_table, gain, shift, weight, query_bias, value_bias)
    return out[0], out[1], [out[2 + r * sources : 2 + (r + 1) * sources] for r in range(rounds)]


def pair_block(step, scalars, pairs):
    at = lax.rem(step, pairs)
    return step - at + (at ^ lax.div(scalars[0], 2))


def mlp_kernel(place_ref, *refs, groups, sources, block):
    (in_groups, out_groups), rounds = groups, sum(map(len, groups[0]))
    gathered, refs = refs[: len(in_groups) * sources], refs[len(in_groups) * sources :]
    pieces = len(out_groups) * sources
    tokens, rows, cotangent, out_w, out_b, gain, shift, up_w, up_b, down_w, down_b = refs[:11]
    result, g_resid = refs[11:13]
    sent_grads = refs[13 : 13 + pieces]
    send, keep, vectors, g_up_b = refs[13 + pieces : 17 + pieces]
    attended, normed, resid, gelu_act, g_up, down_sum, g_normed, g_branch, g_attended, bias = refs[17 + pieces :]
    step, last = pl.program_id(0), pl.num_programs(0) - 1
    tok_here, width = tokens.shape
    count = tok_here // block
    place = place_ref[0]
    low_bit = lax.rem(place, 2) == 0

    def head_rows(groups):
        for index in range(len(groups) * sources):
            group, j = divmod(index, sources)
            for at, r in enumerate(groups[group]):
                start = ((place ^ j) * rounds + r) * HEAD_DIM
                yield index, at, pl.ds(pl.multiple_of(start, HEAD_DIM), HEAD_DIM)

    def put(slot, grad):
        grad = grad.astype(BF16)
        middle = grad.shape[1] // 2
        left, right = grad[:, :middle], grad[:, middle:]

        @pl.when(low_bit)
        def _():
            keep[slot], send[slot] = left, right

        @pl.when(jnp.logical_not(low_bit))
        def _():
            keep[slot], send[slot] = right, left

    @pl.when(step == 0)
    def _():
        bias_row = row_of(up_b)
        for index in range(bias.shape[0]):
            bias[index : index + 1, :] = bias_row[:, index * width : (index + 1) * width]
        for index, at, here in head_rows(in_groups):
            attended[here, :] = gathered[index][at]

        def body(index, _):
            here = token_block(index, block)
            row = rows[pl.ds(lax.div(index, count // 2), 1), :]
            hidden = tokens[here, :].astype(F32) + row
            total = hidden + (dot(attended[:, here], out_w[...], TN) + row_of(out_b))
            resid[here, :] = total
            scaled, _ = normalize(total)
            normed[here, :] = (scaled * row_of(gain) + row_of(shift)).astype(BF16)
            return 0

        lax.fori_loop(0, count, body, 0)
        down_sum[...] = jnp.zeros_like(down_sum)
        g_normed[...] = jnp.zeros_like(g_normed)

    @pl.when(step < last)
    def _():
        def body(index, total):
            here = token_block(index, block)
            act = dot(normed[here, :], up_w[...]) + bias[pl.ds(step, 1), :]
            g_gelu = dot(cotangent[here, :], down_w[...], NT)
            below = 0.5 * (1.0 + lax.erf(act * 0.7071067811865476))
            density = 0.3989422804014327 * jnp.exp(-0.5 * act * act)
            low = (act * below).astype(BF16)
            grad = (g_gelu * (below + act * density)).astype(BF16)
            gelu_act[here, :] = low
            g_up[here, :] = grad
            down_sum[here, :] += dot(low, down_w[...])
            g_normed[here, :] += dot(grad, up_w[...], NT)
            return total + column_sum(grad)

        g_up_b[...] = lax.fori_loop(0, count, body, jnp.zeros(g_up_b.shape, F32))
        put(0, dot(g_up[...], normed[...], TN))
        put(1, dot(cotangent[...], gelu_act[...], TN))

    @pl.when(step == last)
    def _():
        def body(index, sums):
            here = token_block(index, block)
            total = resid[here, :]
            result[here, :] = (total + (down_sum[here, :] + row_of(down_b))).astype(BF16)
            scaled, inverse = normalize(total)
            grad = g_normed[here, :]
            inner = grad * row_of(gain)
            g_out = cotangent[here, :].astype(F32)
            g_total = g_out + inverse * (
                inner
                - jnp.mean(inner, -1, keepdims=True)
                - scaled * jnp.mean(inner * scaled, -1, keepdims=True)
            )
            g_resid[here, :] = g_total
            low = g_total.astype(BF16)
            g_branch[here, :] = low
            g_attended[:, here] = dot(out_w[...], low, NT).astype(BF16)
            parts = (grad * scaled, grad, low, g_out)
            return tuple(old + column_sum(new) for old, new in zip(sums, parts))

        empty = jnp.zeros((1, width), F32)
        sums = lax.fori_loop(0, count, body, (empty,) * 4)
        for index, at, here in head_rows(out_groups):
            sent_grads[index][at] = g_attended[here, :]
        for index, total in enumerate(sums):
            vectors[index : index + 1, :] = total
        put(0, dot(g_branch[...], attended[...], (((0,), (1,)), ((), ()))))
        put(1, jnp.zeros((width, width), F32))


def mlp(place, groups, gathered, tokens, rows, cotangent, out_w, out_b, gain, shift, up_w, up_b, down_w, down_b):
    tok_here, width = tokens.shape
    hidden_units = up_w.shape[1]
    sources = len(gathered[0])
    pieces = [part for group in gathered for part in group]
    depth = pieces[0].shape[1]
    shapes = [(len(group), depth, tok_here) for group in groups[1] for _ in range(sources)]
    steps = hidden_units // width
    slots = pl.BlockSpec((2, width, width // 2), lambda j, b: (j, 0, 0))
    at = lambda j: jnp.minimum(j, steps - 1)
    slot_shape = jax.ShapeDtypeStruct((2 * steps + 2, width, width // 2), BF16)
    out = pl.pallas_call(
        partial(mlp_kernel, groups=groups, sources=sources, block=tok_here // 2),
        grid_spec=pltpu.PrefetchScalarGridSpec(
            num_scalar_prefetch=1,
            grid=(steps + 1,),
            in_specs=[whole(*part.shape) for part in pieces]
            + [
                whole(tok_here, width),
                whole(2, width),
                whole(tok_here, width),
                whole(width, width),
                whole(width),
                whole(width),
                whole(width),
                pl.BlockSpec((width, width), lambda j, b: (0, at(j))),
                whole(hidden_units),
                pl.BlockSpec((width, width), lambda j, b: (at(j), 0)),
                whole(width),
            ],
            out_specs=[whole(tok_here, width)] * 2
            + [whole(*shape) for shape in shapes]
            + [slots, slots, whole(4, width), pl.BlockSpec((1, width), lambda j, b: (0, at(j)))],
            scratch_shapes=[
                pltpu.VMEM((width, tok_here), BF16),
                pltpu.VMEM((tok_here, width), BF16),
                pltpu.VMEM((tok_here, width), F32),
                pltpu.VMEM((tok_here, width), BF16),
                pltpu.VMEM((tok_here, width), BF16),
                pltpu.VMEM((tok_here, width), F32),
                pltpu.VMEM((tok_here, width), F32),
                pltpu.VMEM((tok_here, width), BF16),
                pltpu.VMEM((width, tok_here), BF16),
                pltpu.VMEM((steps, width), F32),
            ],
        ),
        out_shape=[
            jax.ShapeDtypeStruct((tok_here, width), BF16),
            jax.ShapeDtypeStruct((tok_here, width), F32),
        ]
        + [jax.ShapeDtypeStruct(shape, BF16) for shape in shapes]
        + [
            slot_shape,
            slot_shape,
            jax.ShapeDtypeStruct((4, width), F32),
            jax.ShapeDtypeStruct((1, hidden_units), F32),
        ],
        compiler_params=pltpu.CompilerParams(vmem_limit_bytes=VMEM),
        cost_estimate=pl.CostEstimate(
            flops=12 * tok_here * up_w.size, transcendentals=0, bytes_accessed=8 * up_w.size
        ),
        name="mlp",
    )(place, *pieces, tokens, rows, cotangent, out_w, out_b, gain, shift, up_w, up_b, down_w, down_b)
    grads = out[2 : 2 + len(shapes)]
    grads = [grads[g * sources : (g + 1) * sources] for g in range(len(groups[1]))]
    return out[0], out[1], grads, out[-4:]


def unproject(scalars, back, weight, packed, bias, chosen, rounds, sources):
    step, pairs = pl.program_id(0), sources // 2
    pair, high_bit, low_bit = lax.rem(step, pairs), lax.div(scalars[0], 2), lax.rem(scalars[0], 2)
    size = len(chosen) * HEAD_DIM

    @pl.when(step == 0)
    def _():
        bias[...] = jnp.zeros_like(bias)

    for high in range(pairs):

        @pl.when(pair == high)
        def _():
            for j in range(2 * high, 2 * high + 2):
                for index in range(len(chosen)):
                    at = ((j % 2 ^ low_bit) * len(chosen) + index) * HEAD_DIM
                    here = pl.ds(pl.multiple_of(at, HEAD_DIM), HEAD_DIM)
                    packed[here, :] = back[index * sources + j][0]

    columns = [(low * rounds + chosen[0]) * HEAD_DIM for low in range(2)]
    ones = jnp.ones((8, packed.shape[1]), BF16)
    found = dot(ones, packed[...], NT)[0:1]
    for part in range(3):
        for at in range(pairs):

            @pl.when((lax.div(step, pairs) == part) & ((pair ^ high_bit) == at))
            def _():
                for low, column in enumerate(columns):
                    start = 2 * at * rounds * HEAD_DIM + column
                    bias[part : part + 1, start : start + size] = found[:, low * size : (low + 1) * size]

    picked = jnp.concatenate([weight[:, column : column + size] for column in columns], 1)
    return dot(packed[...], picked, (((0,), (1,)), ((), ())))


def begin_kernel(scalars, *refs, chosen, rounds, sources):
    back, (weight, g_normed, bias, packed) = refs[:-4], refs[-4:]
    added = unproject(scalars, back, weight, packed, bias, chosen, rounds, sources)

    @pl.when(pl.program_id(0) == 0)
    def _():
        g_normed[...] = added

    @pl.when(pl.program_id(0) > 0)
    def _():
        g_normed[...] += added


def finish_kernel(scalars, *refs, chosen, rounds, sources, block):
    pieces = len(chosen) * sources
    back, refs = refs[:pieces], refs[pieces:]
    weight, tokens, rows, gain, g_resid, vectors, g_up_b, g_before, bias_before = refs[:9]
    g_tokens, sums, g_normed, packed, bias = refs[9:]
    step, last = pl.program_id(0), pl.num_programs(0) - 1
    added = unproject(scalars, back, weight, packed, bias, chosen, rounds, sources)

    @pl.when(step == 0)
    def _():
        g_normed[...] = g_before[...] + added

    @pl.when(step > 0)
    def _():
        g_normed[...] += added

    @pl.when(step == last)
    def _():
        width = tokens.shape[1]
        count = tokens.shape[0] // block
        empty = jnp.zeros((1, width), F32)

        def half(first):
            def body(index, totals):
                here = token_block(index + first * (count // 2), block)
                scaled, inverse = normalize(tokens[here, :].astype(F32) + rows[first : first + 1, :])
                grad = g_normed[here, :]
                inner = grad * row_of(gain)
                g_hidden = g_resid[here, :] + inverse * (
                    inner
                    - jnp.mean(inner, -1, keepdims=True)
                    - scaled * jnp.mean(inner * scaled, -1, keepdims=True)
                )
                g_tokens[here, :] = g_hidden.astype(BF16)
                parts = (grad * scaled, grad, g_hidden)
                return tuple(old + column_sum(new) for old, new in zip(totals, parts))

            return lax.fori_loop(0, count // 2, body, (empty,) * 3)

        one, two = half(0), half(1)
        sums[0:1, :], sums[1:2, :] = one[0] + two[0], one[1] + two[1]
        sums[2:6, :] = vectors[...]
        for index in range(4):
            sums[6 + index : 7 + index, :] = g_up_b[:, index * width : (index + 1) * width]
        lane = lax.broadcasted_iota(jnp.int32, (1, width), 1)
        is_short = scalars[1] != 0
        sums[10:13, :] = bias_before[...] + bias[...]
        pick = lambda at, other: jnp.where(lane == at, scalars[2 + at].astype(F32), other)
        sums[13:14, :] = jnp.where(scalars[0] == 0, pick(0, pick(1, 0.0)), 0.0)
        sums[14:15, :] = jnp.where(is_short, one[2], one[2] + two[2])
        sums[15:16, :] = jnp.where(is_short, two[2], 0.0)


def back_specs(back, width, sources, rounds):
    pairs = sources // 2
    block = pl.BlockSpec((1,) + back[0].shape[1:], lambda i, p: (lax.div(i, pairs), 0, 0))
    pair = 2 * rounds * HEAD_DIM
    return [block] * len(back) + [
        pl.BlockSpec((width, pair), lambda i, p: (0, pair_block(i, p, pairs)))
    ]


def begin_finish(scalars, back, chosen, weight, rounds):
    sources = len(back[0])
    pieces = [part for group in back for part in group]
    width, tok_here = weight.shape[0], pieces[0].shape[2]
    return pl.pallas_call(
        partial(begin_kernel, chosen=chosen, rounds=rounds, sources=sources),
        grid_spec=pltpu.PrefetchScalarGridSpec(
            num_scalar_prefetch=1,
            grid=(3 * sources // 2,),
            in_specs=back_specs(pieces, width, sources, rounds),
            out_specs=[whole(tok_here, width), whole(3, width)],
            scratch_shapes=[pltpu.VMEM((2 * len(chosen) * HEAD_DIM, tok_here), BF16)],
        ),
        out_shape=[
            jax.ShapeDtypeStruct((tok_here, width), F32),
            jax.ShapeDtypeStruct((3, width), F32),
        ],
        compiler_params=pltpu.CompilerParams(vmem_limit_bytes=SMALL_VMEM),
        cost_estimate=pl.CostEstimate(
            flops=2 * tok_here * weight.size, transcendentals=0, bytes_accessed=4 * weight.size
        ),
        name="begin_finish",
    )(scalars, *pieces, weight)


def finish(scalars, back, chosen, weight, tokens, rows, gain, g_resid, vectors, g_up_b, before, rounds):
    tok_here, width = tokens.shape
    sources = len(back[0])
    pieces = [part for group in back for part in group]
    return pl.pallas_call(
        partial(finish_kernel, chosen=chosen, rounds=rounds, sources=sources, block=tok_here // 4),
        grid_spec=pltpu.PrefetchScalarGridSpec(
            num_scalar_prefetch=1,
            grid=(3 * sources // 2,),
            in_specs=back_specs(pieces, width, sources, rounds)
            + [
                whole(tok_here, width),
                whole(2, width),
                whole(width),
                whole(tok_here, width),
                whole(*vectors.shape),
                whole(*g_up_b.shape),
                whole(tok_here, width),
                whole(3, width),
            ],
            out_specs=[whole(tok_here, width), whole(16, width)],
            scratch_shapes=[
                pltpu.VMEM((tok_here, width), F32),
                pltpu.VMEM((2 * len(chosen) * HEAD_DIM, tok_here), BF16),
                pltpu.VMEM((3, width), F32),
            ],
        ),
        out_shape=[
            jax.ShapeDtypeStruct((tok_here, width), BF16),
            jax.ShapeDtypeStruct((16, width), F32),
        ],
        compiler_params=pltpu.CompilerParams(vmem_limit_bytes=SMALL_VMEM),
        cost_estimate=pl.CostEstimate(
            flops=2 * tok_here * weight.size, transcendentals=0, bytes_accessed=8 * weight.size
        ),
        name="finish",
    )(scalars, *pieces, weight, tokens, rows, gain, g_resid, vectors, g_up_b, *before)


def qkv_grad_kernel(block_ref, *refs, rounds, sources, order):
    grads, refs = refs[: rounds * sources], refs[rounds * sources :]
    normed, (first, second, store) = refs[:sources], refs[sources:]
    size = 3 * HEAD_DIM
    for r in range(rounds):
        total = None
        for grad, part in zip(grads[r * sources : (r + 1) * sources], normed):
            here = jnp.concatenate([grad[p] for p in range(3)], 0)
            term = dot(here, part[...])
            total = term if total is None else total + term
        store[:, r * size : (r + 1) * size] = total.T.astype(BF16)
    half = len(order) // 2
    rows = first.shape[1]
    for at, index in enumerate(order):
        start = (block_ref[0] ^ index) * rows
        here = pl.ds(pl.multiple_of(start, rows), rows) if half > 1 else slice(at * rows, (at + 1) * rows)
        (second if at >= half else first)[at % half] = store[here, :]


def qkv_grad(block, grads, normed, order):
    rounds, sources = len(grads), len(normed)
    tok_here, width = normed[0].shape
    size = 3 * HEAD_DIM * rounds
    pieces = [part for group in grads for part in group]
    half = (len(order) // 2, width // len(order), size)
    return pl.pallas_call(
        partial(qkv_grad_kernel, rounds=rounds, sources=sources, order=order),
        grid_spec=pltpu.PrefetchScalarGridSpec(
            num_scalar_prefetch=1,
            grid=(1,),
            in_specs=[whole(*pieces[0].shape)] * len(pieces) + [whole(tok_here, width)] * sources,
            out_specs=[whole(*half)] * 2,
            scratch_shapes=[pltpu.VMEM((width, size), BF16)],
        ),
        out_shape=[jax.ShapeDtypeStruct(half, BF16)] * 2,
        compiler_params=pltpu.CompilerParams(vmem_limit_bytes=SMALL_VMEM),
        cost_estimate=pl.CostEstimate(
            flops=8 * tok_here * width * size, transcendentals=0, bytes_accessed=12 * tok_here * width
        ),
        name="qkv_grad",
    )(block, *pieces, *normed)


def swap(values, axis, bit):
    size = lax.axis_size(axis)
    return lax.ppermute(values, axis, [(j, j ^ bit) for j in range(size)])


def trade(parts, axis):
    return [parts[0]] + [swap(part, axis, i) for i, part in enumerate(parts) if i]


def spread(values, axis, count):
    return [values] + [swap(values, axis, i) for i in range(1, count)]


def total_of(parts):
    total = parts[0].astype(F32)
    for part in parts[1:]:
        total = total + part.astype(F32)
    return total


def after(values, *others):
    return lax.optimization_barrier((values, *others))[0]


def deal_kernel(bits_ref, *refs, steps):
    keep, got, (outgoing, staying) = refs[: steps + 2], refs[steps + 2 : 2 * steps + 4], refs[-2:]
    gate = bits_ref[0]
    for out, side in ((outgoing, 1 - gate), (staying, gate)):
        at = 0
        for left, right in zip(keep, got):
            rows = left.shape[2] // 2
            here = pl.ds(pl.multiple_of(side * rows, rows), rows)
            total = left[0, 0, here, :].astype(F32) + right[0, 0, here, :].astype(F32)
            out[0, at : at + rows, :] = total.astype(BF16)
            at += rows


def deal(gate, keep, got, dp):
    slots, width, lanes = keep.shape
    steps = slots // 2 - 1
    up_each, each = width * steps // dp, width // dp
    per_slot = width // up_each
    up = pl.BlockSpec(
        (1, 1, up_each, lanes),
        lambda i, b: (2 * (i // per_slot), i % per_slot, 0, 0),
    )
    rest = [
        pl.BlockSpec((1, 1, each, lanes), lambda i, b, slot=slot: (slot, i, 0, 0))
        for slot in [2 * k + 1 for k in range(steps)] + [2 * steps]
    ]
    views = lambda array: [array.reshape(slots, per_slot, up_each, lanes)] + [
        array.reshape(slots, dp, each, lanes)
    ] * (steps + 1)
    rows = up_each // 2 + (steps + 1) * each // 2
    shape = jax.ShapeDtypeStruct((dp, rows, lanes), BF16)
    return pl.pallas_call(
        partial(deal_kernel, steps=steps),
        grid_spec=pltpu.PrefetchScalarGridSpec(
            num_scalar_prefetch=1,
            grid=(dp,),
            in_specs=([up] + rest) * 2,
            out_specs=[pl.BlockSpec((1, rows, lanes), lambda i, b: (i, 0, 0))] * 2,
        ),
        out_shape=[shape, shape],
        cost_estimate=pl.CostEstimate(flops=keep.size, transcendentals=0, bytes_accessed=6 * keep.size),
        name="deal",
    )(gate, *views(keep), *views(got))


def undeal_kernel(place_ref, *refs, sources, steps, each):
    shares, (up, down, out, store) = refs[:sources], refs[sources:]
    lanes = store.shape[2]
    for j, share in enumerate(shares):
        store[place_ref[0] ^ j] = share[...].astype(F32)
    wide = steps * each
    for low in range(2):
        both = lambda at, size: jnp.concatenate([store[low, at : at + size], store[2 + low, at : at + size]], 0).T
        up[low * lanes : (low + 1) * lanes, :] = both(0, wide)
        for half in range(2):
            here = slice(half * each, (half + 1) * each)
            share = store.at[2 * half + low]
            for k in range(steps):
                at, row = (2 * k + low) * lanes, wide + k * each
                down[here, at : at + lanes] = share[row : row + each]
            out[here, low * lanes : (low + 1) * lanes] = share[2 * wide : 2 * wide + each]


def undeal(place, shares, steps, width, dp):
    rows, lanes = shares[0].shape
    shapes = [(width, width * steps // dp), (width // dp, width * steps), (width // dp, width)]
    up, down, out = pl.pallas_call(
        partial(undeal_kernel, sources=len(shares), steps=steps, each=width // dp // 2),
        grid_spec=pltpu.PrefetchScalarGridSpec(
            num_scalar_prefetch=1,
            grid=(1,),
            in_specs=[whole(rows, lanes)] * len(shares),
            out_specs=[whole(*shape) for shape in shapes],
            scratch_shapes=[pltpu.VMEM((len(shares), rows, lanes), F32)],
        ),
        out_shape=[jax.ShapeDtypeStruct(shape, F32) for shape in shapes],
        cost_estimate=pl.CostEstimate(flops=0, transcendentals=0, bytes_accessed=24 * rows * lanes),
        name="undeal",
    )(place, *shares)
    return up, down.T, out.T


def turn_kernel(*refs):
    *parts, out = refs
    out[...] = total_of([part[0] for part in parts]).T.astype(BF16)


def turn(parts):
    _, rows, columns = parts[0].shape
    return pl.pallas_call(
        turn_kernel, out_shape=jax.ShapeDtypeStruct((columns, rows), BF16), name="turn"
    )(*parts)


def regroup_kernel(place_ref, *refs, rounds):
    *shares, out = refs
    sources = len(shares)
    for j, share in enumerate(shares):
        for r in range(rounds):
            for p in range(3):
                at = ((p * sources + (place_ref[0] ^ j)) * rounds + r) * HEAD_DIM
                start = (r * 3 + p) * HEAD_DIM
                out[pl.ds(pl.multiple_of(at, HEAD_DIM), HEAD_DIM), :] = share[start : start + HEAD_DIM]


def regroup(place, shares, rounds):
    columns, rows = shares[0].shape
    total = columns * len(shares)
    return pl.pallas_call(
        partial(regroup_kernel, rounds=rounds),
        grid_spec=pltpu.PrefetchScalarGridSpec(
            num_scalar_prefetch=1,
            grid=(1,),
            in_specs=[whole(columns, rows)] * len(shares),
            out_specs=whole(total, rows),
        ),
        out_shape=jax.ShapeDtypeStruct((total, rows), BF16),
        name="regroup",
    )(place, *shares)


def stack_kernel(parts, out):
    both = [parts[index].astype(F32) for index in range(parts.shape[0])]
    out[...] = jnp.concatenate(both, 1)


def stack_rows(parts):
    count, columns, rows = parts.shape
    return pl.pallas_call(
        stack_kernel, out_shape=jax.ShapeDtypeStruct((columns, rows * count), F32), name="stack_rows"
    )(parts).T


def exchange(values, axis):
    return lax.all_to_all(values, axis, split_axis=0, concat_axis=0, tiled=True)


def wide_sums(slots, place, dp):
    steps, width, lanes = slots.shape[0] // 2 - 1, slots.shape[1], slots.shape[2]
    pairs = slots.reshape(steps + 1, 2, width, lanes)
    up = pairs[:steps, 0].reshape(dp, 2, -1, lanes)
    down = pairs[:steps, 1].reshape(steps, dp, 2, -1, lanes)
    down = jnp.moveaxis(down, 0, 2).reshape(dp, 2, -1, lanes)
    out = pairs[steps, 0].reshape(dp, 2, -1, lanes)
    dealt = jnp.concatenate([up, down, out], 2)
    gate = place // 2
    pick = lambda index: lax.dynamic_index_in_dim(dealt, index, 1, keepdims=False)
    half_sum = total_of([pick(gate), swap(pick(1 - gate), "seq", 2)]).astype(BF16)
    share = jnp.sum(exchange(half_sum, "dp").astype(F32), 0).astype(BF16)
    shares = lax.all_gather(share, "seq", axis=0).reshape(2, 2, -1, lanes).astype(F32)
    each = width // dp // 2
    up, down, out = jnp.split(shares, [steps * each, 2 * steps * each], 2)
    turned = lambda part: jnp.transpose(part, (1, 3, 0, 2)).reshape(2 * lanes, -1)
    down = down.reshape(2, 2, steps, each, lanes)
    down = jnp.transpose(down, (2, 1, 4, 0, 3)).reshape(steps * 2 * lanes, 2 * each)
    return turned(up), down, turned(out)


def wide_columns(grads, dp, sources, rounds):
    grad = jnp.concatenate(grads, 2).reshape(-1, 3 * HEAD_DIM * rounds)
    width, columns = grad.shape
    rows = width // dp
    summed = jnp.sum(exchange(grad.reshape(dp, rows, columns), "dp").astype(F32), 0).astype(BF16)
    gathered = lax.all_gather(summed, "seq", axis=0).reshape(sources, rows, rounds, 3, HEAD_DIM)
    ordered = jnp.transpose(gathered, (1, 3, 0, 2, 4)).reshape(rows, dp, -1)
    return exchange(jnp.swapaxes(ordered, 0, 1), "dp").reshape(width, -1).astype(F32)


def on_device(
    tokens,
    time_steps,
    data_group,
    cotangent,
    attn_norm_gain,
    attn_norm_bias,
    qkv_weight,
    query_bias,
    value_bias,
    out_weight,
    out_bias,
    mlp_norm_gain,
    mlp_norm_bias,
    up_weight,
    up_bias,
    down_weight,
    down_bias,
    time_table,
):
    sources, dp = lax.axis_size("seq"), lax.axis_size("dp")
    place, block = lax.axis_index("seq"), lax.axis_index("dp")
    tokens, cotangent = tokens[0], cotangent[0]
    tok_here, width = tokens.shape
    hidden_units = up_weight.shape[1]
    rounds = HEADS // sources
    is_short = data_group[0] == 0
    short_flag = is_short.astype(jnp.int32)[None]
    place_arg = place.astype(jnp.int32)[None]
    block_arg = block.astype(jnp.int32)[None]
    few = dp <= 8
    row_steps = jnp.where(is_short, time_steps[0], time_steps[0, 0])
    scalars = jnp.concatenate([place_arg, short_flag, lax.div(row_steps, 8), lax.rem(row_steps, 8)])

    normed, rows, sending = project(
        scalars,
        tokens,
        time_table,
        attn_norm_gain,
        attn_norm_bias,
        qkv_weight,
        query_bias,
        value_bias,
        sources,
        rounds,
    )
    heads, saved, sent = [trade(sending[0], "seq")], [], []
    returned = []
    for r in range(rounds):
        if r + 1 < rounds:
            ahead = sending[r + 1] if r < 1 else after(sending[r + 1], saved[r - 1][1])
            heads.append(trade(ahead, "seq"))
        ready = after(heads[r], saved[r - 1][1]) if r else heads[r]
        out, kept = attend(short_flag, ready, sent[0] if r == 1 else ())
        saved.append(kept)
        sent.append(out)
        if r >= 1:
            returned.append(trade(after(out, *returned[-1]) if returned else out, "seq"))

    beside = swap(after(normed, saved[1][1]), "seq", 1)
    across = swap(after(normed, *returned[-1]), "seq", 2)
    groups = (((0, 1), (2,)), ((0,), (1, 2)))
    result, g_resid, sent_grads, (send, keep, vectors, g_up_b) = mlp(
        place_arg,
        groups,
        returned,
        after(tokens, beside),
        rows,
        cotangent,
        out_weight,
        out_bias,
        mlp_norm_gain,
        mlp_norm_bias,
        up_weight,
        up_bias,
        down_weight,
        down_bias,
    )
    send, *sent_grads = after((send, *sent_grads), across)
    got = swap(send, "seq", 1)
    first_grads = trade(sent_grads[0], "seq")
    if few:
        outgoing, staying = deal(place_arg // 2, keep, got, dp)
        got = swap(outgoing, "seq", 2)
        ready = outgoing
    else:
        ready = summed = total_of([keep, got]).astype(BF16)
    rest_grads = trade(after(sent_grads[1], *first_grads), "seq")
    beside = [normed, beside, across, swap(across, "seq", 1)]
    grads = [attend_back(short_flag, after(heads[0], ready, beside[3]), saved[0], first_grads, 0)]
    back = [trade(grads[0], "seq")]
    held = after(heads[1], *grads[0])
    grads.append(attend_back(short_flag, held, saved[1], rest_grads, 0))
    back.append(trade(grads[1], "seq"))
    order = (0, 4, 2, 6, 1, 5, 3, 7) if few else (0, 1)
    stay_a, away_a = qkv_grad(block_arg, grads, beside, order)
    if few:
        got_a = swap(away_a, "dp", 1)
        half_sum = total_of([staying, after(got, grads[1])]).astype(BF16)
        dealt = exchange(half_sum, "dp")
        ready = half_sum
    held = after(heads[2], stay_a, ready, *back[0])
    grads.append(attend_back(short_flag, held, saved[2], rest_grads, 1))
    back.append(trade(grads[2], "seq"))
    grads[2] = after(grads[2], *back[1])
    stay_b, away_b = qkv_grad(block_arg, grads[2:], beside, order)
    earlier = [after(parts, stay_b) for parts in back[:2]]
    before = begin_finish(scalars, earlier, (0, 1), qkv_weight, rounds)
    ready = before[1]
    if few:
        kept, got = [stay_a, stay_b], [after(got_a, grads[2]), swap(away_b, "dp", 1)]
        part = jnp.concatenate([total_of(pair).astype(BF16) for pair in zip(kept, got)], 2)
        share = total_of([after(dealt, before[1])[i] for i in range(dp)]).astype(BF16)
        ready = part, share
        sums = [part[:1]] + [swap(part[at : at + 1], "dp", bit) for at, bit in ((1, 4), (2, 2), (3, 6))]
        share_across = swap(share, "seq", 2)

    steps_arg = time_steps[0].astype(jnp.int32)
    flags = jnp.concatenate([place_arg, short_flag, steps_arg])
    g_tokens, small = finish(
        flags,
        after(back[2:], ready),
        (2,),
        qkv_weight,
        tokens,
        rows,
        attn_norm_gain,
        g_resid,
        vectors,
        g_up_b,
        before,
        rounds,
    )
    if few:
        shares = [share, swap(share, "seq", 1), share_across, swap(share_across, "seq", 1)]
        summed = turn(after(sums, small))
        columns = regroup(place_arg, spread(summed, "seq", sources), rounds)
    small = total_of(spread(small, "seq", sources))
    if few:
        own, other = small, swap(small, "dp", 1)
        small = jnp.concatenate([own[:13] + other[:13], own[13:], other[13:]])
        all_small = jnp.stack([small] + [swap(small, "dp", bit) for bit in (2, 4, 6)])
        small = jnp.sum(all_small[:, :13], 0)
        by_block = all_small[:, 13:].reshape(dp, 3, width)
    else:
        slots = jnp.where((jnp.arange(dp) == block)[:, None, None], small[None, 13:], 0.0)
        small = jnp.concatenate([small[:13], slots.reshape(-1, width)])
        bit = 1
        while bit < dp:
            small = small + swap(small, "dp", bit)
            bit *= 2
        by_block = small[13:].reshape(dp, 3, width)
    steps = by_block[:, 0, :2].reshape(1, -1).astype(jnp.int32)
    all_rows = by_block[:, 1:].reshape(-1, width)
    if few:
        sum_up, sum_down, sum_out = undeal(place_arg, shares, hidden_units // width, width, dp)
        sum_qkv = stack_rows(exchange(columns.reshape(dp, 3 * width // dp, width // dp), "dp"))
    else:
        sum_up, sum_down, sum_out = wide_sums(summed, place, dp)
        sum_qkv = wide_columns(
            [jnp.stack(pair).reshape(2, width // 2, -1) for pair in ((stay_a, away_a), (stay_b, away_b))],
            dp,
            sources,
            rounds,
        )
    share_cols = width // dp
    rows_mine = lax.dynamic_slice_in_dim(all_rows, block * share_cols, share_cols, 1)
    table_rows = time_table.shape[0]
    hits = jnp.arange(table_rows, dtype=jnp.int32)[:, None] == steps
    sum_table = jnp.dot(hits.astype(F32), rows_mine, precision=lax.Precision.HIGHEST)
    return (
        result[None],
        g_tokens[None],
        small[0],
        small[1],
        sum_qkv,
        small[10],
        small[12],
        sum_out,
        small[4],
        small[2],
        small[3],
        sum_up,
        small[6:10].reshape(-1),
        sum_down,
        small[5],
        sum_table,
    )


def solution(mesh):
    placed = (P("dp", "seq", None), P("dp", None), P("dp"), P("dp", "seq", None)) + (P(),) * 14
    column = P(None, "dp")
    return jax.shard_map(
        on_device,
        mesh=mesh,
        in_specs=placed,
        out_specs=(
            P("dp", "seq", None),
            P("dp", "seq", None),
            P(),
            P(),
            column,
            P(),
            P(),
            column,
            P(),
            P(),
            P(),
            column,
            P(),
            column,
            P(),
            column,
        ),
        check_vma=False,
    )
```

```python
from functools import partial

import jax
import jax.numpy as jnp
from jax import lax
from jax.experimental import pallas as pl
from jax.experimental.pallas import tpu as pltpu
from jax.sharding import PartitionSpec as P

HEADS = 12
HEAD_DIM = 64
EPSILON = 1e-05
LOG2E = 1.4426950408889634
SCALE = HEAD_DIM**-0.5
BF16 = jnp.bfloat16
F32 = jnp.float32
NN = (((1,), (0,)), ((), ()))
NT = (((1,), (1,)), ((), ()))
TN = (((0,), (0,)), ((), ()))
VMEM = 62 << 20
SMALL_VMEM = 40 << 20


def dot(left, right, dims=NN):
    return lax.dot_general(left, right, dims, preferred_element_type=F32)


def split_low(values, count):
    parts = []
    for _ in range(count):
        term = values.astype(BF16)
        parts.append(term)
        values = values - term.astype(F32)
    return parts


def whole(*shape):
    return pl.BlockSpec(shape, lambda *_: (0,) * len(shape))


def halves(sources, segment):
    for chunk in range(2 * sources):
        source, part = divmod(chunk, 2)
        yield chunk, source, slice(part * segment, (part + 1) * segment)


def over_chunks(short_ref, chunks, body):
    is_short = short_ref[0] != 0
    part = lax.rem(pl.program_id(0), 2)

    @pl.when(is_short)
    def _():
        body([2 * k + part for k in range(chunks // 2)], True)

    @pl.when(jnp.logical_not(is_short))
    def _():
        body(list(range(chunks)), True)


def attend_kernel(short_ref, *refs, sources, segment, held):
    heads, refs = refs[:sources], refs[sources:]
    earlier, refs = refs[: sources * held], refs[sources * held :]
    sent, refs = refs[:sources], refs[sources:]
    mixed_ref, inverse_ref, weights_ref, queries, keys, values, sums, bounded = refs
    step = pl.program_id(0)
    chunks = 2 * sources
    depth = HEAD_DIM

    @pl.when(step == 0)
    def _():
        for old, new in zip(earlier, sent):
            new[0] = old[0]
        longest = [jnp.zeros((1, segment), F32)] * 2
        for chunk, source, cols in halves(sources, segment):
            scaled = heads[source][0, :, cols].astype(F32) * (SCALE * LOG2E)
            high, low = split_low(scaled, 2)
            queries[chunk, 0:64, :] = high
            queries[chunk, 64:128, :] = low
            queries[chunk, 128:144, :] = jnp.zeros((16, segment), BF16)
            key = heads[source][1, :, cols]
            keys[chunk, 0:64, :] = key
            keys[chunk, 64:128, :] = key
            keys[chunk, 128:144, :] = jnp.full((16, segment), -1.0, BF16)
            values[chunk, 0:64, :] = heads[source][2, :, cols]
            values[chunk, 64:80, :] = jnp.ones((16, segment), BF16)
            sizes = [jnp.sum(x * x, 0, keepdims=True) for x in (scaled, key.astype(F32))]
            longest = [jnp.maximum(old, new) for old, new in zip(longest, sizes)]
        bound = jnp.max(longest[0]) * jnp.max(longest[1])
        bounded[0] = (bound <= 3600.0).astype(jnp.int32)

    @pl.when(bounded[0] == 0)
    def _():
        query = queries[step][0:128]
        is_short = (short_ref[0] != 0).astype(jnp.int32)

        def body(index, peak):
            chunk = jnp.where(is_short != 0, 2 * index + lax.rem(step, 2), index)
            scores = dot(keys[chunk][0:128], query, TN)
            return jnp.maximum(peak, jnp.max(scores, 0, keepdims=True))

        start = jnp.full((1, segment), -jnp.inf, F32)
        peak = lax.fori_loop(0, jnp.where(is_short != 0, chunks // 2, chunks), body, start)
        zeros = jnp.zeros((13, segment), BF16)
        queries[step, 128:144, :] = jnp.concatenate(split_low(peak, 3) + [zeros], 0)

    def body(order, first):
        query = queries[step]
        total = None
        later = dot(keys[order[0]], query, TN)
        for index, chunk in enumerate(order):
            scores = later
            if index + 1 < len(order):
                later = dot(keys[order[index + 1]], query, TN)
            weights = jnp.exp2(scores).astype(BF16)
            weights_ref[0, chunk] = weights.T
            mixed = dot(values[chunk], weights)
            total = mixed if total is None else total + mixed
        sums[...] = total if first else sums[...] + total

    over_chunks(short_ref, chunks, body)
    total = sums[...]
    inverse = 1.0 / total[depth : depth + 1, :]
    result = total[:depth] * inverse
    mixed_ref[step] = result
    inverse_ref[step] = inverse
    for chunk, source, cols in halves(sources, segment):

        @pl.when(step == chunk)
        def _():
            sent[source][held, :, cols] = result.astype(BF16)


def attend(is_short, heads, earlier=()):
    sources = len(heads)
    _, depth, tokens = heads[0].shape
    segment, chunks = tokens // 2, 2 * sources
    work = (sources * tokens) ** 2
    held = len(earlier) // sources
    out = pl.pallas_call(
        partial(attend_kernel, sources=sources, segment=segment, held=held),
        grid_spec=pltpu.PrefetchScalarGridSpec(
            num_scalar_prefetch=1,
            grid=(chunks,),
            in_specs=[whole(3, depth, tokens)] * sources + [whole(1, depth, tokens)] * len(earlier),
            out_specs=[whole(1 + held, depth, tokens)] * sources
            + [
                whole(chunks, depth, segment),
                whole(chunks, 1, segment),
                pl.BlockSpec((1, chunks, segment, segment), lambda i, s: (i, 0, 0, 0)),
            ],
            scratch_shapes=[
                pltpu.VMEM((chunks, 144, segment), BF16),
                pltpu.VMEM((chunks, 144, segment), BF16),
                pltpu.VMEM((chunks, 80, segment), BF16),
                pltpu.VMEM((80, segment), F32),
                pltpu.SMEM((1,), jnp.int32),
            ],
        ),
        out_shape=[jax.ShapeDtypeStruct((1 + held, depth, tokens), BF16)] * sources
        + [
            jax.ShapeDtypeStruct((chunks, depth, segment), F32),
            jax.ShapeDtypeStruct((chunks, 1, segment), F32),
            jax.ShapeDtypeStruct((chunks, chunks, segment, segment), BF16),
        ],
        compiler_params=pltpu.CompilerParams(vmem_limit_bytes=SMALL_VMEM),
        cost_estimate=pl.CostEstimate(
            flops=16 * work * depth, transcendentals=work, bytes_accessed=2 * work
        ),
        name="attend",
    )(is_short, *heads, *earlier)
    return out[:sources], out[-3:]


def attend_back_kernel(short_ref, *refs, sources, segment):
    heads, grads, (mixed_ref, inverse_ref, weights_ref), refs = (
        refs[:sources],
        refs[sources : 2 * sources],
        refs[2 * sources : 2 * sources + 3],
        refs[2 * sources + 3 :],
    )
    outs, (queries, g_aug, v_aug, grad_q, grad_kv) = refs[:sources], refs[sources:]
    step = pl.program_id(0)
    chunks = 2 * sources

    @pl.when(step == 0)
    def _():
        zeros = jnp.zeros((13, segment), BF16)
        for chunk, source, cols in halves(sources, segment):
            queries[chunk] = heads[source][0, :, cols]
            grad = grads[source][0, :, cols].astype(F32) * inverse_ref[chunk]
            high, low = split_low(grad, 2)
            g_aug[chunk, 0:64, :] = high
            g_aug[chunk, 64:128, :] = low
            inner = jnp.sum(grad * mixed_ref[chunk], 0, keepdims=True)
            g_aug[chunk, 128:144, :] = jnp.concatenate(split_low(inner, 3) + [zeros], 0)
        grad_q[...] = jnp.zeros_like(grad_q)

    def column(index):
        for chunk, source, cols in halves(sources, segment):

            @pl.when(step == chunk)
            def _():
                index(source, cols)

    def load(source, cols):
        value = heads[source][2, :, cols]
        v_aug[0:64, :] = value
        v_aug[64:128, :] = value
        v_aug[128:144, :] = jnp.full((16, segment), -1.0, BF16)
        v_aug[144:208, :] = heads[source][1, :, cols]

    column(load)
    value = v_aug[0:144]
    turned = v_aug[144:208].T

    def body(order, first):
        key_total = value_total = None
        later = dot(g_aug[order[0]], value, TN)
        for index, chunk in enumerate(order):
            slopes = later
            if index + 1 < len(order):
                later = dot(g_aug[order[index + 1]], value, TN)
            weights = weights_ref[chunk, 0]
            g_scores = (weights.astype(F32) * slopes).astype(BF16)
            value_part = dot(g_aug[chunk, 0:128, :], weights)
            key_part = dot(queries[chunk], g_scores)
            value_total = value_part if value_total is None else value_total + value_part
            key_total = key_part if key_total is None else key_total + key_part
            grad_q[chunk] += dot(g_scores, turned)
        both = jnp.concatenate([key_total, value_total[0:64] + value_total[64:128]], 0)
        grad_kv[...] = both if first else grad_kv[...] + both

    over_chunks(short_ref, chunks, body)

    def save(source, cols):
        outs[source][1, :, cols] = (grad_kv[0:64] * SCALE).astype(BF16)
        outs[source][2, :, cols] = grad_kv[64:128].astype(BF16)

    column(save)

    @pl.when(step == chunks - 1)
    def _():
        for chunk, source, cols in halves(sources, segment):
            outs[source][0, :, cols] = (grad_q[chunk] * SCALE).T.astype(BF16)


def attend_back(is_short, heads, saved, grads, at):
    sources = len(heads)
    _, depth, tokens = heads[0].shape
    segment, chunks = tokens // 2, 2 * sources
    work = (sources * tokens) ** 2
    return pl.pallas_call(
        partial(attend_back_kernel, sources=sources, segment=segment),
        grid_spec=pltpu.PrefetchScalarGridSpec(
            num_scalar_prefetch=1,
            grid=(chunks,),
            in_specs=[whole(3, depth, tokens)] * sources
            + [pl.BlockSpec((1, depth, tokens), lambda i, s: (at, 0, 0))] * sources
            + [
                whole(chunks, depth, segment),
                whole(chunks, 1, segment),
                pl.BlockSpec((chunks, 1, segment, segment), lambda i, s: (0, i, 0, 0)),
            ],
            out_specs=[whole(3, depth, tokens)] * sources,
            scratch_shapes=[
                pltpu.VMEM((chunks, 64, segment), BF16),
                pltpu.VMEM((chunks, 144, segment), BF16),
                pltpu.VMEM((208, segment), BF16),
                pltpu.VMEM((chunks, segment, depth), F32),
                pltpu.VMEM((2 * depth, segment), F32),
            ],
        ),
        out_shape=[jax.ShapeDtypeStruct((3, depth, tokens), BF16)] * sources,
        compiler_params=pltpu.CompilerParams(vmem_limit_bytes=VMEM),
        cost_estimate=pl.CostEstimate(
            flops=40 * work * depth, transcendentals=work, bytes_accessed=2 * work
        ),
        name="attend_back",
    )(is_short, *heads, *grads, *saved)


def normalize(hidden):
    center = hidden - jnp.mean(hidden, -1, keepdims=True)
    spread = jnp.mean(center * center, -1, keepdims=True)
    inverse = lax.rsqrt(spread + EPSILON)
    return center * inverse, inverse


def token_block(index, size):
    return pl.ds(pl.multiple_of(index * size, size), size)


def column_sum(values):
    return jnp.sum(values.astype(F32), 0, keepdims=True)


def row_of(vector):
    return vector[...].astype(F32)[None, :]


def project_kernel(
    scalars, tokens, first_rows, second_rows, gain, shift, weight, query_bias, value_bias, normed, rows, *refs,
    sources, rounds, block
):
    outs, turned, column = refs[:-2], refs[-2], refs[-1]
    step = pl.program_id(0)
    pairs = sources // 2
    count = tokens.shape[0] // block
    size = column.shape[1]

    @pl.when(step == 0)
    def _():
        for index, group in enumerate((first_rows, second_rows)):
            all_rows = group[...].astype(F32)
            chosen = lax.broadcasted_iota(jnp.int32, all_rows.shape, 0) == scalars[4 + index]
            rows[index : index + 1, :] = jnp.sum(jnp.where(chosen, all_rows, 0.0), 0, keepdims=True)
        biases = row_of(query_bias), jnp.zeros((1, pairs * size), F32), row_of(value_bias)
        for part, bias in enumerate(biases):
            for pair in range(pairs):
                here = jnp.broadcast_to(bias[:, pair * size : (pair + 1) * size], (128, size))
                column[part * pairs + pair] = here.T

        def body(index, _):
            here = token_block(index, block)
            row = rows[pl.ds(lax.div(index, count // 2), 1), :]
            scaled, _ = normalize(tokens[here, :].astype(F32) + row)
            low = (scaled * row_of(gain) + row_of(shift)).astype(BF16)
            normed[here, :] = low
            turned[:, here] = low.T
            return 0

        lax.fori_loop(0, count, body, 0)

    pair, high_bit, low_bit = lax.rem(step, pairs), lax.div(scalars[0], 2), lax.rem(scalars[0], 2)
    bias = column[step - pair + (pair ^ high_bit)][:, 0:1]
    result = (dot(weight[...], turned[...], TN) + bias).astype(BF16)
    for high in range(pairs):
        for bit in range(2):

            @pl.when((pair == high) & (low_bit == bit))
            def _():
                for low in range(2):
                    for r in range(rounds):
                        at = (low * rounds + r) * HEAD_DIM
                        outs[r * sources + 2 * high + (low ^ bit)][0] = result[at : at + HEAD_DIM]


def project(scalars, tokens, time_table, gain, shift, weight, query_bias, value_bias, sources, rounds):
    tok_here, width = tokens.shape
    pair = 2 * rounds * HEAD_DIM
    pairs = sources // 2
    group = lambda index: pl.BlockSpec((8, width), lambda i, p: (p[2 + index], 0))
    out = pl.pallas_call(
        partial(project_kernel, sources=sources, rounds=rounds, block=tok_here // 4),
        grid_spec=pltpu.PrefetchScalarGridSpec(
            num_scalar_prefetch=1,
            grid=(3 * pairs,),
            in_specs=[
                whole(tok_here, width),
                group(0),
                group(1),
                whole(width),
                whole(width),
                pl.BlockSpec((width, pair), lambda i, p: (0, pair_block(i, p, pairs))),
                whole(width),
                whole(width),
            ],
            out_specs=[whole(tok_here, width), whole(2, width)]
            + [pl.BlockSpec((1, HEAD_DIM, tok_here), lambda i, p: (lax.div(i, pairs), 0, 0))]
            * (rounds * sources),
            scratch_shapes=[
                pltpu.VMEM((width, tok_here), BF16),
                pltpu.VMEM((3 * pairs, pair, 128), F32),
            ],
        ),
        out_shape=[
            jax.ShapeDtypeStruct((tok_here, width), BF16),
            jax.ShapeDtypeStruct((2, width), F32),
        ]
        + [jax.ShapeDtypeStruct((3, HEAD_DIM, tok_here), BF16)] * (rounds * sources),
        compiler_params=pltpu.CompilerParams(vmem_limit_bytes=VMEM),
        cost_estimate=pl.CostEstimate(
            flops=2 * tok_here * weight.size, transcendentals=0, bytes_accessed=4 * weight.size
        ),
        name="project",
    )(scalars, tokens, time_table, time_table, gain, shift, weight, query_bias, value_bias)
    return out[0], out[1], [out[2 + r * sources : 2 + (r + 1) * sources] for r in range(rounds)]


def pair_block(step, scalars, pairs):
    at = lax.rem(step, pairs)
    return step - at + (at ^ lax.div(scalars[0], 2))


def mlp_kernel(place_ref, *refs, groups, sources, block):
    (in_groups, out_groups), rounds = groups, sum(map(len, groups[0]))
    gathered, refs = refs[: len(in_groups) * sources], refs[len(in_groups) * sources :]
    pieces = len(out_groups) * sources
    tokens, rows, cotangent, out_w, out_b, gain, shift, up_w, up_b, down_w, down_b = refs[:11]
    result, g_resid = refs[11:13]
    sent_grads = refs[13 : 13 + pieces]
    send, keep, vectors, g_up_b = refs[13 + pieces : 17 + pieces]
    attended, normed, resid, gelu_act, g_up, down_sum, g_normed, g_branch, g_attended, bias = refs[17 + pieces :]
    step, last = pl.program_id(0), pl.num_programs(0) - 1
    tok_here, width = tokens.shape
    count = tok_here // block
    place = place_ref[0]
    low_bit = lax.rem(place, 2) == 0

    def head_rows(groups):
        for index in range(len(groups) * sources):
            group, j = divmod(index, sources)
            for at, r in enumerate(groups[group]):
                start = ((place ^ j) * rounds + r) * HEAD_DIM
                yield index, at, pl.ds(pl.multiple_of(start, HEAD_DIM), HEAD_DIM)

    def put(slot, grad):
        grad = grad.astype(BF16)
        middle = grad.shape[1] // 2
        left, right = grad[:, :middle], grad[:, middle:]

        @pl.when(low_bit)
        def _():
            keep[slot], send[slot] = left, right

        @pl.when(jnp.logical_not(low_bit))
        def _():
            keep[slot], send[slot] = right, left

    @pl.when(step == 0)
    def _():
        bias_row = row_of(up_b)
        for index in range(bias.shape[0]):
            bias[index : index + 1, :] = bias_row[:, index * width : (index + 1) * width]
        for index, at, here in head_rows(in_groups):
            attended[here, :] = gathered[index][at]

        def body(index, _):
            here = token_block(index, block)
            row = rows[pl.ds(lax.div(index, count // 2), 1), :]
            hidden = tokens[here, :].astype(F32) + row
            total = hidden + (dot(attended[:, here], out_w[...], TN) + row_of(out_b))
            resid[here, :] = total
            scaled, _ = normalize(total)
            normed[here, :] = (scaled * row_of(gain) + row_of(shift)).astype(BF16)
            return 0

        lax.fori_loop(0, count, body, 0)
        down_sum[...] = jnp.zeros_like(down_sum)
        g_normed[...] = jnp.zeros_like(g_normed)

    @pl.when(step < last)
    def _():
        def body(index, total):
            here = token_block(index, block)
            act = dot(normed[here, :], up_w[...]) + bias[pl.ds(step, 1), :]
            g_gelu = dot(cotangent[here, :], down_w[...], NT)
            below = 0.5 * (1.0 + lax.erf(act * 0.7071067811865476))
            density = 0.3989422804014327 * jnp.exp(-0.5 * act * act)
            low = (act * below).astype(BF16)
            grad = (g_gelu * (below + act * density)).astype(BF16)
            gelu_act[here, :] = low
            g_up[here, :] = grad
            down_sum[here, :] += dot(low, down_w[...])
            g_normed[here, :] += dot(grad, up_w[...], NT)
            return total + column_sum(grad)

        g_up_b[...] = lax.fori_loop(0, count, body, jnp.zeros(g_up_b.shape, F32))
        put(0, dot(g_up[...], normed[...], TN))
        put(1, dot(cotangent[...], gelu_act[...], TN))

    @pl.when(step == last)
    def _():
        def body(index, sums):
            here = token_block(index, block)
            total = resid[here, :]
            result[here, :] = (total + (down_sum[here, :] + row_of(down_b))).astype(BF16)
            scaled, inverse = normalize(total)
            grad = g_normed[here, :]
            inner = grad * row_of(gain)
            g_out = cotangent[here, :].astype(F32)
            g_total = g_out + inverse * (
                inner
                - jnp.mean(inner, -1, keepdims=True)
                - scaled * jnp.mean(inner * scaled, -1, keepdims=True)
            )
            g_resid[here, :] = g_total
            low = g_total.astype(BF16)
            g_branch[here, :] = low
            g_attended[:, here] = dot(out_w[...], low, NT).astype(BF16)
            parts = (grad * scaled, grad, low, g_out)
            return tuple(old + column_sum(new) for old, new in zip(sums, parts))

        empty = jnp.zeros((1, width), F32)
        sums = lax.fori_loop(0, count, body, (empty,) * 4)
        for index, at, here in head_rows(out_groups):
            sent_grads[index][at] = g_attended[here, :]
        for index, total in enumerate(sums):
            vectors[index : index + 1, :] = total
        put(0, dot(g_branch[...], attended[...], (((0,), (1,)), ((), ()))))
        put(1, jnp.zeros((width, width), F32))


def mlp(place, groups, gathered, tokens, rows, cotangent, out_w, out_b, gain, shift, up_w, up_b, down_w, down_b):
    tok_here, width = tokens.shape
    hidden_units = up_w.shape[1]
    sources = len(gathered[0])
    pieces = [part for group in gathered for part in group]
    depth = pieces[0].shape[1]
    shapes = [(len(group), depth, tok_here) for group in groups[1] for _ in range(sources)]
    steps = hidden_units // width
    slots = pl.BlockSpec((2, width, width // 2), lambda j, b: (j, 0, 0))
    at = lambda j: jnp.minimum(j, steps - 1)
    slot_shape = jax.ShapeDtypeStruct((2 * steps + 2, width, width // 2), BF16)
    out = pl.pallas_call(
        partial(mlp_kernel, groups=groups, sources=sources, block=tok_here // 2),
        grid_spec=pltpu.PrefetchScalarGridSpec(
            num_scalar_prefetch=1,
            grid=(steps + 1,),
            in_specs=[whole(*part.shape) for part in pieces]
            + [
                whole(tok_here, width),
                whole(2, width),
                whole(tok_here, width),
                whole(width, width),
                whole(width),
                whole(width),
                whole(width),
                pl.BlockSpec((width, width), lambda j, b: (0, at(j))),
                whole(hidden_units),
                pl.BlockSpec((width, width), lambda j, b: (at(j), 0)),
                whole(width),
            ],
            out_specs=[whole(tok_here, width)] * 2
            + [whole(*shape) for shape in shapes]
            + [slots, slots, whole(4, width), pl.BlockSpec((1, width), lambda j, b: (0, at(j)))],
            scratch_shapes=[
                pltpu.VMEM((width, tok_here), BF16),
                pltpu.VMEM((tok_here, width), BF16),
                pltpu.VMEM((tok_here, width), F32),
                pltpu.VMEM((tok_here, width), BF16),
                pltpu.VMEM((tok_here, width), BF16),
                pltpu.VMEM((tok_here, width), F32),
                pltpu.VMEM((tok_here, width), F32),
                pltpu.VMEM((tok_here, width), BF16),
                pltpu.VMEM((width, tok_here), BF16),
                pltpu.VMEM((steps, width), F32),
            ],
        ),
        out_shape=[
            jax.ShapeDtypeStruct((tok_here, width), BF16),
            jax.ShapeDtypeStruct((tok_here, width), F32),
        ]
        + [jax.ShapeDtypeStruct(shape, BF16) for shape in shapes]
        + [
            slot_shape,
            slot_shape,
            jax.ShapeDtypeStruct((4, width), F32),
            jax.ShapeDtypeStruct((1, hidden_units), F32),
        ],
        compiler_params=pltpu.CompilerParams(vmem_limit_bytes=VMEM),
        cost_estimate=pl.CostEstimate(
            flops=12 * tok_here * up_w.size, transcendentals=0, bytes_accessed=8 * up_w.size
        ),
        name="mlp",
    )(place, *pieces, tokens, rows, cotangent, out_w, out_b, gain, shift, up_w, up_b, down_w, down_b)
    grads = out[2 : 2 + len(shapes)]
    grads = [grads[g * sources : (g + 1) * sources] for g in range(len(groups[1]))]
    return out[0], out[1], grads, out[-4:]


def unproject(scalars, back, weight, packed, bias, chosen, rounds, sources):
    step = pl.program_id(0)
    size = len(chosen) * HEAD_DIM
    for index, part in enumerate(back):
        group, j = divmod(index, sources)
        at = (scalars[0] ^ j) * size + group * HEAD_DIM
        packed[pl.ds(pl.multiple_of(at, HEAD_DIM), HEAD_DIM), :] = part[0]
    columns = [(source * rounds + chosen[0]) * HEAD_DIM for source in range(sources)]
    ones = jnp.ones((8, packed.shape[1]), BF16)
    found = dot(ones, packed[...], NT)[0:1]

    @pl.when(step == 0)
    def _():
        bias[...] = jnp.zeros_like(bias)

    for part in range(3):

        @pl.when(step == part)
        def _():
            for source, start in enumerate(columns):
                here = found[:, source * size : (source + 1) * size]
                bias[part : part + 1, start : start + size] = here

    picked = jnp.concatenate([weight[:, start : start + size] for start in columns], 1)
    return dot(packed[...], picked, (((0,), (1,)), ((), ())))


def begin_kernel(scalars, *refs, chosen, rounds, sources):
    back, (weight, g_normed, bias, packed) = refs[:-4], refs[-4:]
    added = unproject(scalars, back, weight, packed, bias, chosen, rounds, sources)

    @pl.when(pl.program_id(0) == 0)
    def _():
        g_normed[...] = added

    @pl.when(pl.program_id(0) > 0)
    def _():
        g_normed[...] += added


def finish_kernel(scalars, *refs, chosen, rounds, sources, block):
    pieces = len(chosen) * sources
    back, refs = refs[:pieces], refs[pieces:]
    weight, tokens, rows, gain, g_resid, vectors, g_up_b, g_before, bias_before = refs[:9]
    g_tokens, sums, g_normed, packed, bias = refs[9:]
    step, last = pl.program_id(0), pl.num_programs(0) - 1
    added = unproject(scalars, back, weight, packed, bias, chosen, rounds, sources)

    @pl.when(step == 0)
    def _():
        g_normed[...] = g_before[...] + added

    @pl.when(step > 0)
    def _():
        g_normed[...] += added

    @pl.when(step == last)
    def _():
        width = tokens.shape[1]
        count = tokens.shape[0] // block
        empty = jnp.zeros((1, width), F32)

        def half(first):
            def body(index, totals):
                here = token_block(index + first * (count // 2), block)
                scaled, inverse = normalize(tokens[here, :].astype(F32) + rows[first : first + 1, :])
                grad = g_normed[here, :]
                inner = grad * row_of(gain)
                g_hidden = g_resid[here, :] + inverse * (
                    inner
                    - jnp.mean(inner, -1, keepdims=True)
                    - scaled * jnp.mean(inner * scaled, -1, keepdims=True)
                )
                g_tokens[here, :] = g_hidden.astype(BF16)
                parts = (grad * scaled, grad, g_hidden)
                return tuple(old + column_sum(new) for old, new in zip(totals, parts))

            return lax.fori_loop(0, count // 2, body, (empty,) * 3)

        one, two = half(0), half(1)
        sums[0:1, :], sums[1:2, :] = one[0] + two[0], one[1] + two[1]
        sums[2:6, :] = vectors[...]
        for index in range(4):
            sums[6 + index : 7 + index, :] = g_up_b[:, index * width : (index + 1) * width]
        lane = lax.broadcasted_iota(jnp.int32, (1, width), 1)
        is_short = scalars[1] != 0
        sums[10:13, :] = bias_before[...] + bias[...]
        pick = lambda at, other: jnp.where(lane == at, scalars[2 + at].astype(F32), other)
        sums[13:14, :] = jnp.where(scalars[0] == 0, pick(0, pick(1, 0.0)), 0.0)
        sums[14:15, :] = jnp.where(is_short, one[2], one[2] + two[2])
        sums[15:16, :] = jnp.where(is_short, two[2], 0.0)


def back_specs(back, width):
    block = pl.BlockSpec((1,) + back[0].shape[1:], lambda i, p: (i, 0, 0))
    return [block] * len(back) + [pl.BlockSpec((width, width), lambda i, p: (0, i))]


def begin_finish(scalars, back, chosen, weight, rounds):
    sources = len(back[0])
    pieces = [part for group in back for part in group]
    width, tok_here = weight.shape[0], pieces[0].shape[2]
    return pl.pallas_call(
        partial(begin_kernel, chosen=chosen, rounds=rounds, sources=sources),
        grid_spec=pltpu.PrefetchScalarGridSpec(
            num_scalar_prefetch=1,
            grid=(3,),
            in_specs=back_specs(pieces, width),
            out_specs=[whole(tok_here, width), whole(3, width)],
            scratch_shapes=[pltpu.VMEM((sources * len(chosen) * HEAD_DIM, tok_here), BF16)],
        ),
        out_shape=[
            jax.ShapeDtypeStruct((tok_here, width), F32),
            jax.ShapeDtypeStruct((3, width), F32),
        ],
        compiler_params=pltpu.CompilerParams(vmem_limit_bytes=VMEM),
        cost_estimate=pl.CostEstimate(
            flops=2 * tok_here * weight.size, transcendentals=0, bytes_accessed=4 * weight.size
        ),
        name="begin_finish",
    )(scalars, *pieces, weight)


def finish(scalars, back, chosen, weight, tokens, rows, gain, g_resid, vectors, g_up_b, before, rounds):
    tok_here, width = tokens.shape
    sources = len(back[0])
    pieces = [part for group in back for part in group]
    return pl.pallas_call(
        partial(finish_kernel, chosen=chosen, rounds=rounds, sources=sources, block=tok_here // 4),
        grid_spec=pltpu.PrefetchScalarGridSpec(
            num_scalar_prefetch=1,
            grid=(3,),
            in_specs=back_specs(pieces, width)
            + [
                whole(tok_here, width),
                whole(2, width),
                whole(width),
                whole(tok_here, width),
                whole(*vectors.shape),
                whole(*g_up_b.shape),
                whole(tok_here, width),
                whole(3, width),
            ],
            out_specs=[whole(tok_here, width), whole(16, width)],
            scratch_shapes=[
                pltpu.VMEM((tok_here, width), F32),
                pltpu.VMEM((sources * len(chosen) * HEAD_DIM, tok_here), BF16),
                pltpu.VMEM((3, width), F32),
            ],
        ),
        out_shape=[
            jax.ShapeDtypeStruct((tok_here, width), BF16),
            jax.ShapeDtypeStruct((16, width), F32),
        ],
        compiler_params=pltpu.CompilerParams(vmem_limit_bytes=VMEM),
        cost_estimate=pl.CostEstimate(
            flops=2 * tok_here * weight.size, transcendentals=0, bytes_accessed=8 * weight.size
        ),
        name="finish",
    )(scalars, *pieces, weight, tokens, rows, gain, g_resid, vectors, g_up_b, *before)


def qkv_grad_kernel(block_ref, *refs, rounds, sources, order):
    grads, refs = refs[: rounds * sources], refs[rounds * sources :]
    normed, (first, second, store) = refs[:sources], refs[sources:]
    size = 3 * HEAD_DIM
    for r in range(rounds):
        total = None
        for grad, part in zip(grads[r * sources : (r + 1) * sources], normed):
            here = jnp.concatenate([grad[p] for p in range(3)], 0)
            term = dot(here, part[...])
            total = term if total is None else total + term
        store[:, r * size : (r + 1) * size] = total.T.astype(BF16)
    half = len(order) // 2
    rows = first.shape[1]
    for at, index in enumerate(order):
        start = (block_ref[0] ^ index) * rows
        here = pl.ds(pl.multiple_of(start, rows), rows) if half > 1 else slice(at * rows, (at + 1) * rows)
        (second if at >= half else first)[at % half] = store[here, :]


def qkv_grad(block, grads, normed, order):
    rounds, sources = len(grads), len(normed)
    tok_here, width = normed[0].shape
    size = 3 * HEAD_DIM * rounds
    pieces = [part for group in grads for part in group]
    half = (len(order) // 2, width // len(order), size)
    return pl.pallas_call(
        partial(qkv_grad_kernel, rounds=rounds, sources=sources, order=order),
        grid_spec=pltpu.PrefetchScalarGridSpec(
            num_scalar_prefetch=1,
            grid=(1,),
            in_specs=[whole(*pieces[0].shape)] * len(pieces) + [whole(tok_here, width)] * sources,
            out_specs=[whole(*half)] * 2,
            scratch_shapes=[pltpu.VMEM((width, size), BF16)],
        ),
        out_shape=[jax.ShapeDtypeStruct(half, BF16)] * 2,
        compiler_params=pltpu.CompilerParams(vmem_limit_bytes=VMEM),
        cost_estimate=pl.CostEstimate(
            flops=8 * tok_here * width * size, transcendentals=0, bytes_accessed=12 * tok_here * width
        ),
        name="qkv_grad",
    )(block, *pieces, *normed)


def swap(values, axis, bit):
    size = lax.axis_size(axis)
    return lax.ppermute(values, axis, [(j, j ^ bit) for j in range(size)])


def trade(parts, axis):
    return [parts[0]] + [swap(part, axis, i) for i, part in enumerate(parts) if i]


def spread(values, axis, count):
    return [values] + [swap(values, axis, i) for i in range(1, count)]


def total_of(parts):
    total = parts[0].astype(F32)
    for part in parts[1:]:
        total = total + part.astype(F32)
    return total


def after(values, *others):
    return lax.optimization_barrier((values, *others))[0]


def deal_kernel(bits_ref, *refs, steps):
    keep, got, (outgoing, staying) = refs[: steps + 2], refs[steps + 2 : 2 * steps + 4], refs[-2:]
    gate = bits_ref[0]
    for out, side in ((outgoing, 1 - gate), (staying, gate)):
        at = 0
        for left, right in zip(keep, got):
            rows = left.shape[2] // 2
            here = pl.ds(pl.multiple_of(side * rows, rows), rows)
            total = left[0, 0, here, :].astype(F32) + right[0, 0, here, :].astype(F32)
            out[0, at : at + rows, :] = total.astype(BF16)
            at += rows


def deal(gate, keep, got, dp):
    slots, width, lanes = keep.shape
    steps = slots // 2 - 1
    up_each, each = width * steps // dp, width // dp
    per_slot = width // up_each
    up = pl.BlockSpec(
        (1, 1, up_each, lanes),
        lambda i, b: (2 * (i // per_slot), i % per_slot, 0, 0),
    )
    rest = [
        pl.BlockSpec((1, 1, each, lanes), lambda i, b, slot=slot: (slot, i, 0, 0))
        for slot in [2 * k + 1 for k in range(steps)] + [2 * steps]
    ]
    views = lambda array: [array.reshape(slots, per_slot, up_each, lanes)] + [
        array.reshape(slots, dp, each, lanes)
    ] * (steps + 1)
    rows = up_each // 2 + (steps + 1) * each // 2
    shape = jax.ShapeDtypeStruct((dp, rows, lanes), BF16)
    return pl.pallas_call(
        partial(deal_kernel, steps=steps),
        grid_spec=pltpu.PrefetchScalarGridSpec(
            num_scalar_prefetch=1,
            grid=(dp,),
            in_specs=([up] + rest) * 2,
            out_specs=[pl.BlockSpec((1, rows, lanes), lambda i, b: (i, 0, 0))] * 2,
        ),
        out_shape=[shape, shape],
        cost_estimate=pl.CostEstimate(flops=keep.size, transcendentals=0, bytes_accessed=6 * keep.size),
        name="deal",
    )(gate, *views(keep), *views(got))


def undeal_kernel(place_ref, *refs, sources, steps, each):
    shares, (up, down, out, store) = refs[:sources], refs[sources:]
    lanes = store.shape[2]
    for j, share in enumerate(shares):
        store[place_ref[0] ^ j] = share[...].astype(F32)
    wide = steps * each
    for low in range(2):
        both = lambda at, size: jnp.concatenate([store[low, at : at + size], store[2 + low, at : at + size]], 0).T
        up[low * lanes : (low + 1) * lanes, :] = both(0, wide)
        for half in range(2):
            here = slice(half * each, (half + 1) * each)
            share = store.at[2 * half + low]
            for k in range(steps):
                at, row = (2 * k + low) * lanes, wide + k * each
                down[here, at : at + lanes] = share[row : row + each]
            out[here, low * lanes : (low + 1) * lanes] = share[2 * wide : 2 * wide + each]


def undeal(place, shares, steps, width, dp):
    rows, lanes = shares[0].shape
    shapes = [(width, width * steps // dp), (width // dp, width * steps), (width // dp, width)]
    up, down, out = pl.pallas_call(
        partial(undeal_kernel, sources=len(shares), steps=steps, each=width // dp // 2),
        grid_spec=pltpu.PrefetchScalarGridSpec(
            num_scalar_prefetch=1,
            grid=(1,),
            in_specs=[whole(rows, lanes)] * len(shares),
            out_specs=[whole(*shape) for shape in shapes],
            scratch_shapes=[pltpu.VMEM((len(shares), rows, lanes), F32)],
        ),
        out_shape=[jax.ShapeDtypeStruct(shape, F32) for shape in shapes],
        cost_estimate=pl.CostEstimate(flops=0, transcendentals=0, bytes_accessed=24 * rows * lanes),
        name="undeal",
    )(place, *shares)
    return up, down.T, out.T


def turn_kernel(*refs):
    *parts, out = refs
    out[...] = total_of([part[0] for part in parts]).T.astype(BF16)


def turn(parts):
    _, rows, columns = parts[0].shape
    return pl.pallas_call(
        turn_kernel, out_shape=jax.ShapeDtypeStruct((columns, rows), BF16), name="turn"
    )(*parts)


def regroup_kernel(place_ref, *refs, rounds):
    *shares, out = refs
    sources = len(shares)
    for j, share in enumerate(shares):
        for r in range(rounds):
            for p in range(3):
                at = ((p * sources + (place_ref[0] ^ j)) * rounds + r) * HEAD_DIM
                start = (r * 3 + p) * HEAD_DIM
                out[pl.ds(pl.multiple_of(at, HEAD_DIM), HEAD_DIM), :] = share[start : start + HEAD_DIM]


def regroup(place, shares, rounds):
    columns, rows = shares[0].shape
    total = columns * len(shares)
    return pl.pallas_call(
        partial(regroup_kernel, rounds=rounds),
        grid_spec=pltpu.PrefetchScalarGridSpec(
            num_scalar_prefetch=1,
            grid=(1,),
            in_specs=[whole(columns, rows)] * len(shares),
            out_specs=whole(total, rows),
        ),
        out_shape=jax.ShapeDtypeStruct((total, rows), BF16),
        name="regroup",
    )(place, *shares)


def stack_kernel(parts, out):
    both = [parts[index].astype(F32) for index in range(parts.shape[0])]
    out[...] = jnp.concatenate(both, 1)


def stack_rows(parts):
    count, columns, rows = parts.shape
    return pl.pallas_call(
        stack_kernel, out_shape=jax.ShapeDtypeStruct((columns, rows * count), F32), name="stack_rows"
    )(parts).T


def exchange(values, axis):
    return lax.all_to_all(values, axis, split_axis=0, concat_axis=0, tiled=True)


def wide_sums(slots, place, dp):
    steps, width, lanes = slots.shape[0] // 2 - 1, slots.shape[1], slots.shape[2]
    pairs = slots.reshape(steps + 1, 2, width, lanes)
    up = pairs[:steps, 0].reshape(dp, 2, -1, lanes)
    down = pairs[:steps, 1].reshape(steps, dp, 2, -1, lanes)
    down = jnp.moveaxis(down, 0, 2).reshape(dp, 2, -1, lanes)
    out = pairs[steps, 0].reshape(dp, 2, -1, lanes)
    dealt = jnp.concatenate([up, down, out], 2)
    gate = place // 2
    pick = lambda index: lax.dynamic_index_in_dim(dealt, index, 1, keepdims=False)
    half_sum = total_of([pick(gate), swap(pick(1 - gate), "seq", 2)]).astype(BF16)
    share = jnp.sum(exchange(half_sum, "dp").astype(F32), 0).astype(BF16)
    shares = lax.all_gather(share, "seq", axis=0).reshape(2, 2, -1, lanes).astype(F32)
    each = width // dp // 2
    up, down, out = jnp.split(shares, [steps * each, 2 * steps * each], 2)
    turned = lambda part: jnp.transpose(part, (1, 3, 0, 2)).reshape(2 * lanes, -1)
    down = down.reshape(2, 2, steps, each, lanes)
    down = jnp.transpose(down, (2, 1, 4, 0, 3)).reshape(steps * 2 * lanes, 2 * each)
    return turned(up), down, turned(out)


def wide_columns(grads, dp, sources, rounds):
    grad = jnp.concatenate(grads, 2).reshape(-1, 3 * HEAD_DIM * rounds)
    width, columns = grad.shape
    rows = width // dp
    summed = jnp.sum(exchange(grad.reshape(dp, rows, columns), "dp").astype(F32), 0).astype(BF16)
    gathered = lax.all_gather(summed, "seq", axis=0).reshape(sources, rows, rounds, 3, HEAD_DIM)
    ordered = jnp.transpose(gathered, (1, 3, 0, 2, 4)).reshape(rows, dp, -1)
    return exchange(jnp.swapaxes(ordered, 0, 1), "dp").reshape(width, -1).astype(F32)


def on_device(
    tokens,
    time_steps,
    data_group,
    cotangent,
    attn_norm_gain,
    attn_norm_bias,
    qkv_weight,
    query_bias,
    value_bias,
    out_weight,
    out_bias,
    mlp_norm_gain,
    mlp_norm_bias,
    up_weight,
    up_bias,
    down_weight,
    down_bias,
    time_table,
):
    sources, dp = lax.axis_size("seq"), lax.axis_size("dp")
    place, block = lax.axis_index("seq"), lax.axis_index("dp")
    tokens, cotangent = tokens[0], cotangent[0]
    tok_here, width = tokens.shape
    hidden_units = up_weight.shape[1]
    rounds = HEADS // sources
    is_short = data_group[0] == 0
    short_flag = is_short.astype(jnp.int32)[None]
    place_arg = place.astype(jnp.int32)[None]
    block_arg = block.astype(jnp.int32)[None]
    few = dp <= 8
    row_steps = jnp.where(is_short, time_steps[0], time_steps[0, 0])
    scalars = jnp.concatenate([place_arg, short_flag, lax.div(row_steps, 8), lax.rem(row_steps, 8)])

    normed, rows, sending = project(
        scalars,
        tokens,
        time_table,
        attn_norm_gain,
        attn_norm_bias,
        qkv_weight,
        query_bias,
        value_bias,
        sources,
        rounds,
    )
    heads, saved, sent = [trade(sending[0], "seq")], [], []
    returned = []
    for r in range(rounds):
        if r + 1 < rounds:
            ahead = sending[r + 1] if r < 1 else after(sending[r + 1], saved[r - 1][1])
            heads.append(trade(ahead, "seq"))
        ready = after(heads[r], saved[r - 1][1]) if r else heads[r]
        out, kept = attend(short_flag, ready, sent[0] if r == 1 else ())
        saved.append(kept)
        sent.append(out)
        if r >= 1:
            returned.append(trade(after(out, *returned[-1]) if returned else out, "seq"))

    beside = swap(after(normed, saved[1][1]), "seq", 1)
    across = swap(after(normed, *returned[-1]), "seq", 2)
    groups = (((0, 1), (2,)), ((0,), (1, 2)))
    result, g_resid, sent_grads, (send, keep, vectors, g_up_b) = mlp(
        place_arg,
        groups,
        returned,
        after(tokens, beside),
        rows,
        cotangent,
        out_weight,
        out_bias,
        mlp_norm_gain,
        mlp_norm_bias,
        up_weight,
        up_bias,
        down_weight,
        down_bias,
    )
    send, *sent_grads = after((send, *sent_grads), across)
    got = swap(send, "seq", 1)
    first_grads = trade(sent_grads[0], "seq")
    if few:
        outgoing, staying = deal(place_arg // 2, keep, got, dp)
        got = swap(outgoing, "seq", 2)
        ready = outgoing
    else:
        ready = summed = total_of([keep, got]).astype(BF16)
    rest_grads = trade(after(sent_grads[1], *first_grads), "seq")
    beside = [normed, beside, across, swap(across, "seq", 1)]
    grads = [attend_back(short_flag, after(heads[0], ready, beside[3]), saved[0], first_grads, 0)]
    back = [trade(grads[0], "seq")]
    held = after(heads[1], *grads[0])
    grads.append(attend_back(short_flag, held, saved[1], rest_grads, 0))
    back.append(trade(grads[1], "seq"))
    order = (0, 4, 2, 6, 1, 5, 3, 7) if few else (0, 1)
    stay_a, away_a = qkv_grad(block_arg, grads, beside, order)
    if few:
        got_a = swap(away_a, "dp", 1)
        half_sum = total_of([staying, after(got, grads[1])]).astype(BF16)
        dealt = exchange(half_sum, "dp")
        ready = half_sum
    held = after(heads[2], stay_a, ready, *back[0])
    grads.append(attend_back(short_flag, held, saved[2], rest_grads, 1))
    back.append(trade(grads[2], "seq"))
    grads[2] = after(grads[2], *back[1])
    stay_b, away_b = qkv_grad(block_arg, grads[2:], beside, order)
    earlier = [after(parts, stay_b) for parts in back[:2]]
    before = begin_finish(scalars, earlier, (0, 1), qkv_weight, rounds)
    ready = before[1]
    if few:
        kept, got = [stay_a, stay_b], [after(got_a, grads[2]), swap(away_b, "dp", 1)]
        part = jnp.concatenate([total_of(pair).astype(BF16) for pair in zip(kept, got)], 2)
        share = total_of([after(dealt, before[1])[i] for i in range(dp)]).astype(BF16)
        ready = part, share
        sums = [part[:1]] + [swap(part[at : at + 1], "dp", bit) for at, bit in ((1, 4), (2, 2), (3, 6))]
        share_across = swap(share, "seq", 2)

    steps_arg = time_steps[0].astype(jnp.int32)
    flags = jnp.concatenate([place_arg, short_flag, steps_arg])
    g_tokens, small = finish(
        flags,
        after(back[2:], ready),
        (2,),
        qkv_weight,
        tokens,
        rows,
        attn_norm_gain,
        g_resid,
        vectors,
        g_up_b,
        before,
        rounds,
    )
    if few:
        shares = [share, swap(share, "seq", 1), share_across, swap(share_across, "seq", 1)]
        small_parts = spread(small, "seq", sources)
        summed = turn(after(sums, small))
        columns = regroup(place_arg, spread(summed, "seq", sources), rounds)
        small = total_of(after(small_parts, summed))
    else:
        small = total_of(spread(small, "seq", sources))
    if few:
        own, other = small, swap(small, "dp", 1)
        small = jnp.concatenate([own[:13] + other[:13], own[13:], other[13:]])
        all_small = jnp.stack([small] + [swap(small, "dp", bit) for bit in (2, 4, 6)])
        small = jnp.sum(all_small[:, :13], 0)
        by_block = all_small[:, 13:].reshape(dp, 3, width)
    else:
        slots = jnp.where((jnp.arange(dp) == block)[:, None, None], small[None, 13:], 0.0)
        small = jnp.concatenate([small[:13], slots.reshape(-1, width)])
        bit = 1
        while bit < dp:
            small = small + swap(small, "dp", bit)
            bit *= 2
        by_block = small[13:].reshape(dp, 3, width)
    steps = by_block[:, 0, :2].reshape(1, -1).astype(jnp.int32)
    all_rows = by_block[:, 1:].reshape(-1, width)
    if few:
        sum_up, sum_down, sum_out = undeal(place_arg, shares, hidden_units // width, width, dp)
        sum_qkv = stack_rows(exchange(columns.reshape(dp, 3 * width // dp, width // dp), "dp"))
    else:
        sum_up, sum_down, sum_out = wide_sums(summed, place, dp)
        sum_qkv = wide_columns(
            [jnp.stack(pair).reshape(2, width // 2, -1) for pair in ((stay_a, away_a), (stay_b, away_b))],
            dp,
            sources,
            rounds,
        )
    share_cols = width // dp
    rows_mine = lax.dynamic_slice_in_dim(all_rows, block * share_cols, share_cols, 1)
    table_rows = time_table.shape[0]
    hits = jnp.arange(table_rows, dtype=jnp.int32)[:, None] == steps
    sum_table = jnp.dot(hits.astype(F32), rows_mine, precision=lax.Precision.HIGHEST)
    return (
        result[None],
        g_tokens[None],
        small[0],
        small[1],
        sum_qkv,
        small[10],
        small[12],
        sum_out,
        small[4],
        small[2],
        small[3],
        sum_up,
        small[6:10].reshape(-1),
        sum_down,
        small[5],
        sum_table,
    )


def solution(mesh):
    placed = (P("dp", "seq", None), P("dp", None), P("dp"), P("dp", "seq", None)) + (P(),) * 14
    column = P(None, "dp")
    return jax.shard_map(
        on_device,
        mesh=mesh,
        in_specs=placed,
        out_specs=(
            P("dp", "seq", None),
            P("dp", "seq", None),
            P(),
            P(),
            column,
            P(),
            P(),
            column,
            P(),
            P(),
            P(),
            column,
            P(),
            column,
            P(),
            column,
        ),
        check_vma=False,
    )
```

```python
from functools import partial

import jax
import jax.numpy as jnp
from jax import lax
from jax.experimental import pallas as pl
from jax.experimental.pallas import tpu as pltpu
from jax.sharding import PartitionSpec as P

HEADS = 12
HEAD_DIM = 64
EPSILON = 1e-05
LOG2E = 1.4426950408889634
SCALE = HEAD_DIM**-0.5
BF16 = jnp.bfloat16
F32 = jnp.float32
NN = (((1,), (0,)), ((), ()))
NT = (((1,), (1,)), ((), ()))
TN = (((0,), (0,)), ((), ()))
VMEM = 62 << 20
SMALL_VMEM = 40 << 20


def dot(left, right, dims=NN):
    return lax.dot_general(left, right, dims, preferred_element_type=F32)


def split_low(values, count):
    parts = []
    for _ in range(count):
        term = values.astype(BF16)
        parts.append(term)
        values = values - term.astype(F32)
    return parts


def whole(*shape):
    return pl.BlockSpec(shape, lambda *_: (0,) * len(shape))


def halves(sources, segment):
    for chunk in range(2 * sources):
        source, part = divmod(chunk, 2)
        yield chunk, source, slice(part * segment, (part + 1) * segment)


def over_chunks(short_ref, chunks, body):
    is_short = short_ref[0] != 0
    part = lax.rem(pl.program_id(0), 2)

    @pl.when(is_short)
    def _():
        body([2 * k + part for k in range(chunks // 2)], True)

    @pl.when(jnp.logical_not(is_short))
    def _():
        body(list(range(chunks)), True)


def attend_kernel(short_ref, *refs, sources, segment, held):
    heads, refs = refs[:sources], refs[sources:]
    earlier, refs = refs[: sources * held], refs[sources * held :]
    sent, refs = refs[:sources], refs[sources:]
    mixed_ref, inverse_ref, weights_ref, queries, keys, values, sums, bounded = refs
    step = pl.program_id(0)
    chunks = 2 * sources
    depth = HEAD_DIM

    @pl.when(step == 0)
    def _():
        for old, new in zip(earlier, sent):
            new[0] = old[0]
        longest = [jnp.zeros((1, segment), F32)] * 2
        for chunk, source, cols in halves(sources, segment):
            scaled = heads[source][0, :, cols].astype(F32) * (SCALE * LOG2E)
            high, low = split_low(scaled, 2)
            queries[chunk, 0:64, :] = high
            queries[chunk, 64:128, :] = low
            queries[chunk, 128:144, :] = jnp.zeros((16, segment), BF16)
            key = heads[source][1, :, cols]
            keys[chunk, 0:64, :] = key
            keys[chunk, 64:128, :] = key
            keys[chunk, 128:144, :] = jnp.full((16, segment), -1.0, BF16)
            values[chunk, 0:64, :] = heads[source][2, :, cols]
            values[chunk, 64:80, :] = jnp.ones((16, segment), BF16)
            sizes = [jnp.sum(x * x, 0, keepdims=True) for x in (scaled, key.astype(F32))]
            longest = [jnp.maximum(old, new) for old, new in zip(longest, sizes)]
        bound = jnp.max(longest[0]) * jnp.max(longest[1])
        bounded[0] = (bound <= 3600.0).astype(jnp.int32)

    @pl.when(bounded[0] == 0)
    def _():
        query = queries[step][0:128]
        is_short = (short_ref[0] != 0).astype(jnp.int32)

        def body(index, peak):
            chunk = jnp.where(is_short != 0, 2 * index + lax.rem(step, 2), index)
            scores = dot(keys[chunk][0:128], query, TN)
            return jnp.maximum(peak, jnp.max(scores, 0, keepdims=True))

        start = jnp.full((1, segment), -jnp.inf, F32)
        peak = lax.fori_loop(0, jnp.where(is_short != 0, chunks // 2, chunks), body, start)
        zeros = jnp.zeros((13, segment), BF16)
        queries[step, 128:144, :] = jnp.concatenate(split_low(peak, 3) + [zeros], 0)

    def body(order, first):
        query = queries[step]
        total = None
        later = dot(keys[order[0]], query, TN)
        for index, chunk in enumerate(order):
            scores = later
            if index + 1 < len(order):
                later = dot(keys[order[index + 1]], query, TN)
            weights = jnp.exp2(scores).astype(BF16)
            weights_ref[0, chunk] = weights.T
            mixed = dot(values[chunk], weights)
            total = mixed if total is None else total + mixed
        sums[...] = total if first else sums[...] + total

    over_chunks(short_ref, chunks, body)
    total = sums[...]
    inverse = 1.0 / total[depth : depth + 1, :]
    result = total[:depth] * inverse
    mixed_ref[step] = result
    inverse_ref[step] = inverse
    for chunk, source, cols in halves(sources, segment):

        @pl.when(step == chunk)
        def _():
            sent[source][held, :, cols] = result.astype(BF16)


def attend(is_short, heads, earlier=()):
    sources = len(heads)
    _, depth, tokens = heads[0].shape
    segment, chunks = tokens // 2, 2 * sources
    work = (sources * tokens) ** 2
    held = len(earlier) // sources
    out = pl.pallas_call(
        partial(attend_kernel, sources=sources, segment=segment, held=held),
        grid_spec=pltpu.PrefetchScalarGridSpec(
            num_scalar_prefetch=1,
            grid=(chunks,),
            in_specs=[whole(3, depth, tokens)] * sources + [whole(1, depth, tokens)] * len(earlier),
            out_specs=[whole(1 + held, depth, tokens)] * sources
            + [
                whole(chunks, depth, segment),
                whole(chunks, 1, segment),
                pl.BlockSpec((1, chunks, segment, segment), lambda i, s: (i, 0, 0, 0)),
            ],
            scratch_shapes=[
                pltpu.VMEM((chunks, 144, segment), BF16),
                pltpu.VMEM((chunks, 144, segment), BF16),
                pltpu.VMEM((chunks, 80, segment), BF16),
                pltpu.VMEM((80, segment), F32),
                pltpu.SMEM((1,), jnp.int32),
            ],
        ),
        out_shape=[jax.ShapeDtypeStruct((1 + held, depth, tokens), BF16)] * sources
        + [
            jax.ShapeDtypeStruct((chunks, depth, segment), F32),
            jax.ShapeDtypeStruct((chunks, 1, segment), F32),
            jax.ShapeDtypeStruct((chunks, chunks, segment, segment), BF16),
        ],
        compiler_params=pltpu.CompilerParams(vmem_limit_bytes=SMALL_VMEM),
        cost_estimate=pl.CostEstimate(
            flops=16 * work * depth, transcendentals=work, bytes_accessed=2 * work
        ),
        name="attend",
    )(is_short, *heads, *earlier)
    return out[:sources], out[-3:]


def attend_back_kernel(short_ref, *refs, sources, segment):
    heads, grads, (mixed_ref, inverse_ref, weights_ref), refs = (
        refs[:sources],
        refs[sources : 2 * sources],
        refs[2 * sources : 2 * sources + 3],
        refs[2 * sources + 3 :],
    )
    outs, (queries, g_aug, v_aug, grad_q, grad_kv) = refs[:sources], refs[sources:]
    step = pl.program_id(0)
    chunks = 2 * sources

    @pl.when(step == 0)
    def _():
        zeros = jnp.zeros((13, segment), BF16)
        for chunk, source, cols in halves(sources, segment):
            queries[chunk] = heads[source][0, :, cols]
            grad = grads[source][0, :, cols].astype(F32) * inverse_ref[chunk]
            high, low = split_low(grad, 2)
            g_aug[chunk, 0:64, :] = high
            g_aug[chunk, 64:128, :] = low
            inner = jnp.sum(grad * mixed_ref[chunk], 0, keepdims=True)
            g_aug[chunk, 128:144, :] = jnp.concatenate(split_low(inner, 3) + [zeros], 0)
        grad_q[...] = jnp.zeros_like(grad_q)

    def column(index):
        for chunk, source, cols in halves(sources, segment):

            @pl.when(step == chunk)
            def _():
                index(source, cols)

    def load(source, cols):
        value = heads[source][2, :, cols]
        v_aug[0:64, :] = value
        v_aug[64:128, :] = value
        v_aug[128:144, :] = jnp.full((16, segment), -1.0, BF16)
        v_aug[144:208, :] = heads[source][1, :, cols]

    column(load)
    value = v_aug[0:144]
    turned = v_aug[144:208].T

    def body(order, first):
        key_total = value_total = None
        later = dot(g_aug[order[0]], value, TN)
        for index, chunk in enumerate(order):
            slopes = later
            if index + 1 < len(order):
                later = dot(g_aug[order[index + 1]], value, TN)
            weights = weights_ref[chunk, 0]
            g_scores = (weights.astype(F32) * slopes).astype(BF16)
            value_part = dot(g_aug[chunk, 0:128, :], weights)
            key_part = dot(queries[chunk], g_scores)
            value_total = value_part if value_total is None else value_total + value_part
            key_total = key_part if key_total is None else key_total + key_part
            grad_q[chunk] += dot(g_scores, turned)
        both = jnp.concatenate([key_total, value_total[0:64] + value_total[64:128]], 0)
        grad_kv[...] = both if first else grad_kv[...] + both

    over_chunks(short_ref, chunks, body)

    def save(source, cols):
        outs[source][1, :, cols] = (grad_kv[0:64] * SCALE).astype(BF16)
        outs[source][2, :, cols] = grad_kv[64:128].astype(BF16)

    column(save)

    @pl.when(step == chunks - 1)
    def _():
        for chunk, source, cols in halves(sources, segment):
            outs[source][0, :, cols] = (grad_q[chunk] * SCALE).T.astype(BF16)


def attend_back(is_short, heads, saved, grads, at):
    sources = len(heads)
    _, depth, tokens = heads[0].shape
    segment, chunks = tokens // 2, 2 * sources
    work = (sources * tokens) ** 2
    return pl.pallas_call(
        partial(attend_back_kernel, sources=sources, segment=segment),
        grid_spec=pltpu.PrefetchScalarGridSpec(
            num_scalar_prefetch=1,
            grid=(chunks,),
            in_specs=[whole(3, depth, tokens)] * sources
            + [pl.BlockSpec((1, depth, tokens), lambda i, s: (at, 0, 0))] * sources
            + [
                whole(chunks, depth, segment),
                whole(chunks, 1, segment),
                pl.BlockSpec((chunks, 1, segment, segment), lambda i, s: (0, i, 0, 0)),
            ],
            out_specs=[whole(3, depth, tokens)] * sources,
            scratch_shapes=[
                pltpu.VMEM((chunks, 64, segment), BF16),
                pltpu.VMEM((chunks, 144, segment), BF16),
                pltpu.VMEM((208, segment), BF16),
                pltpu.VMEM((chunks, segment, depth), F32),
                pltpu.VMEM((2 * depth, segment), F32),
            ],
        ),
        out_shape=[jax.ShapeDtypeStruct((3, depth, tokens), BF16)] * sources,
        compiler_params=pltpu.CompilerParams(vmem_limit_bytes=VMEM),
        cost_estimate=pl.CostEstimate(
            flops=40 * work * depth, transcendentals=work, bytes_accessed=2 * work
        ),
        name="attend_back",
    )(is_short, *heads, *grads, *saved)


def normalize(hidden):
    center = hidden - jnp.mean(hidden, -1, keepdims=True)
    spread = jnp.mean(center * center, -1, keepdims=True)
    inverse = lax.rsqrt(spread + EPSILON)
    return center * inverse, inverse


def token_block(index, size):
    return pl.ds(pl.multiple_of(index * size, size), size)


def column_sum(values):
    return jnp.sum(values.astype(F32), 0, keepdims=True)


def row_of(vector):
    return vector[...].astype(F32)[None, :]


def project_kernel(
    scalars, tokens, first_rows, second_rows, gain, shift, weight, query_bias, value_bias, normed, rows, *refs,
    sources, rounds, block
):
    outs, turned, column = refs[:-2], refs[-2], refs[-1]
    step = pl.program_id(0)
    pairs = sources // 2
    count = tokens.shape[0] // block
    size = column.shape[1]

    @pl.when(step == 0)
    def _():
        for index, group in enumerate((first_rows, second_rows)):
            all_rows = group[...].astype(F32)
            chosen = lax.broadcasted_iota(jnp.int32, all_rows.shape, 0) == scalars[4 + index]
            rows[index : index + 1, :] = jnp.sum(jnp.where(chosen, all_rows, 0.0), 0, keepdims=True)
        biases = row_of(query_bias), jnp.zeros((1, pairs * size), F32), row_of(value_bias)
        for part, bias in enumerate(biases):
            for pair in range(pairs):
                here = jnp.broadcast_to(bias[:, pair * size : (pair + 1) * size], (128, size))
                column[part * pairs + pair] = here.T

        def body(index, _):
            here = token_block(index, block)
            row = rows[pl.ds(lax.div(index, count // 2), 1), :]
            scaled, _ = normalize(tokens[here, :].astype(F32) + row)
            low = (scaled * row_of(gain) + row_of(shift)).astype(BF16)
            normed[here, :] = low
            turned[:, here] = low.T
            return 0

        lax.fori_loop(0, count, body, 0)

    pair, high_bit, low_bit = lax.rem(step, pairs), lax.div(scalars[0], 2), lax.rem(scalars[0], 2)
    bias = column[step - pair + (pair ^ high_bit)][:, 0:1]
    result = (dot(weight[...], turned[...], TN) + bias).astype(BF16)
    for high in range(pairs):
        for bit in range(2):

            @pl.when((pair == high) & (low_bit == bit))
            def _():
                for low in range(2):
                    for r in range(rounds):
                        at = (low * rounds + r) * HEAD_DIM
                        outs[r * sources + 2 * high + (low ^ bit)][0] = result[at : at + HEAD_DIM]


def project(scalars, tokens, time_table, gain, shift, weight, query_bias, value_bias, sources, rounds):
    tok_here, width = tokens.shape
    pair = 2 * rounds * HEAD_DIM
    pairs = sources // 2
    group = lambda index: pl.BlockSpec((8, width), lambda i, p: (p[2 + index], 0))
    out = pl.pallas_call(
        partial(project_kernel, sources=sources, rounds=rounds, block=tok_here // 4),
        grid_spec=pltpu.PrefetchScalarGridSpec(
            num_scalar_prefetch=1,
            grid=(3 * pairs,),
            in_specs=[
                whole(tok_here, width),
                group(0),
                group(1),
                whole(width),
                whole(width),
                pl.BlockSpec((width, pair), lambda i, p: (0, pair_block(i, p, pairs))),
                whole(width),
                whole(width),
            ],
            out_specs=[whole(tok_here, width), whole(2, width)]
            + [pl.BlockSpec((1, HEAD_DIM, tok_here), lambda i, p: (lax.div(i, pairs), 0, 0))]
            * (rounds * sources),
            scratch_shapes=[
                pltpu.VMEM((width, tok_here), BF16),
                pltpu.VMEM((3 * pairs, pair, 128), F32),
            ],
        ),
        out_shape=[
            jax.ShapeDtypeStruct((tok_here, width), BF16),
            jax.ShapeDtypeStruct((2, width), F32),
        ]
        + [jax.ShapeDtypeStruct((3, HEAD_DIM, tok_here), BF16)] * (rounds * sources),
        compiler_params=pltpu.CompilerParams(vmem_limit_bytes=VMEM),
        cost_estimate=pl.CostEstimate(
            flops=2 * tok_here * weight.size, transcendentals=0, bytes_accessed=4 * weight.size
        ),
        name="project",
    )(scalars, tokens, time_table, time_table, gain, shift, weight, query_bias, value_bias)
    return out[0], out[1], [out[2 + r * sources : 2 + (r + 1) * sources] for r in range(rounds)]


def pair_block(step, scalars, pairs):
    at = lax.rem(step, pairs)
    return step - at + (at ^ lax.div(scalars[0], 2))


def mlp_kernel(place_ref, *refs, groups, sources, block):
    (in_groups, out_groups), rounds = groups, sum(map(len, groups[0]))
    gathered, refs = refs[: len(in_groups) * sources], refs[len(in_groups) * sources :]
    pieces = len(out_groups) * sources
    tokens, rows, cotangent, out_w, out_b, gain, shift, up_w, up_b, down_w, down_b = refs[:11]
    result, g_resid = refs[11:13]
    sent_grads = refs[13 : 13 + pieces]
    send, keep, vectors, g_up_b = refs[13 + pieces : 17 + pieces]
    attended, normed, resid, gelu_act, g_up, down_sum, g_normed, g_branch, g_attended, bias = refs[17 + pieces :]
    step, last = pl.program_id(0), pl.num_programs(0) - 1
    tok_here, width = tokens.shape
    count = tok_here // block
    place = place_ref[0]
    low_bit = lax.rem(place, 2) == 0

    def head_rows(groups):
        for index in range(len(groups) * sources):
            group, j = divmod(index, sources)
            for at, r in enumerate(groups[group]):
                start = ((place ^ j) * rounds + r) * HEAD_DIM
                yield index, at, pl.ds(pl.multiple_of(start, HEAD_DIM), HEAD_DIM)

    def put(slot, grad):
        grad = grad.astype(BF16)
        middle = grad.shape[1] // 2
        left, right = grad[:, :middle], grad[:, middle:]

        @pl.when(low_bit)
        def _():
            keep[slot], send[slot] = left, right

        @pl.when(jnp.logical_not(low_bit))
        def _():
            keep[slot], send[slot] = right, left

    @pl.when(step == 0)
    def _():
        bias_row = row_of(up_b)
        for index in range(bias.shape[0]):
            bias[index : index + 1, :] = bias_row[:, index * width : (index + 1) * width]
        for index, at, here in head_rows(in_groups):
            attended[here, :] = gathered[index][at]

        def body(index, _):
            here = token_block(index, block)
            row = rows[pl.ds(lax.div(index, count // 2), 1), :]
            hidden = tokens[here, :].astype(F32) + row
            total = hidden + (dot(attended[:, here], out_w[...], TN) + row_of(out_b))
            resid[here, :] = total
            scaled, _ = normalize(total)
            normed[here, :] = (scaled * row_of(gain) + row_of(shift)).astype(BF16)
            return 0

        lax.fori_loop(0, count, body, 0)
        down_sum[...] = jnp.zeros_like(down_sum)
        g_normed[...] = jnp.zeros_like(g_normed)

    @pl.when(step < last)
    def _():
        def body(index, total):
            here = token_block(index, block)
            act = dot(normed[here, :], up_w[...]) + bias[pl.ds(step, 1), :]
            g_gelu = dot(cotangent[here, :], down_w[...], NT)
            below = 0.5 * (1.0 + lax.erf(act * 0.7071067811865476))
            density = 0.3989422804014327 * jnp.exp(-0.5 * act * act)
            low = (act * below).astype(BF16)
            grad = (g_gelu * (below + act * density)).astype(BF16)
            gelu_act[here, :] = low
            g_up[here, :] = grad
            down_sum[here, :] += dot(low, down_w[...])
            g_normed[here, :] += dot(grad, up_w[...], NT)
            return total + column_sum(grad)

        g_up_b[...] = lax.fori_loop(0, count, body, jnp.zeros(g_up_b.shape, F32))
        put(0, dot(g_up[...], normed[...], TN))
        put(1, dot(cotangent[...], gelu_act[...], TN))

    @pl.when(step == last)
    def _():
        def body(index, sums):
            here = token_block(index, block)
            total = resid[here, :]
            result[here, :] = (total + (down_sum[here, :] + row_of(down_b))).astype(BF16)
            scaled, inverse = normalize(total)
            grad = g_normed[here, :]
            inner = grad * row_of(gain)
            g_out = cotangent[here, :].astype(F32)
            g_total = g_out + inverse * (
                inner
                - jnp.mean(inner, -1, keepdims=True)
                - scaled * jnp.mean(inner * scaled, -1, keepdims=True)
            )
            g_resid[here, :] = g_total
            low = g_total.astype(BF16)
            g_branch[here, :] = low
            g_attended[:, here] = dot(out_w[...], low, NT).astype(BF16)
            parts = (grad * scaled, grad, low, g_out)
            return tuple(old + column_sum(new) for old, new in zip(sums, parts))

        empty = jnp.zeros((1, width), F32)
        sums = lax.fori_loop(0, count, body, (empty,) * 4)
        for index, at, here in head_rows(out_groups):
            sent_grads[index][at] = g_attended[here, :]
        for index, total in enumerate(sums):
            vectors[index : index + 1, :] = total
        put(0, dot(g_branch[...], attended[...], (((0,), (1,)), ((), ()))))
        put(1, jnp.zeros((width, width), F32))


def mlp(place, groups, gathered, tokens, rows, cotangent, out_w, out_b, gain, shift, up_w, up_b, down_w, down_b):
    tok_here, width = tokens.shape
    hidden_units = up_w.shape[1]
    sources = len(gathered[0])
    pieces = [part for group in gathered for part in group]
    depth = pieces[0].shape[1]
    shapes = [(len(group), depth, tok_here) for group in groups[1] for _ in range(sources)]
    steps = hidden_units // width
    slots = pl.BlockSpec((2, width, width // 2), lambda j, b: (j, 0, 0))
    at = lambda j: jnp.minimum(j, steps - 1)
    slot_shape = jax.ShapeDtypeStruct((2 * steps + 2, width, width // 2), BF16)
    out = pl.pallas_call(
        partial(mlp_kernel, groups=groups, sources=sources, block=tok_here // 2),
        grid_spec=pltpu.PrefetchScalarGridSpec(
            num_scalar_prefetch=1,
            grid=(steps + 1,),
            in_specs=[whole(*part.shape) for part in pieces]
            + [
                whole(tok_here, width),
                whole(2, width),
                whole(tok_here, width),
                whole(width, width),
                whole(width),
                whole(width),
                whole(width),
                pl.BlockSpec((width, width), lambda j, b: (0, at(j))),
                whole(hidden_units),
                pl.BlockSpec((width, width), lambda j, b: (at(j), 0)),
                whole(width),
            ],
            out_specs=[whole(tok_here, width)] * 2
            + [whole(*shape) for shape in shapes]
            + [slots, slots, whole(4, width), pl.BlockSpec((1, width), lambda j, b: (0, at(j)))],
            scratch_shapes=[
                pltpu.VMEM((width, tok_here), BF16),
                pltpu.VMEM((tok_here, width), BF16),
                pltpu.VMEM((tok_here, width), F32),
                pltpu.VMEM((tok_here, width), BF16),
                pltpu.VMEM((tok_here, width), BF16),
                pltpu.VMEM((tok_here, width), F32),
                pltpu.VMEM((tok_here, width), F32),
                pltpu.VMEM((tok_here, width), BF16),
                pltpu.VMEM((width, tok_here), BF16),
                pltpu.VMEM((steps, width), F32),
            ],
        ),
        out_shape=[
            jax.ShapeDtypeStruct((tok_here, width), BF16),
            jax.ShapeDtypeStruct((tok_here, width), F32),
        ]
        + [jax.ShapeDtypeStruct(shape, BF16) for shape in shapes]
        + [
            slot_shape,
            slot_shape,
            jax.ShapeDtypeStruct((4, width), F32),
            jax.ShapeDtypeStruct((1, hidden_units), F32),
        ],
        compiler_params=pltpu.CompilerParams(vmem_limit_bytes=VMEM),
        cost_estimate=pl.CostEstimate(
            flops=12 * tok_here * up_w.size, transcendentals=0, bytes_accessed=8 * up_w.size
        ),
        name="mlp",
    )(place, *pieces, tokens, rows, cotangent, out_w, out_b, gain, shift, up_w, up_b, down_w, down_b)
    grads = out[2 : 2 + len(shapes)]
    grads = [grads[g * sources : (g + 1) * sources] for g in range(len(groups[1]))]
    return out[0], out[1], grads, out[-4:]


def unproject(scalars, back, weight, packed, bias, chosen, rounds, sources):
    step = pl.program_id(0)
    size = len(chosen) * HEAD_DIM
    for index, part in enumerate(back):
        group, j = divmod(index, sources)
        at = (scalars[0] ^ j) * size + group * HEAD_DIM
        packed[pl.ds(pl.multiple_of(at, HEAD_DIM), HEAD_DIM), :] = part[0]
    columns = [(source * rounds + chosen[0]) * HEAD_DIM for source in range(sources)]
    ones = jnp.ones((8, packed.shape[1]), BF16)
    found = dot(ones, packed[...], NT)[0:1]

    @pl.when(step == 0)
    def _():
        bias[...] = jnp.zeros_like(bias)

    for part in range(3):

        @pl.when(step == part)
        def _():
            for source, start in enumerate(columns):
                here = found[:, source * size : (source + 1) * size]
                bias[part : part + 1, start : start + size] = here

    picked = jnp.concatenate([weight[:, start : start + size] for start in columns], 1)
    return dot(packed[...], picked, (((0,), (1,)), ((), ())))


def begin_kernel(scalars, *refs, chosen, rounds, sources):
    back, (weight, g_normed, bias, packed) = refs[:-4], refs[-4:]
    added = unproject(scalars, back, weight, packed, bias, chosen, rounds, sources)

    @pl.when(pl.program_id(0) == 0)
    def _():
        g_normed[...] = added

    @pl.when(pl.program_id(0) > 0)
    def _():
        g_normed[...] += added


def finish_kernel(scalars, *refs, chosen, rounds, sources, block):
    pieces = len(chosen) * sources
    back, refs = refs[:pieces], refs[pieces:]
    weight, tokens, rows, gain, g_resid, vectors, g_up_b, g_before, bias_before = refs[:9]
    g_tokens, sums, g_normed, packed, bias = refs[9:]
    step, last = pl.program_id(0), pl.num_programs(0) - 1
    added = unproject(scalars, back, weight, packed, bias, chosen, rounds, sources)

    @pl.when(step == 0)
    def _():
        g_normed[...] = g_before[...] + added

    @pl.when(step > 0)
    def _():
        g_normed[...] += added

    @pl.when(step == last)
    def _():
        width = tokens.shape[1]
        count = tokens.shape[0] // block
        empty = jnp.zeros((1, width), F32)

        def half(first):
            def body(index, totals):
                here = token_block(index + first * (count // 2), block)
                scaled, inverse = normalize(tokens[here, :].astype(F32) + rows[first : first + 1, :])
                grad = g_normed[here, :]
                inner = grad * row_of(gain)
                g_hidden = g_resid[here, :] + inverse * (
                    inner
                    - jnp.mean(inner, -1, keepdims=True)
                    - scaled * jnp.mean(inner * scaled, -1, keepdims=True)
                )
                g_tokens[here, :] = g_hidden.astype(BF16)
                parts = (grad * scaled, grad, g_hidden)
                return tuple(old + column_sum(new) for old, new in zip(totals, parts))

            return lax.fori_loop(0, count // 2, body, (empty,) * 3)

        one, two = half(0), half(1)
        sums[0:1, :], sums[1:2, :] = one[0] + two[0], one[1] + two[1]
        sums[2:6, :] = vectors[...]
        for index in range(4):
            sums[6 + index : 7 + index, :] = g_up_b[:, index * width : (index + 1) * width]
        lane = lax.broadcasted_iota(jnp.int32, (1, width), 1)
        is_short = scalars[1] != 0
        sums[10:13, :] = bias_before[...] + bias[...]
        pick = lambda at, other: jnp.where(lane == at, scalars[2 + at].astype(F32), other)
        sums[13:14, :] = jnp.where(scalars[0] == 0, pick(0, pick(1, 0.0)), 0.0)
        sums[14:15, :] = jnp.where(is_short, one[2], one[2] + two[2])
        sums[15:16, :] = jnp.where(is_short, two[2], 0.0)


def back_specs(back, width):
    block = pl.BlockSpec((1,) + back[0].shape[1:], lambda i, p: (i, 0, 0))
    return [block] * len(back) + [pl.BlockSpec((width, width), lambda i, p: (0, i))]


def begin_finish(scalars, back, chosen, weight, rounds):
    sources = len(back[0])
    pieces = [part for group in back for part in group]
    width, tok_here = weight.shape[0], pieces[0].shape[2]
    return pl.pallas_call(
        partial(begin_kernel, chosen=chosen, rounds=rounds, sources=sources),
        grid_spec=pltpu.PrefetchScalarGridSpec(
            num_scalar_prefetch=1,
            grid=(3,),
            in_specs=back_specs(pieces, width),
            out_specs=[whole(tok_here, width), whole(3, width)],
            scratch_shapes=[pltpu.VMEM((sources * len(chosen) * HEAD_DIM, tok_here), BF16)],
        ),
        out_shape=[
            jax.ShapeDtypeStruct((tok_here, width), F32),
            jax.ShapeDtypeStruct((3, width), F32),
        ],
        compiler_params=pltpu.CompilerParams(vmem_limit_bytes=VMEM),
        cost_estimate=pl.CostEstimate(
            flops=2 * tok_here * weight.size, transcendentals=0, bytes_accessed=4 * weight.size
        ),
        name="begin_finish",
    )(scalars, *pieces, weight)


def finish(scalars, back, chosen, weight, tokens, rows, gain, g_resid, vectors, g_up_b, before, rounds):
    tok_here, width = tokens.shape
    sources = len(back[0])
    pieces = [part for group in back for part in group]
    return pl.pallas_call(
        partial(finish_kernel, chosen=chosen, rounds=rounds, sources=sources, block=tok_here // 4),
        grid_spec=pltpu.PrefetchScalarGridSpec(
            num_scalar_prefetch=1,
            grid=(3,),
            in_specs=back_specs(pieces, width)
            + [
                whole(tok_here, width),
                whole(2, width),
                whole(width),
                whole(tok_here, width),
                whole(*vectors.shape),
                whole(*g_up_b.shape),
                whole(tok_here, width),
                whole(3, width),
            ],
            out_specs=[whole(tok_here, width), whole(16, width)],
            scratch_shapes=[
                pltpu.VMEM((tok_here, width), F32),
                pltpu.VMEM((sources * len(chosen) * HEAD_DIM, tok_here), BF16),
                pltpu.VMEM((3, width), F32),
            ],
        ),
        out_shape=[
            jax.ShapeDtypeStruct((tok_here, width), BF16),
            jax.ShapeDtypeStruct((16, width), F32),
        ],
        compiler_params=pltpu.CompilerParams(vmem_limit_bytes=VMEM),
        cost_estimate=pl.CostEstimate(
            flops=2 * tok_here * weight.size, transcendentals=0, bytes_accessed=8 * weight.size
        ),
        name="finish",
    )(scalars, *pieces, weight, tokens, rows, gain, g_resid, vectors, g_up_b, *before)


def qkv_grad_kernel(block_ref, *refs, rounds, sources, order):
    grads, refs = refs[: rounds * sources], refs[rounds * sources :]
    normed, (first, second, store) = refs[:sources], refs[sources:]
    size = 3 * HEAD_DIM
    for r in range(rounds):
        total = None
        for grad, part in zip(grads[r * sources : (r + 1) * sources], normed):
            here = jnp.concatenate([grad[p] for p in range(3)], 0)
            term = dot(here, part[...])
            total = term if total is None else total + term
        store[:, r * size : (r + 1) * size] = total.T.astype(BF16)
    half = len(order) // 2
    rows = first.shape[1]
    for at, index in enumerate(order):
        start = (block_ref[0] ^ index) * rows
        here = pl.ds(pl.multiple_of(start, rows), rows) if half > 1 else slice(at * rows, (at + 1) * rows)
        (second if at >= half else first)[at % half] = store[here, :]


def qkv_grad(block, grads, normed, order):
    rounds, sources = len(grads), len(normed)
    tok_here, width = normed[0].shape
    size = 3 * HEAD_DIM * rounds
    pieces = [part for group in grads for part in group]
    half = (len(order) // 2, width // len(order), size)
    return pl.pallas_call(
        partial(qkv_grad_kernel, rounds=rounds, sources=sources, order=order),
        grid_spec=pltpu.PrefetchScalarGridSpec(
            num_scalar_prefetch=1,
            grid=(1,),
            in_specs=[whole(*pieces[0].shape)] * len(pieces) + [whole(tok_here, width)] * sources,
            out_specs=[whole(*half)] * 2,
            scratch_shapes=[pltpu.VMEM((width, size), BF16)],
        ),
        out_shape=[jax.ShapeDtypeStruct(half, BF16)] * 2,
        compiler_params=pltpu.CompilerParams(vmem_limit_bytes=VMEM),
        cost_estimate=pl.CostEstimate(
            flops=8 * tok_here * width * size, transcendentals=0, bytes_accessed=12 * tok_here * width
        ),
        name="qkv_grad",
    )(block, *pieces, *normed)


def swap(values, axis, bit):
    size = lax.axis_size(axis)
    return lax.ppermute(values, axis, [(j, j ^ bit) for j in range(size)])


def trade(parts, axis):
    return [parts[0]] + [swap(part, axis, i) for i, part in enumerate(parts) if i]


def spread(values, axis, count):
    return [values] + [swap(values, axis, i) for i in range(1, count)]


def total_of(parts):
    total = parts[0].astype(F32)
    for part in parts[1:]:
        total = total + part.astype(F32)
    return total


def after(values, *others):
    return lax.optimization_barrier((values, *others))[0]


def deal_kernel(bits_ref, *refs, steps):
    keep, got, (outgoing, staying) = refs[: steps + 2], refs[steps + 2 : 2 * steps + 4], refs[-2:]
    gate = bits_ref[0]
    for out, side in ((outgoing, 1 - gate), (staying, gate)):
        at = 0
        for left, right in zip(keep, got):
            rows = left.shape[2] // 2
            here = pl.ds(pl.multiple_of(side * rows, rows), rows)
            for index in range(2):
                total = left[0, index, here, :].astype(F32) + right[0, index, here, :].astype(F32)
                out[index, at : at + rows, :] = total.astype(BF16)
            at += rows


def deal(gate, keep, got, dp):
    slots, width, lanes = keep.shape
    steps = slots // 2 - 1
    up_each, each = width * steps // dp, width // dp
    per_slot = width // up_each
    up = pl.BlockSpec(
        (1, 2, up_each, lanes),
        lambda i, b: (2 * lax.div(2 * i, per_slot), lax.rem(i, per_slot // 2), 0, 0),
    )
    rest = [
        pl.BlockSpec((1, 2, each, lanes), lambda i, b, slot=slot: (slot, i, 0, 0))
        for slot in [2 * k + 1 for k in range(steps)] + [2 * steps]
    ]
    views = lambda array: [array.reshape(slots, per_slot, up_each, lanes)] + [
        array.reshape(slots, dp, each, lanes)
    ] * (steps + 1)
    rows = up_each // 2 + (steps + 1) * each // 2
    shape = jax.ShapeDtypeStruct((dp, rows, lanes), BF16)
    return pl.pallas_call(
        partial(deal_kernel, steps=steps),
        grid_spec=pltpu.PrefetchScalarGridSpec(
            num_scalar_prefetch=1,
            grid=(dp // 2,),
            in_specs=([up] + rest) * 2,
            out_specs=[pl.BlockSpec((2, rows, lanes), lambda i, b: (i, 0, 0))] * 2,
        ),
        out_shape=[shape, shape],
        cost_estimate=pl.CostEstimate(flops=keep.size, transcendentals=0, bytes_accessed=6 * keep.size),
        name="deal",
    )(gate, *views(keep), *views(got))


def undeal_kernel(place_ref, *refs, sources, steps, each):
    shares, (up, down, out, store) = refs[:sources], refs[sources:]
    lanes = store.shape[2]
    for j, share in enumerate(shares):
        store[place_ref[0] ^ j] = share[...].astype(F32)
    wide = steps * each
    for low in range(2):
        both = lambda at, size: jnp.concatenate([store[low, at : at + size], store[2 + low, at : at + size]], 0).T
        up[low * lanes : (low + 1) * lanes, :] = both(0, wide)
        for half in range(2):
            here = slice(half * each, (half + 1) * each)
            share = store.at[2 * half + low]
            for k in range(steps):
                at, row = (2 * k + low) * lanes, wide + k * each
                down[here, at : at + lanes] = share[row : row + each]
            out[here, low * lanes : (low + 1) * lanes] = share[2 * wide : 2 * wide + each]


def undeal(place, shares, steps, width, dp):
    rows, lanes = shares[0].shape
    shapes = [(width, width * steps // dp), (width // dp, width * steps), (width // dp, width)]
    up, down, out = pl.pallas_call(
        partial(undeal_kernel, sources=len(shares), steps=steps, each=width // dp // 2),
        grid_spec=pltpu.PrefetchScalarGridSpec(
            num_scalar_prefetch=1,
            grid=(1,),
            in_specs=[whole(rows, lanes)] * len(shares),
            out_specs=[whole(*shape) for shape in shapes],
            scratch_shapes=[pltpu.VMEM((len(shares), rows, lanes), F32)],
        ),
        out_shape=[jax.ShapeDtypeStruct(shape, F32) for shape in shapes],
        cost_estimate=pl.CostEstimate(flops=0, transcendentals=0, bytes_accessed=24 * rows * lanes),
        name="undeal",
    )(place, *shares)
    return up, down.T, out.T


def turn_kernel(*refs):
    *parts, out = refs
    out[...] = total_of([part[0] for part in parts]).T.astype(BF16)


def turn(parts):
    _, rows, columns = parts[0].shape
    return pl.pallas_call(
        turn_kernel, out_shape=jax.ShapeDtypeStruct((columns, rows), BF16), name="turn"
    )(*parts)


def regroup_kernel(place_ref, *refs, rounds):
    *shares, out = refs
    sources = len(shares)
    for j, share in enumerate(shares):
        for r in range(rounds):
            for p in range(3):
                at = ((p * sources + (place_ref[0] ^ j)) * rounds + r) * HEAD_DIM
                start = (r * 3 + p) * HEAD_DIM
                out[pl.ds(pl.multiple_of(at, HEAD_DIM), HEAD_DIM), :] = share[start : start + HEAD_DIM]


def regroup(place, shares, rounds):
    columns, rows = shares[0].shape
    total = columns * len(shares)
    return pl.pallas_call(
        partial(regroup_kernel, rounds=rounds),
        grid_spec=pltpu.PrefetchScalarGridSpec(
            num_scalar_prefetch=1,
            grid=(1,),
            in_specs=[whole(columns, rows)] * len(shares),
            out_specs=whole(total, rows),
        ),
        out_shape=jax.ShapeDtypeStruct((total, rows), BF16),
        name="regroup",
    )(place, *shares)


def stack_kernel(parts, out):
    both = [parts[index].astype(F32) for index in range(parts.shape[0])]
    out[...] = jnp.concatenate(both, 1)


def stack_rows(parts):
    count, columns, rows = parts.shape
    return pl.pallas_call(
        stack_kernel, out_shape=jax.ShapeDtypeStruct((columns, rows * count), F32), name="stack_rows"
    )(parts).T


def exchange(values, axis):
    return lax.all_to_all(values, axis, split_axis=0, concat_axis=0, tiled=True)


def wide_sums(slots, place, dp):
    steps, width, lanes = slots.shape[0] // 2 - 1, slots.shape[1], slots.shape[2]
    pairs = slots.reshape(steps + 1, 2, width, lanes)
    up = pairs[:steps, 0].reshape(dp, 2, -1, lanes)
    down = pairs[:steps, 1].reshape(steps, dp, 2, -1, lanes)
    down = jnp.moveaxis(down, 0, 2).reshape(dp, 2, -1, lanes)
    out = pairs[steps, 0].reshape(dp, 2, -1, lanes)
    dealt = jnp.concatenate([up, down, out], 2)
    gate = place // 2
    pick = lambda index: lax.dynamic_index_in_dim(dealt, index, 1, keepdims=False)
    half_sum = total_of([pick(gate), swap(pick(1 - gate), "seq", 2)]).astype(BF16)
    share = jnp.sum(exchange(half_sum, "dp").astype(F32), 0).astype(BF16)
    shares = lax.all_gather(share, "seq", axis=0).reshape(2, 2, -1, lanes).astype(F32)
    each = width // dp // 2
    up, down, out = jnp.split(shares, [steps * each, 2 * steps * each], 2)
    turned = lambda part: jnp.transpose(part, (1, 3, 0, 2)).reshape(2 * lanes, -1)
    down = down.reshape(2, 2, steps, each, lanes)
    down = jnp.transpose(down, (2, 1, 4, 0, 3)).reshape(steps * 2 * lanes, 2 * each)
    return turned(up), down, turned(out)


def wide_columns(grads, dp, sources, rounds):
    grad = jnp.concatenate(grads, 2).reshape(-1, 3 * HEAD_DIM * rounds)
    width, columns = grad.shape
    rows = width // dp
    summed = jnp.sum(exchange(grad.reshape(dp, rows, columns), "dp").astype(F32), 0).astype(BF16)
    gathered = lax.all_gather(summed, "seq", axis=0).reshape(sources, rows, rounds, 3, HEAD_DIM)
    ordered = jnp.transpose(gathered, (1, 3, 0, 2, 4)).reshape(rows, dp, -1)
    return exchange(jnp.swapaxes(ordered, 0, 1), "dp").reshape(width, -1).astype(F32)


def on_device(
    tokens,
    time_steps,
    data_group,
    cotangent,
    attn_norm_gain,
    attn_norm_bias,
    qkv_weight,
    query_bias,
    value_bias,
    out_weight,
    out_bias,
    mlp_norm_gain,
    mlp_norm_bias,
    up_weight,
    up_bias,
    down_weight,
    down_bias,
    time_table,
):
    sources, dp = lax.axis_size("seq"), lax.axis_size("dp")
    place, block = lax.axis_index("seq"), lax.axis_index("dp")
    tokens, cotangent = tokens[0], cotangent[0]
    tok_here, width = tokens.shape
    hidden_units = up_weight.shape[1]
    rounds = HEADS // sources
    is_short = data_group[0] == 0
    short_flag = is_short.astype(jnp.int32)[None]
    place_arg = place.astype(jnp.int32)[None]
    block_arg = block.astype(jnp.int32)[None]
    few = dp <= 8
    row_steps = jnp.where(is_short, time_steps[0], time_steps[0, 0])
    scalars = jnp.concatenate([place_arg, short_flag, lax.div(row_steps, 8), lax.rem(row_steps, 8)])

    normed, rows, sending = project(
        scalars,
        tokens,
        time_table,
        attn_norm_gain,
        attn_norm_bias,
        qkv_weight,
        query_bias,
        value_bias,
        sources,
        rounds,
    )
    heads, saved, sent = [trade(sending[0], "seq")], [], []
    returned = []
    for r in range(rounds):
        if r + 1 < rounds:
            ahead = sending[r + 1] if r < 1 else after(sending[r + 1], saved[r - 1][1])
            heads.append(trade(ahead, "seq"))
        ready = after(heads[r], saved[r - 1][1]) if r else heads[r]
        out, kept = attend(short_flag, ready, sent[0] if r == 1 else ())
        saved.append(kept)
        sent.append(out)
        if r >= 1:
            returned.append(trade(after(out, *returned[-1]) if returned else out, "seq"))

    beside = swap(after(normed, saved[1][1]), "seq", 1)
    across = swap(after(normed, *returned[-1]), "seq", 2)
    groups = (((0, 1), (2,)), ((0,), (1, 2)))
    result, g_resid, sent_grads, (send, keep, vectors, g_up_b) = mlp(
        place_arg,
        groups,
        returned,
        after(tokens, beside),
        rows,
        cotangent,
        out_weight,
        out_bias,
        mlp_norm_gain,
        mlp_norm_bias,
        up_weight,
        up_bias,
        down_weight,
        down_bias,
    )
    send, *sent_grads = after((send, *sent_grads), across)
    got = swap(send, "seq", 1)
    first_grads = trade(sent_grads[0], "seq")
    if few:
        outgoing, staying = deal(place_arg // 2, keep, got, dp)
        got = swap(outgoing, "seq", 2)
        ready = outgoing
    else:
        ready = summed = total_of([keep, got]).astype(BF16)
    rest_grads = trade(after(sent_grads[1], *first_grads), "seq")
    beside = [normed, beside, across, swap(across, "seq", 1)]
    grads = [attend_back(short_flag, after(heads[0], ready, beside[3]), saved[0], first_grads, 0)]
    back = [trade(grads[0], "seq")]
    held = after(heads[1], *grads[0])
    grads.append(attend_back(short_flag, held, saved[1], rest_grads, 0))
    back.append(trade(grads[1], "seq"))
    order = (0, 4, 2, 6, 1, 5, 3, 7) if few else (0, 1)
    stay_a, away_a = qkv_grad(block_arg, grads, beside, order)
    if few:
        got_a = swap(away_a, "dp", 1)
        half_sum = total_of([staying, after(got, grads[1])]).astype(BF16)
        dealt = exchange(half_sum, "dp")
        ready = half_sum
    held = after(heads[2], stay_a, ready, *back[0])
    grads.append(attend_back(short_flag, held, saved[2], rest_grads, 1))
    back.append(trade(grads[2], "seq"))
    grads[2] = after(grads[2], *back[1])
    stay_b, away_b = qkv_grad(block_arg, grads[2:], beside, order)
    earlier = [after(parts, stay_b) for parts in back[:2]]
    before = begin_finish(scalars, earlier, (0, 1), qkv_weight, rounds)
    ready = before[1]
    if few:
        kept, got = [stay_a, stay_b], [after(got_a, grads[2]), swap(away_b, "dp", 1)]
        part = jnp.concatenate([total_of(pair).astype(BF16) for pair in zip(kept, got)], 2)
        ready = part
        sums = [part[:1]] + [swap(part[at : at + 1], "dp", bit) for at, bit in ((1, 4), (2, 2), (3, 6))]

    steps_arg = time_steps[0].astype(jnp.int32)
    flags = jnp.concatenate([place_arg, short_flag, steps_arg])
    g_tokens, small = finish(
        flags,
        after(back[2:], ready),
        (2,),
        qkv_weight,
        tokens,
        rows,
        attn_norm_gain,
        g_resid,
        vectors,
        g_up_b,
        before,
        rounds,
    )
    if few:
        small_parts = spread(small, "seq", sources)
        summed = turn(after(sums, small))
        share = total_of([after(dealt, summed)[i] for i in range(dp)]).astype(BF16)
        columns = regroup(place_arg, after(spread(summed, "seq", sources), share), rounds)
        small = total_of(after(small_parts, summed))
        share_across = swap(share, "seq", 2)
        shares = [share, swap(share, "seq", 1), share_across, swap(share_across, "seq", 1)]
    else:
        small = total_of(spread(small, "seq", sources))
    if few:
        own, other = small, swap(small, "dp", 1)
        small = jnp.concatenate([own[:13] + other[:13], own[13:], other[13:]])
        all_small = jnp.stack([small] + [swap(small, "dp", bit) for bit in (2, 4, 6)])
        small = jnp.sum(all_small[:, :13], 0)
        by_block = all_small[:, 13:].reshape(dp, 3, width)
    else:
        slots = jnp.where((jnp.arange(dp) == block)[:, None, None], small[None, 13:], 0.0)
        small = jnp.concatenate([small[:13], slots.reshape(-1, width)])
        bit = 1
        while bit < dp:
            small = small + swap(small, "dp", bit)
            bit *= 2
        by_block = small[13:].reshape(dp, 3, width)
    steps = by_block[:, 0, :2].reshape(1, -1).astype(jnp.int32)
    all_rows = by_block[:, 1:].reshape(-1, width)
    if few:
        sum_up, sum_down, sum_out = undeal(place_arg, shares, hidden_units // width, width, dp)
        sum_qkv = stack_rows(exchange(columns.reshape(dp, 3 * width // dp, width // dp), "dp"))
    else:
        sum_up, sum_down, sum_out = wide_sums(summed, place, dp)
        sum_qkv = wide_columns(
            [jnp.stack(pair).reshape(2, width // 2, -1) for pair in ((stay_a, away_a), (stay_b, away_b))],
            dp,
            sources,
            rounds,
        )
    share_cols = width // dp
    rows_mine = lax.dynamic_slice_in_dim(all_rows, block * share_cols, share_cols, 1)
    table_rows = time_table.shape[0]
    hits = jnp.arange(table_rows, dtype=jnp.int32)[:, None] == steps
    sum_table = jnp.dot(hits.astype(F32), rows_mine, precision=lax.Precision.HIGHEST)
    return (
        result[None],
        g_tokens[None],
        small[0],
        small[1],
        sum_qkv,
        small[10],
        small[12],
        sum_out,
        small[4],
        small[2],
        small[3],
        sum_up,
        small[6:10].reshape(-1),
        sum_down,
        small[5],
        sum_table,
    )


def solution(mesh):
    placed = (P("dp", "seq", None), P("dp", None), P("dp"), P("dp", "seq", None)) + (P(),) * 14
    column = P(None, "dp")
    return jax.shard_map(
        on_device,
        mesh=mesh,
        in_specs=placed,
        out_specs=(
            P("dp", "seq", None),
            P("dp", "seq", None),
            P(),
            P(),
            column,
            P(),
            P(),
            column,
            P(),
            P(),
            P(),
            column,
            P(),
            column,
            P(),
            column,
        ),
        check_vma=False,
    )
```

```python
from functools import partial

import jax
import jax.numpy as jnp
from jax import lax
from jax.experimental import pallas as pl
from jax.experimental.pallas import tpu as pltpu
from jax.sharding import PartitionSpec as P

HEADS = 12
HEAD_DIM = 64
EPSILON = 1e-05
LOG2E = 1.4426950408889634
SCALE = HEAD_DIM**-0.5
BF16 = jnp.bfloat16
F32 = jnp.float32
NN = (((1,), (0,)), ((), ()))
NT = (((1,), (1,)), ((), ()))
TN = (((0,), (0,)), ((), ()))
VMEM = 62 << 20
SMALL_VMEM = 40 << 20


def dot(left, right, dims=NN):
    return lax.dot_general(left, right, dims, preferred_element_type=F32)


def split_low(values, count):
    parts = []
    for _ in range(count):
        term = values.astype(BF16)
        parts.append(term)
        values = values - term.astype(F32)
    return parts


def whole(*shape):
    return pl.BlockSpec(shape, lambda *_: (0,) * len(shape))


def halves(sources, segment):
    for chunk in range(2 * sources):
        source, part = divmod(chunk, 2)
        yield chunk, source, slice(part * segment, (part + 1) * segment)


def over_chunks(short_ref, chunks, body):
    is_short = short_ref[0] != 0
    part = lax.rem(pl.program_id(0), 2)

    @pl.when(is_short)
    def _():
        body([2 * k + part for k in range(chunks // 2)], True)

    @pl.when(jnp.logical_not(is_short))
    def _():
        body(list(range(chunks)), True)


def attend_kernel(short_ref, *refs, sources, segment, held):
    heads, refs = refs[:sources], refs[sources:]
    earlier, refs = refs[: sources * held], refs[sources * held :]
    sent, refs = refs[:sources], refs[sources:]
    mixed_ref, inverse_ref, weights_ref, queries, keys, values, sums, bounded = refs
    step = pl.program_id(0)
    chunks = 2 * sources
    depth = HEAD_DIM

    @pl.when(step == 0)
    def _():
        for old, new in zip(earlier, sent):
            new[0] = old[0]
        longest = [jnp.zeros((1, segment), F32)] * 2
        for chunk, source, cols in halves(sources, segment):
            scaled = heads[source][0, :, cols].astype(F32) * (SCALE * LOG2E)
            high, low = split_low(scaled, 2)
            queries[chunk, 0:64, :] = high
            queries[chunk, 64:128, :] = low
            queries[chunk, 128:144, :] = jnp.zeros((16, segment), BF16)
            key = heads[source][1, :, cols]
            keys[chunk, 0:64, :] = key
            keys[chunk, 64:128, :] = key
            keys[chunk, 128:144, :] = jnp.full((16, segment), -1.0, BF16)
            values[chunk, 0:64, :] = heads[source][2, :, cols]
            values[chunk, 64:80, :] = jnp.ones((16, segment), BF16)
            sizes = [jnp.sum(x * x, 0, keepdims=True) for x in (scaled, key.astype(F32))]
            longest = [jnp.maximum(old, new) for old, new in zip(longest, sizes)]
        bound = jnp.max(longest[0]) * jnp.max(longest[1])
        bounded[0] = (bound <= 3600.0).astype(jnp.int32)

    @pl.when(bounded[0] == 0)
    def _():
        query = queries[step][0:128]
        is_short = (short_ref[0] != 0).astype(jnp.int32)

        def body(index, peak):
            chunk = jnp.where(is_short != 0, 2 * index + lax.rem(step, 2), index)
            scores = dot(keys[chunk][0:128], query, TN)
            return jnp.maximum(peak, jnp.max(scores, 0, keepdims=True))

        start = jnp.full((1, segment), -jnp.inf, F32)
        peak = lax.fori_loop(0, jnp.where(is_short != 0, chunks // 2, chunks), body, start)
        zeros = jnp.zeros((13, segment), BF16)
        queries[step, 128:144, :] = jnp.concatenate(split_low(peak, 3) + [zeros], 0)

    def body(order, first):
        query = queries[step]
        total = None
        later = dot(keys[order[0]], query, TN)
        for index, chunk in enumerate(order):
            scores = later
            if index + 1 < len(order):
                later = dot(keys[order[index + 1]], query, TN)
            weights = jnp.exp2(scores).astype(BF16)
            weights_ref[0, chunk] = weights.T
            mixed = dot(values[chunk], weights)
            total = mixed if total is None else total + mixed
        sums[...] = total if first else sums[...] + total

    over_chunks(short_ref, chunks, body)
    total = sums[...]
    inverse = 1.0 / total[depth : depth + 1, :]
    result = total[:depth] * inverse
    mixed_ref[step] = result
    inverse_ref[step] = inverse
    for chunk, source, cols in halves(sources, segment):

        @pl.when(step == chunk)
        def _():
            sent[source][held, :, cols] = result.astype(BF16)


def attend(is_short, heads, earlier=()):
    sources = len(heads)
    _, depth, tokens = heads[0].shape
    segment, chunks = tokens // 2, 2 * sources
    work = (sources * tokens) ** 2
    held = len(earlier) // sources
    out = pl.pallas_call(
        partial(attend_kernel, sources=sources, segment=segment, held=held),
        grid_spec=pltpu.PrefetchScalarGridSpec(
            num_scalar_prefetch=1,
            grid=(chunks,),
            in_specs=[whole(3, depth, tokens)] * sources + [whole(1, depth, tokens)] * len(earlier),
            out_specs=[whole(1 + held, depth, tokens)] * sources
            + [
                whole(chunks, depth, segment),
                whole(chunks, 1, segment),
                pl.BlockSpec((1, chunks, segment, segment), lambda i, s: (i, 0, 0, 0)),
            ],
            scratch_shapes=[
                pltpu.VMEM((chunks, 144, segment), BF16),
                pltpu.VMEM((chunks, 144, segment), BF16),
                pltpu.VMEM((chunks, 80, segment), BF16),
                pltpu.VMEM((80, segment), F32),
                pltpu.SMEM((1,), jnp.int32),
            ],
        ),
        out_shape=[jax.ShapeDtypeStruct((1 + held, depth, tokens), BF16)] * sources
        + [
            jax.ShapeDtypeStruct((chunks, depth, segment), F32),
            jax.ShapeDtypeStruct((chunks, 1, segment), F32),
            jax.ShapeDtypeStruct((chunks, chunks, segment, segment), BF16),
        ],
        compiler_params=pltpu.CompilerParams(vmem_limit_bytes=SMALL_VMEM),
        cost_estimate=pl.CostEstimate(
            flops=16 * work * depth, transcendentals=work, bytes_accessed=2 * work
        ),
        name="attend",
    )(is_short, *heads, *earlier)
    return out[:sources], out[-3:]


def attend_back_kernel(short_ref, *refs, sources, segment):
    heads, grads, (mixed_ref, inverse_ref, weights_ref), refs = (
        refs[:sources],
        refs[sources : 2 * sources],
        refs[2 * sources : 2 * sources + 3],
        refs[2 * sources + 3 :],
    )
    outs, (queries, g_aug, v_aug, grad_q, grad_kv) = refs[:sources], refs[sources:]
    step = pl.program_id(0)
    chunks = 2 * sources

    @pl.when(step == 0)
    def _():
        zeros = jnp.zeros((13, segment), BF16)
        for chunk, source, cols in halves(sources, segment):
            queries[chunk] = heads[source][0, :, cols]
            grad = grads[source][0, :, cols].astype(F32) * inverse_ref[chunk]
            high, low = split_low(grad, 2)
            g_aug[chunk, 0:64, :] = high
            g_aug[chunk, 64:128, :] = low
            inner = jnp.sum(grad * mixed_ref[chunk], 0, keepdims=True)
            g_aug[chunk, 128:144, :] = jnp.concatenate(split_low(inner, 3) + [zeros], 0)
        grad_q[...] = jnp.zeros_like(grad_q)

    def column(index):
        for chunk, source, cols in halves(sources, segment):

            @pl.when(step == chunk)
            def _():
                index(source, cols)

    def load(source, cols):
        value = heads[source][2, :, cols]
        v_aug[0:64, :] = value
        v_aug[64:128, :] = value
        v_aug[128:144, :] = jnp.full((16, segment), -1.0, BF16)
        v_aug[144:208, :] = heads[source][1, :, cols]

    column(load)
    value = v_aug[0:144]
    turned = v_aug[144:208].T

    def body(order, first):
        key_total = value_total = None
        later = dot(g_aug[order[0]], value, TN)
        for index, chunk in enumerate(order):
            slopes = later
            if index + 1 < len(order):
                later = dot(g_aug[order[index + 1]], value, TN)
            weights = weights_ref[chunk, 0]
            g_scores = (weights.astype(F32) * slopes).astype(BF16)
            value_part = dot(g_aug[chunk, 0:128, :], weights)
            key_part = dot(queries[chunk], g_scores)
            value_total = value_part if value_total is None else value_total + value_part
            key_total = key_part if key_total is None else key_total + key_part
            grad_q[chunk] += dot(g_scores, turned)
        both = jnp.concatenate([key_total, value_total[0:64] + value_total[64:128]], 0)
        grad_kv[...] = both if first else grad_kv[...] + both

    over_chunks(short_ref, chunks, body)

    def save(source, cols):
        outs[source][1, :, cols] = (grad_kv[0:64] * SCALE).astype(BF16)
        outs[source][2, :, cols] = grad_kv[64:128].astype(BF16)

    column(save)

    @pl.when(step == chunks - 1)
    def _():
        for chunk, source, cols in halves(sources, segment):
            outs[source][0, :, cols] = (grad_q[chunk] * SCALE).T.astype(BF16)


def attend_back(is_short, heads, saved, grads, at):
    sources = len(heads)
    _, depth, tokens = heads[0].shape
    segment, chunks = tokens // 2, 2 * sources
    work = (sources * tokens) ** 2
    return pl.pallas_call(
        partial(attend_back_kernel, sources=sources, segment=segment),
        grid_spec=pltpu.PrefetchScalarGridSpec(
            num_scalar_prefetch=1,
            grid=(chunks,),
            in_specs=[whole(3, depth, tokens)] * sources
            + [pl.BlockSpec((1, depth, tokens), lambda i, s: (at, 0, 0))] * sources
            + [
                whole(chunks, depth, segment),
                whole(chunks, 1, segment),
                pl.BlockSpec((chunks, 1, segment, segment), lambda i, s: (0, i, 0, 0)),
            ],
            out_specs=[whole(3, depth, tokens)] * sources,
            scratch_shapes=[
                pltpu.VMEM((chunks, 64, segment), BF16),
                pltpu.VMEM((chunks, 144, segment), BF16),
                pltpu.VMEM((208, segment), BF16),
                pltpu.VMEM((chunks, segment, depth), F32),
                pltpu.VMEM((2 * depth, segment), F32),
            ],
        ),
        out_shape=[jax.ShapeDtypeStruct((3, depth, tokens), BF16)] * sources,
        compiler_params=pltpu.CompilerParams(vmem_limit_bytes=VMEM),
        cost_estimate=pl.CostEstimate(
            flops=40 * work * depth, transcendentals=work, bytes_accessed=2 * work
        ),
        name="attend_back",
    )(is_short, *heads, *grads, *saved)


def normalize(hidden):
    center = hidden - jnp.mean(hidden, -1, keepdims=True)
    spread = jnp.mean(center * center, -1, keepdims=True)
    inverse = lax.rsqrt(spread + EPSILON)
    return center * inverse, inverse


def token_block(index, size):
    return pl.ds(pl.multiple_of(index * size, size), size)


def column_sum(values):
    return jnp.sum(values.astype(F32), 0, keepdims=True)


def row_of(vector):
    return vector[...].astype(F32)[None, :]


def project_kernel(
    scalars, tokens, first_rows, second_rows, gain, shift, weight, query_bias, value_bias, normed, rows, *refs,
    sources, rounds, block
):
    outs, turned, column = refs[:-2], refs[-2], refs[-1]
    step = pl.program_id(0)
    pairs = sources // 2
    count = tokens.shape[0] // block
    size = column.shape[1]

    @pl.when(step == 0)
    def _():
        for index, group in enumerate((first_rows, second_rows)):
            all_rows = group[...].astype(F32)
            chosen = lax.broadcasted_iota(jnp.int32, all_rows.shape, 0) == scalars[4 + index]
            rows[index : index + 1, :] = jnp.sum(jnp.where(chosen, all_rows, 0.0), 0, keepdims=True)
        biases = row_of(query_bias), jnp.zeros((1, pairs * size), F32), row_of(value_bias)
        for part, bias in enumerate(biases):
            for pair in range(pairs):
                here = jnp.broadcast_to(bias[:, pair * size : (pair + 1) * size], (128, size))
                column[part * pairs + pair] = here.T

        def body(index, _):
            here = token_block(index, block)
            row = rows[pl.ds(lax.div(index, count // 2), 1), :]
            scaled, _ = normalize(tokens[here, :].astype(F32) + row)
            low = (scaled * row_of(gain) + row_of(shift)).astype(BF16)
            normed[here, :] = low
            turned[:, here] = low.T
            return 0

        lax.fori_loop(0, count, body, 0)

    pair, high_bit, low_bit = lax.rem(step, pairs), lax.div(scalars[0], 2), lax.rem(scalars[0], 2)
    bias = column[step - pair + (pair ^ high_bit)][:, 0:1]
    result = (dot(weight[...], turned[...], TN) + bias).astype(BF16)
    for high in range(pairs):
        for bit in range(2):

            @pl.when((pair == high) & (low_bit == bit))
            def _():
                for low in range(2):
                    for r in range(rounds):
                        at = (low * rounds + r) * HEAD_DIM
                        outs[r * sources + 2 * high + (low ^ bit)][0] = result[at : at + HEAD_DIM]


def project(scalars, tokens, time_table, gain, shift, weight, query_bias, value_bias, sources, rounds):
    tok_here, width = tokens.shape
    pair = 2 * rounds * HEAD_DIM
    pairs = sources // 2
    group = lambda index: pl.BlockSpec((8, width), lambda i, p: (p[2 + index], 0))
    out = pl.pallas_call(
        partial(project_kernel, sources=sources, rounds=rounds, block=tok_here // 2),
        grid_spec=pltpu.PrefetchScalarGridSpec(
            num_scalar_prefetch=1,
            grid=(3 * pairs,),
            in_specs=[
                whole(tok_here, width),
                group(0),
                group(1),
                whole(width),
                whole(width),
                pl.BlockSpec((width, pair), lambda i, p: (0, pair_block(i, p, pairs))),
                whole(width),
                whole(width),
            ],
            out_specs=[whole(tok_here, width), whole(2, width)]
            + [pl.BlockSpec((1, HEAD_DIM, tok_here), lambda i, p: (lax.div(i, pairs), 0, 0))]
            * (rounds * sources),
            scratch_shapes=[
                pltpu.VMEM((width, tok_here), BF16),
                pltpu.VMEM((3 * pairs, pair, 128), F32),
            ],
        ),
        out_shape=[
            jax.ShapeDtypeStruct((tok_here, width), BF16),
            jax.ShapeDtypeStruct((2, width), F32),
        ]
        + [jax.ShapeDtypeStruct((3, HEAD_DIM, tok_here), BF16)] * (rounds * sources),
        compiler_params=pltpu.CompilerParams(vmem_limit_bytes=VMEM),
        cost_estimate=pl.CostEstimate(
            flops=2 * tok_here * weight.size, transcendentals=0, bytes_accessed=4 * weight.size
        ),
        name="project",
    )(scalars, tokens, time_table, time_table, gain, shift, weight, query_bias, value_bias)
    return out[0], out[1], [out[2 + r * sources : 2 + (r + 1) * sources] for r in range(rounds)]


def pair_block(step, scalars, pairs):
    at = lax.rem(step, pairs)
    return step - at + (at ^ lax.div(scalars[0], 2))


def mlp_kernel(place_ref, *refs, groups, sources, block):
    (in_groups, out_groups), rounds = groups, sum(map(len, groups[0]))
    gathered, refs = refs[: len(in_groups) * sources], refs[len(in_groups) * sources :]
    pieces = len(out_groups) * sources
    tokens, rows, cotangent, out_w, out_b, gain, shift, up_w, up_b, down_w, down_b = refs[:11]
    result, g_resid = refs[11:13]
    sent_grads = refs[13 : 13 + pieces]
    send, keep, vectors, g_up_b = refs[13 + pieces : 17 + pieces]
    attended, normed, resid, gelu_act, g_up, down_sum, g_normed, g_branch, g_attended, bias = refs[17 + pieces :]
    step, last = pl.program_id(0), pl.num_programs(0) - 1
    tok_here, width = tokens.shape
    count = tok_here // block
    place = place_ref[0]
    low_bit = lax.rem(place, 2) == 0

    def head_rows(groups):
        for index in range(len(groups) * sources):
            group, j = divmod(index, sources)
            for at, r in enumerate(groups[group]):
                start = ((place ^ j) * rounds + r) * HEAD_DIM
                yield index, at, pl.ds(pl.multiple_of(start, HEAD_DIM), HEAD_DIM)

    def put(slot, grad):
        grad = grad.astype(BF16)
        middle = grad.shape[1] // 2
        left, right = grad[:, :middle], grad[:, middle:]

        @pl.when(low_bit)
        def _():
            keep[slot], send[slot] = left, right

        @pl.when(jnp.logical_not(low_bit))
        def _():
            keep[slot], send[slot] = right, left

    @pl.when(step == 0)
    def _():
        bias_row = row_of(up_b)
        for index in range(bias.shape[0]):
            bias[index : index + 1, :] = bias_row[:, index * width : (index + 1) * width]
        for index, at, here in head_rows(in_groups):
            attended[here, :] = gathered[index][at]

        def body(index, _):
            here = token_block(index, block)
            row = rows[pl.ds(lax.div(index, count // 2), 1), :]
            hidden = tokens[here, :].astype(F32) + row
            total = hidden + (dot(attended[:, here], out_w[...], TN) + row_of(out_b))
            resid[here, :] = total
            scaled, _ = normalize(total)
            normed[here, :] = (scaled * row_of(gain) + row_of(shift)).astype(BF16)
            return 0

        lax.fori_loop(0, count, body, 0)
        down_sum[...] = jnp.zeros_like(down_sum)
        g_normed[...] = jnp.zeros_like(g_normed)

    @pl.when(step < last)
    def _():
        def body(index, total):
            here = token_block(index, block)
            act = dot(normed[here, :], up_w[...]) + bias[pl.ds(step, 1), :]
            g_gelu = dot(cotangent[here, :], down_w[...], NT)
            below = 0.5 * (1.0 + lax.erf(act * 0.7071067811865476))
            density = 0.3989422804014327 * jnp.exp(-0.5 * act * act)
            low = (act * below).astype(BF16)
            grad = (g_gelu * (below + act * density)).astype(BF16)
            gelu_act[here, :] = low
            g_up[here, :] = grad
            down_sum[here, :] += dot(low, down_w[...])
            g_normed[here, :] += dot(grad, up_w[...], NT)
            return total + column_sum(grad)

        g_up_b[...] = lax.fori_loop(0, count, body, jnp.zeros(g_up_b.shape, F32))
        put(0, dot(g_up[...], normed[...], TN))
        put(1, dot(cotangent[...], gelu_act[...], TN))

    @pl.when(step == last)
    def _():
        def body(index, sums):
            here = token_block(index, block)
            total = resid[here, :]
            result[here, :] = (total + (down_sum[here, :] + row_of(down_b))).astype(BF16)
            scaled, inverse = normalize(total)
            grad = g_normed[here, :]
            inner = grad * row_of(gain)
            g_out = cotangent[here, :].astype(F32)
            g_total = g_out + inverse * (
                inner
                - jnp.mean(inner, -1, keepdims=True)
                - scaled * jnp.mean(inner * scaled, -1, keepdims=True)
            )
            g_resid[here, :] = g_total
            low = g_total.astype(BF16)
            g_branch[here, :] = low
            g_attended[:, here] = dot(out_w[...], low, NT).astype(BF16)
            parts = (grad * scaled, grad, low, g_out)
            return tuple(old + column_sum(new) for old, new in zip(sums, parts))

        empty = jnp.zeros((1, width), F32)
        sums = lax.fori_loop(0, count, body, (empty,) * 4)
        for index, at, here in head_rows(out_groups):
            sent_grads[index][at] = g_attended[here, :]
        for index, total in enumerate(sums):
            vectors[index : index + 1, :] = total
        put(0, dot(g_branch[...], attended[...], (((0,), (1,)), ((), ()))))
        put(1, jnp.zeros((width, width), F32))


def mlp(place, groups, gathered, tokens, rows, cotangent, out_w, out_b, gain, shift, up_w, up_b, down_w, down_b):
    tok_here, width = tokens.shape
    hidden_units = up_w.shape[1]
    sources = len(gathered[0])
    pieces = [part for group in gathered for part in group]
    depth = pieces[0].shape[1]
    shapes = [(len(group), depth, tok_here) for group in groups[1] for _ in range(sources)]
    steps = hidden_units // width
    slots = pl.BlockSpec((2, width, width // 2), lambda j, b: (j, 0, 0))
    at = lambda j: jnp.minimum(j, steps - 1)
    slot_shape = jax.ShapeDtypeStruct((2 * steps + 2, width, width // 2), BF16)
    out = pl.pallas_call(
        partial(mlp_kernel, groups=groups, sources=sources, block=tok_here // 2),
        grid_spec=pltpu.PrefetchScalarGridSpec(
            num_scalar_prefetch=1,
            grid=(steps + 1,),
            in_specs=[whole(*part.shape) for part in pieces]
            + [
                whole(tok_here, width),
                whole(2, width),
                whole(tok_here, width),
                whole(width, width),
                whole(width),
                whole(width),
                whole(width),
                pl.BlockSpec((width, width), lambda j, b: (0, at(j))),
                whole(hidden_units),
                pl.BlockSpec((width, width), lambda j, b: (at(j), 0)),
                whole(width),
            ],
            out_specs=[whole(tok_here, width)] * 2
            + [whole(*shape) for shape in shapes]
            + [slots, slots, whole(4, width), pl.BlockSpec((1, width), lambda j, b: (0, at(j)))],
            scratch_shapes=[
                pltpu.VMEM((width, tok_here), BF16),
                pltpu.VMEM((tok_here, width), BF16),
                pltpu.VMEM((tok_here, width), F32),
                pltpu.VMEM((tok_here, width), BF16),
                pltpu.VMEM((tok_here, width), BF16),
                pltpu.VMEM((tok_here, width), F32),
                pltpu.VMEM((tok_here, width), F32),
                pltpu.VMEM((tok_here, width), BF16),
                pltpu.VMEM((width, tok_here), BF16),
                pltpu.VMEM((steps, width), F32),
            ],
        ),
        out_shape=[
            jax.ShapeDtypeStruct((tok_here, width), BF16),
            jax.ShapeDtypeStruct((tok_here, width), F32),
        ]
        + [jax.ShapeDtypeStruct(shape, BF16) for shape in shapes]
        + [
            slot_shape,
            slot_shape,
            jax.ShapeDtypeStruct((4, width), F32),
            jax.ShapeDtypeStruct((1, hidden_units), F32),
        ],
        compiler_params=pltpu.CompilerParams(vmem_limit_bytes=VMEM),
        cost_estimate=pl.CostEstimate(
            flops=12 * tok_here * up_w.size, transcendentals=0, bytes_accessed=8 * up_w.size
        ),
        name="mlp",
    )(place, *pieces, tokens, rows, cotangent, out_w, out_b, gain, shift, up_w, up_b, down_w, down_b)
    grads = out[2 : 2 + len(shapes)]
    grads = [grads[g * sources : (g + 1) * sources] for g in range(len(groups[1]))]
    return out[0], out[1], grads, out[-4:]


def unproject(scalars, back, weight, packed, bias, chosen, rounds, sources):
    step = pl.program_id(0)
    size = len(chosen) * HEAD_DIM
    for index, part in enumerate(back):
        group, j = divmod(index, sources)
        at = (scalars[0] ^ j) * size + group * HEAD_DIM
        packed[pl.ds(pl.multiple_of(at, HEAD_DIM), HEAD_DIM), :] = part[0]
    columns = [(source * rounds + chosen[0]) * HEAD_DIM for source in range(sources)]
    ones = jnp.ones((8, packed.shape[1]), BF16)
    found = dot(ones, packed[...], NT)[0:1]

    @pl.when(step == 0)
    def _():
        bias[...] = jnp.zeros_like(bias)

    for part in range(3):

        @pl.when(step == part)
        def _():
            for source, start in enumerate(columns):
                here = found[:, source * size : (source + 1) * size]
                bias[part : part + 1, start : start + size] = here

    picked = jnp.concatenate([weight[:, start : start + size] for start in columns], 1)
    return dot(packed[...], picked, (((0,), (1,)), ((), ())))


def begin_kernel(scalars, *refs, chosen, rounds, sources):
    back, (weight, g_normed, bias, packed) = refs[:-4], refs[-4:]
    added = unproject(scalars, back, weight, packed, bias, chosen, rounds, sources)

    @pl.when(pl.program_id(0) == 0)
    def _():
        g_normed[...] = added

    @pl.when(pl.program_id(0) > 0)
    def _():
        g_normed[...] += added


def finish_kernel(scalars, *refs, chosen, rounds, sources, block):
    pieces = len(chosen) * sources
    back, refs = refs[:pieces], refs[pieces:]
    weight, tokens, rows, gain, g_resid, vectors, g_up_b, g_before, bias_before = refs[:9]
    g_tokens, sums, g_normed, packed, bias = refs[9:]
    step, last = pl.program_id(0), pl.num_programs(0) - 1
    added = unproject(scalars, back, weight, packed, bias, chosen, rounds, sources)

    @pl.when(step == 0)
    def _():
        g_normed[...] = g_before[...] + added

    @pl.when(step > 0)
    def _():
        g_normed[...] += added

    @pl.when(step == last)
    def _():
        width = tokens.shape[1]
        count = tokens.shape[0] // block
        empty = jnp.zeros((1, width), F32)

        def half(first):
            def body(index, totals):
                here = token_block(index + first * (count // 2), block)
                scaled, inverse = normalize(tokens[here, :].astype(F32) + rows[first : first + 1, :])
                grad = g_normed[here, :]
                inner = grad * row_of(gain)
                g_hidden = g_resid[here, :] + inverse * (
                    inner
                    - jnp.mean(inner, -1, keepdims=True)
                    - scaled * jnp.mean(inner * scaled, -1, keepdims=True)
                )
                g_tokens[here, :] = g_hidden.astype(BF16)
                parts = (grad * scaled, grad, g_hidden)
                return tuple(old + column_sum(new) for old, new in zip(totals, parts))

            return lax.fori_loop(0, count // 2, body, (empty,) * 3)

        one, two = half(0), half(1)
        sums[0:1, :], sums[1:2, :] = one[0] + two[0], one[1] + two[1]
        sums[2:6, :] = vectors[...]
        for index in range(4):
            sums[6 + index : 7 + index, :] = g_up_b[:, index * width : (index + 1) * width]
        lane = lax.broadcasted_iota(jnp.int32, (1, width), 1)
        is_short = scalars[1] != 0
        sums[10:13, :] = bias_before[...] + bias[...]
        pick = lambda at, other: jnp.where(lane == at, scalars[2 + at].astype(F32), other)
        sums[13:14, :] = jnp.where(scalars[0] == 0, pick(0, pick(1, 0.0)), 0.0)
        sums[14:15, :] = jnp.where(is_short, one[2], one[2] + two[2])
        sums[15:16, :] = jnp.where(is_short, two[2], 0.0)


def back_specs(back, width):
    block = pl.BlockSpec((1,) + back[0].shape[1:], lambda i, p: (i, 0, 0))
    return [block] * len(back) + [pl.BlockSpec((width, width), lambda i, p: (0, i))]


def begin_finish(scalars, back, chosen, weight, rounds):
    sources = len(back[0])
    pieces = [part for group in back for part in group]
    width, tok_here = weight.shape[0], pieces[0].shape[2]
    return pl.pallas_call(
        partial(begin_kernel, chosen=chosen, rounds=rounds, sources=sources),
        grid_spec=pltpu.PrefetchScalarGridSpec(
            num_scalar_prefetch=1,
            grid=(3,),
            in_specs=back_specs(pieces, width),
            out_specs=[whole(tok_here, width), whole(3, width)],
            scratch_shapes=[pltpu.VMEM((sources * len(chosen) * HEAD_DIM, tok_here), BF16)],
        ),
        out_shape=[
            jax.ShapeDtypeStruct((tok_here, width), F32),
            jax.ShapeDtypeStruct((3, width), F32),
        ],
        compiler_params=pltpu.CompilerParams(vmem_limit_bytes=VMEM),
        cost_estimate=pl.CostEstimate(
            flops=2 * tok_here * weight.size, transcendentals=0, bytes_accessed=4 * weight.size
        ),
        name="begin_finish",
    )(scalars, *pieces, weight)


def finish(scalars, back, chosen, weight, tokens, rows, gain, g_resid, vectors, g_up_b, before, rounds):
    tok_here, width = tokens.shape
    sources = len(back[0])
    pieces = [part for group in back for part in group]
    return pl.pallas_call(
        partial(finish_kernel, chosen=chosen, rounds=rounds, sources=sources, block=tok_here // 2),
        grid_spec=pltpu.PrefetchScalarGridSpec(
            num_scalar_prefetch=1,
            grid=(3,),
            in_specs=back_specs(pieces, width)
            + [
                whole(tok_here, width),
                whole(2, width),
                whole(width),
                whole(tok_here, width),
                whole(*vectors.shape),
                whole(*g_up_b.shape),
                whole(tok_here, width),
                whole(3, width),
            ],
            out_specs=[whole(tok_here, width), whole(16, width)],
            scratch_shapes=[
                pltpu.VMEM((tok_here, width), F32),
                pltpu.VMEM((sources * len(chosen) * HEAD_DIM, tok_here), BF16),
                pltpu.VMEM((3, width), F32),
            ],
        ),
        out_shape=[
            jax.ShapeDtypeStruct((tok_here, width), BF16),
            jax.ShapeDtypeStruct((16, width), F32),
        ],
        compiler_params=pltpu.CompilerParams(vmem_limit_bytes=VMEM),
        cost_estimate=pl.CostEstimate(
            flops=2 * tok_here * weight.size, transcendentals=0, bytes_accessed=8 * weight.size
        ),
        name="finish",
    )(scalars, *pieces, weight, tokens, rows, gain, g_resid, vectors, g_up_b, *before)


def qkv_grad_kernel(block_ref, *refs, rounds, sources, order):
    grads, refs = refs[: rounds * sources], refs[rounds * sources :]
    normed, (first, second, store) = refs[:sources], refs[sources:]
    size = 3 * HEAD_DIM
    for r in range(rounds):
        total = None
        for grad, part in zip(grads[r * sources : (r + 1) * sources], normed):
            here = jnp.concatenate([grad[p] for p in range(3)], 0)
            term = dot(here, part[...])
            total = term if total is None else total + term
        store[:, r * size : (r + 1) * size] = total.T.astype(BF16)
    half = len(order) // 2
    rows = first.shape[1]
    for at, index in enumerate(order):
        start = (block_ref[0] ^ index) * rows
        here = pl.ds(pl.multiple_of(start, rows), rows) if half > 1 else slice(at * rows, (at + 1) * rows)
        (second if at >= half else first)[at % half] = store[here, :]


def qkv_grad(block, grads, normed, order):
    rounds, sources = len(grads), len(normed)
    tok_here, width = normed[0].shape
    size = 3 * HEAD_DIM * rounds
    pieces = [part for group in grads for part in group]
    half = (len(order) // 2, width // len(order), size)
    return pl.pallas_call(
        partial(qkv_grad_kernel, rounds=rounds, sources=sources, order=order),
        grid_spec=pltpu.PrefetchScalarGridSpec(
            num_scalar_prefetch=1,
            grid=(1,),
            in_specs=[whole(*pieces[0].shape)] * len(pieces) + [whole(tok_here, width)] * sources,
            out_specs=[whole(*half)] * 2,
            scratch_shapes=[pltpu.VMEM((width, size), BF16)],
        ),
        out_shape=[jax.ShapeDtypeStruct(half, BF16)] * 2,
        compiler_params=pltpu.CompilerParams(vmem_limit_bytes=VMEM),
        cost_estimate=pl.CostEstimate(
            flops=8 * tok_here * width * size, transcendentals=0, bytes_accessed=12 * tok_here * width
        ),
        name="qkv_grad",
    )(block, *pieces, *normed)


def swap(values, axis, bit):
    size = lax.axis_size(axis)
    return lax.ppermute(values, axis, [(j, j ^ bit) for j in range(size)])


def trade(parts, axis):
    return [parts[0]] + [swap(part, axis, i) for i, part in enumerate(parts) if i]


def spread(values, axis, count):
    return [values] + [swap(values, axis, i) for i in range(1, count)]


def total_of(parts):
    total = parts[0].astype(F32)
    for part in parts[1:]:
        total = total + part.astype(F32)
    return total


def after(values, *others):
    return lax.optimization_barrier((values, *others))[0]


def deal_kernel(bits_ref, *refs, steps):
    keep, got, (outgoing, staying) = refs[: steps + 2], refs[steps + 2 : 2 * steps + 4], refs[-2:]
    gate = bits_ref[0]
    for out, side in ((outgoing, 1 - gate), (staying, gate)):
        at = 0
        for left, right in zip(keep, got):
            rows = left.shape[2] // 2
            here = pl.ds(pl.multiple_of(side * rows, rows), rows)
            for index in range(2):
                total = left[0, index, here, :].astype(F32) + right[0, index, here, :].astype(F32)
                out[index, at : at + rows, :] = total.astype(BF16)
            at += rows


def deal(gate, keep, got, dp):
    slots, width, lanes = keep.shape
    steps = slots // 2 - 1
    up_each, each = width * steps // dp, width // dp
    per_slot = width // up_each
    up = pl.BlockSpec(
        (1, 2, up_each, lanes),
        lambda i, b: (2 * lax.div(2 * i, per_slot), lax.rem(i, per_slot // 2), 0, 0),
    )
    rest = [
        pl.BlockSpec((1, 2, each, lanes), lambda i, b, slot=slot: (slot, i, 0, 0))
        for slot in [2 * k + 1 for k in range(steps)] + [2 * steps]
    ]
    views = lambda array: [array.reshape(slots, per_slot, up_each, lanes)] + [
        array.reshape(slots, dp, each, lanes)
    ] * (steps + 1)
    rows = up_each // 2 + (steps + 1) * each // 2
    shape = jax.ShapeDtypeStruct((dp, rows, lanes), BF16)
    return pl.pallas_call(
        partial(deal_kernel, steps=steps),
        grid_spec=pltpu.PrefetchScalarGridSpec(
            num_scalar_prefetch=1,
            grid=(dp // 2,),
            in_specs=([up] + rest) * 2,
            out_specs=[pl.BlockSpec((2, rows, lanes), lambda i, b: (i, 0, 0))] * 2,
        ),
        out_shape=[shape, shape],
        cost_estimate=pl.CostEstimate(flops=keep.size, transcendentals=0, bytes_accessed=6 * keep.size),
        name="deal",
    )(gate, *views(keep), *views(got))


def undeal_kernel(place_ref, *refs, sources, steps, each):
    shares, (up, down, out, store) = refs[:sources], refs[sources:]
    lanes = store.shape[2]
    for j, share in enumerate(shares):
        store[place_ref[0] ^ j] = share[...].astype(F32)
    wide = steps * each
    for low in range(2):
        both = lambda at, size: jnp.concatenate([store[low, at : at + size], store[2 + low, at : at + size]], 0).T
        up[low * lanes : (low + 1) * lanes, :] = both(0, wide)
        for half in range(2):
            here = slice(half * each, (half + 1) * each)
            share = store.at[2 * half + low]
            for k in range(steps):
                at, row = (2 * k + low) * lanes, wide + k * each
                down[here, at : at + lanes] = share[row : row + each]
            out[here, low * lanes : (low + 1) * lanes] = share[2 * wide : 2 * wide + each]


def undeal(place, shares, steps, width, dp):
    rows, lanes = shares[0].shape
    shapes = [(width, width * steps // dp), (width // dp, width * steps), (width // dp, width)]
    up, down, out = pl.pallas_call(
        partial(undeal_kernel, sources=len(shares), steps=steps, each=width // dp // 2),
        grid_spec=pltpu.PrefetchScalarGridSpec(
            num_scalar_prefetch=1,
            grid=(1,),
            in_specs=[whole(rows, lanes)] * len(shares),
            out_specs=[whole(*shape) for shape in shapes],
            scratch_shapes=[pltpu.VMEM((len(shares), rows, lanes), F32)],
        ),
        out_shape=[jax.ShapeDtypeStruct(shape, F32) for shape in shapes],
        cost_estimate=pl.CostEstimate(flops=0, transcendentals=0, bytes_accessed=24 * rows * lanes),
        name="undeal",
    )(place, *shares)
    return up, down.T, out.T


def turn_kernel(*refs):
    *parts, out = refs
    out[...] = total_of([part[0] for part in parts]).T.astype(BF16)


def turn(parts):
    _, rows, columns = parts[0].shape
    return pl.pallas_call(
        turn_kernel, out_shape=jax.ShapeDtypeStruct((columns, rows), BF16), name="turn"
    )(*parts)


def regroup_kernel(place_ref, *refs, rounds):
    *shares, out = refs
    sources = len(shares)
    for j, share in enumerate(shares):
        for r in range(rounds):
            for p in range(3):
                at = ((p * sources + (place_ref[0] ^ j)) * rounds + r) * HEAD_DIM
                start = (r * 3 + p) * HEAD_DIM
                out[pl.ds(pl.multiple_of(at, HEAD_DIM), HEAD_DIM), :] = share[start : start + HEAD_DIM]


def regroup(place, shares, rounds):
    columns, rows = shares[0].shape
    total = columns * len(shares)
    return pl.pallas_call(
        partial(regroup_kernel, rounds=rounds),
        grid_spec=pltpu.PrefetchScalarGridSpec(
            num_scalar_prefetch=1,
            grid=(1,),
            in_specs=[whole(columns, rows)] * len(shares),
            out_specs=whole(total, rows),
        ),
        out_shape=jax.ShapeDtypeStruct((total, rows), BF16),
        name="regroup",
    )(place, *shares)


def stack_kernel(parts, out):
    both = [parts[index].astype(F32) for index in range(parts.shape[0])]
    out[...] = jnp.concatenate(both, 1)


def stack_rows(parts):
    count, columns, rows = parts.shape
    return pl.pallas_call(
        stack_kernel, out_shape=jax.ShapeDtypeStruct((columns, rows * count), F32), name="stack_rows"
    )(parts).T


def exchange(values, axis):
    return lax.all_to_all(values, axis, split_axis=0, concat_axis=0, tiled=True)


def wide_sums(slots, place, dp):
    steps, width, lanes = slots.shape[0] // 2 - 1, slots.shape[1], slots.shape[2]
    pairs = slots.reshape(steps + 1, 2, width, lanes)
    up = pairs[:steps, 0].reshape(dp, 2, -1, lanes)
    down = pairs[:steps, 1].reshape(steps, dp, 2, -1, lanes)
    down = jnp.moveaxis(down, 0, 2).reshape(dp, 2, -1, lanes)
    out = pairs[steps, 0].reshape(dp, 2, -1, lanes)
    dealt = jnp.concatenate([up, down, out], 2)
    gate = place // 2
    pick = lambda index: lax.dynamic_index_in_dim(dealt, index, 1, keepdims=False)
    half_sum = total_of([pick(gate), swap(pick(1 - gate), "seq", 2)]).astype(BF16)
    share = jnp.sum(exchange(half_sum, "dp").astype(F32), 0).astype(BF16)
    shares = lax.all_gather(share, "seq", axis=0).reshape(2, 2, -1, lanes).astype(F32)
    each = width // dp // 2
    up, down, out = jnp.split(shares, [steps * each, 2 * steps * each], 2)
    turned = lambda part: jnp.transpose(part, (1, 3, 0, 2)).reshape(2 * lanes, -1)
    down = down.reshape(2, 2, steps, each, lanes)
    down = jnp.transpose(down, (2, 1, 4, 0, 3)).reshape(steps * 2 * lanes, 2 * each)
    return turned(up), down, turned(out)


def wide_columns(grads, dp, sources, rounds):
    grad = jnp.concatenate(grads, 2).reshape(-1, 3 * HEAD_DIM * rounds)
    width, columns = grad.shape
    rows = width // dp
    summed = jnp.sum(exchange(grad.reshape(dp, rows, columns), "dp").astype(F32), 0).astype(BF16)
    gathered = lax.all_gather(summed, "seq", axis=0).reshape(sources, rows, rounds, 3, HEAD_DIM)
    ordered = jnp.transpose(gathered, (1, 3, 0, 2, 4)).reshape(rows, dp, -1)
    return exchange(jnp.swapaxes(ordered, 0, 1), "dp").reshape(width, -1).astype(F32)


def on_device(
    tokens,
    time_steps,
    data_group,
    cotangent,
    attn_norm_gain,
    attn_norm_bias,
    qkv_weight,
    query_bias,
    value_bias,
    out_weight,
    out_bias,
    mlp_norm_gain,
    mlp_norm_bias,
    up_weight,
    up_bias,
    down_weight,
    down_bias,
    time_table,
):
    sources, dp = lax.axis_size("seq"), lax.axis_size("dp")
    place, block = lax.axis_index("seq"), lax.axis_index("dp")
    tokens, cotangent = tokens[0], cotangent[0]
    tok_here, width = tokens.shape
    hidden_units = up_weight.shape[1]
    rounds = HEADS // sources
    is_short = data_group[0] == 0
    short_flag = is_short.astype(jnp.int32)[None]
    place_arg = place.astype(jnp.int32)[None]
    block_arg = block.astype(jnp.int32)[None]
    few = dp <= 8
    row_steps = jnp.where(is_short, time_steps[0], time_steps[0, 0])
    scalars = jnp.concatenate([place_arg, short_flag, lax.div(row_steps, 8), lax.rem(row_steps, 8)])

    normed, rows, sending = project(
        scalars,
        tokens,
        time_table,
        attn_norm_gain,
        attn_norm_bias,
        qkv_weight,
        query_bias,
        value_bias,
        sources,
        rounds,
    )
    heads, saved, sent = [trade(sending[0], "seq")], [], []
    returned = []
    for r in range(rounds):
        if r + 1 < rounds:
            ahead = sending[r + 1] if r < 1 else after(sending[r + 1], saved[r - 1][1])
            heads.append(trade(ahead, "seq"))
        ready = after(heads[r], saved[r - 1][1]) if r else heads[r]
        out, kept = attend(short_flag, ready, sent[0] if r == 1 else ())
        saved.append(kept)
        sent.append(out)
        if r >= 1:
            returned.append(trade(after(out, *returned[-1]) if returned else out, "seq"))

    beside = swap(after(normed, saved[1][1]), "seq", 1)
    across = swap(after(normed, *returned[-1]), "seq", 2)
    groups = (((0, 1), (2,)), ((0,), (1, 2)))
    result, g_resid, sent_grads, (send, keep, vectors, g_up_b) = mlp(
        place_arg,
        groups,
        returned,
        after(tokens, beside),
        rows,
        cotangent,
        out_weight,
        out_bias,
        mlp_norm_gain,
        mlp_norm_bias,
        up_weight,
        up_bias,
        down_weight,
        down_bias,
    )
    send, *sent_grads = after((send, *sent_grads), across)
    got = swap(send, "seq", 1)
    first_grads = trade(sent_grads[0], "seq")
    if few:
        outgoing, staying = deal(place_arg // 2, keep, got, dp)
        got = swap(outgoing, "seq", 2)
        ready = outgoing
    else:
        ready = summed = total_of([keep, got]).astype(BF16)
    rest_grads = trade(after(sent_grads[1], *first_grads), "seq")
    beside = [normed, beside, across, swap(across, "seq", 1)]
    grads = [attend_back(short_flag, after(heads[0], ready, beside[3]), saved[0], first_grads, 0)]
    back = [trade(grads[0], "seq")]
    held = after(heads[1], *grads[0])
    grads.append(attend_back(short_flag, held, saved[1], rest_grads, 0))
    back.append(trade(grads[1], "seq"))
    order = (0, 4, 2, 6, 1, 5, 3, 7) if few else (0, 1)
    stay_a, away_a = qkv_grad(block_arg, grads, beside, order)
    if few:
        got_a = swap(away_a, "dp", 1)
        half_sum = total_of([staying, after(got, grads[1])]).astype(BF16)
        dealt = exchange(half_sum, "dp")
        ready = half_sum
    held = after(heads[2], stay_a, ready, *back[0])
    grads.append(attend_back(short_flag, held, saved[2], rest_grads, 1))
    back.append(trade(grads[2], "seq"))
    grads[2] = after(grads[2], *back[1])
    stay_b, away_b = qkv_grad(block_arg, grads[2:], beside, order)
    earlier = [after(parts, stay_b) for parts in back[:2]]
    before = begin_finish(scalars, earlier, (0, 1), qkv_weight, rounds)
    ready = before[1]
    if few:
        kept, got = [stay_a, stay_b], [after(got_a, grads[2]), swap(away_b, "dp", 1)]
        part = jnp.concatenate([total_of(pair).astype(BF16) for pair in zip(kept, got)], 2)
        ready = part
        sums = [part[:1]] + [swap(part[at : at + 1], "dp", bit) for at, bit in ((1, 4), (2, 2), (3, 6))]

    steps_arg = time_steps[0].astype(jnp.int32)
    flags = jnp.concatenate([place_arg, short_flag, steps_arg])
    g_tokens, small = finish(
        flags,
        after(back[2:], ready),
        (2,),
        qkv_weight,
        tokens,
        rows,
        attn_norm_gain,
        g_resid,
        vectors,
        g_up_b,
        before,
        rounds,
    )
    if few:
        small_parts = spread(small, "seq", sources)
        summed = turn(after(sums, small))
        share = total_of([after(dealt, summed)[i] for i in range(dp)]).astype(BF16)
        columns = regroup(place_arg, after(spread(summed, "seq", sources), share), rounds)
        small = total_of(after(small_parts, summed))
        share_across = swap(share, "seq", 2)
        shares = [share, swap(share, "seq", 1), share_across, swap(share_across, "seq", 1)]
    else:
        small = total_of(spread(small, "seq", sources))
    if few:
        own, other = small, swap(small, "dp", 1)
        small = jnp.concatenate([own[:13] + other[:13], own[13:], other[13:]])
        all_small = jnp.stack([small] + [swap(small, "dp", bit) for bit in (2, 4, 6)])
        small = jnp.sum(all_small[:, :13], 0)
        by_block = all_small[:, 13:].reshape(dp, 3, width)
    else:
        slots = jnp.where((jnp.arange(dp) == block)[:, None, None], small[None, 13:], 0.0)
        small = jnp.concatenate([small[:13], slots.reshape(-1, width)])
        bit = 1
        while bit < dp:
            small = small + swap(small, "dp", bit)
            bit *= 2
        by_block = small[13:].reshape(dp, 3, width)
    steps = by_block[:, 0, :2].reshape(1, -1).astype(jnp.int32)
    all_rows = by_block[:, 1:].reshape(-1, width)
    if few:
        sum_up, sum_down, sum_out = undeal(place_arg, shares, hidden_units // width, width, dp)
        sum_qkv = stack_rows(exchange(columns.reshape(dp, 3 * width // dp, width // dp), "dp"))
    else:
        sum_up, sum_down, sum_out = wide_sums(summed, place, dp)
        sum_qkv = wide_columns(
            [jnp.stack(pair).reshape(2, width // 2, -1) for pair in ((stay_a, away_a), (stay_b, away_b))],
            dp,
            sources,
            rounds,
        )
    share_cols = width // dp
    rows_mine = lax.dynamic_slice_in_dim(all_rows, block * share_cols, share_cols, 1)
    table_rows = time_table.shape[0]
    hits = jnp.arange(table_rows, dtype=jnp.int32)[:, None] == steps
    sum_table = jnp.dot(hits.astype(F32), rows_mine, precision=lax.Precision.HIGHEST)
    return (
        result[None],
        g_tokens[None],
        small[0],
        small[1],
        sum_qkv,
        small[10],
        small[12],
        sum_out,
        small[4],
        small[2],
        small[3],
        sum_up,
        small[6:10].reshape(-1),
        sum_down,
        small[5],
        sum_table,
    )


def solution(mesh):
    placed = (P("dp", "seq", None), P("dp", None), P("dp"), P("dp", "seq", None)) + (P(),) * 14
    column = P(None, "dp")
    return jax.shard_map(
        on_device,
        mesh=mesh,
        in_specs=placed,
        out_specs=(
            P("dp", "seq", None),
            P("dp", "seq", None),
            P(),
            P(),
            column,
            P(),
            P(),
            column,
            P(),
            P(),
            P(),
            column,
            P(),
            column,
            P(),
            column,
        ),
        check_vma=False,
    )
```
